32 devices in a mesh: dp: 8 (over z, x), tensor: 4 (over y, core).
Axes of the slice: x: 2, y: 2, z: 4, core: 2. Of those that a mesh axis runs over, the one named last changes fastest.
Arguments:
- embedded: bfloat16 [8192, 768], P(('dp', 'tensor')), may hold values from -6 to 6
- bigram_ids: int32 [8192], P(('dp', 'tensor')), may hold values from 0 to 16383, as said below
- trigram_ids: int32 [8192], P(('dp', 'tensor')), may hold values from 0 to 16383, as said below
- prefix_lens: int32 [8], P('dp'), may hold values from 102 to 512
- bigram_table: bfloat16 [16384, 192], P('dp'), may hold values from -6 to 6
- trigram_table: bfloat16 [16384, 192], P('dp'), may hold values from -6 to 6
- ngram_weight: bfloat16 [384, 768], replicated, may hold values from -0.3125 to 0.3125
- first_gain: float32 [768], replicated, may hold values from 0.5 to 1.5
- attend_weight: bfloat16 [768, 2304], P(None, 'tensor'), may hold values from -0.21875 to 0.21875
- output_weight: bfloat16 [768, 768], P('tensor'), may hold values from -0.875 to 0.875
- second_gain: float32 [768], replicated, may hold values from 0.5 to 1.5
- gate_weight: bfloat16 [768, 2048], P(None, 'tensor'), may hold values from -0.21875 to 0.21875
- up_weight: bfloat16 [768, 2048], P(None, 'tensor'), may hold values from -0.21875 to 0.21875
- down_weight: bfloat16 [2048, 768], P('tensor'), may hold values from -0.125 to 0.125
- cotangent: bfloat16 [8192, 768], P('dp'), may hold values from -6 to 6
Outputs:
- block_out: bfloat16 [8192, 768], P(('dp', 'tensor'))
- embed_grad: float32 [8192, 768], P(('dp', 'tensor'))
- bigram_grad: float32 [16384, 192], P(('dp', 'tensor'))
- trigram_grad: float32 [16384, 192], P(('dp', 'tensor'))
- ngram_weight_grad: float32 [384, 768], P(None, ('dp', 'tensor'))
- first_gain_grad: float32 [768], P(('dp', 'tensor'))
- attend_weight_grad: float32 [768, 2304], P('dp', 'tensor')
- output_weight_grad: float32 [768, 768], P('tensor', 'dp')
- second_gain_grad: float32 [768], P(('dp', 'tensor'))
- gate_weight_grad: float32 [768, 2048], P('dp', 'tensor')
- up_weight_grad: float32 [768, 2048], P('dp', 'tensor')
- down_weight_grad: float32 [2048, 768], P('tensor', 'dp')
The draws below stay inside these ranges and needn't reach their ends.
Inputs may be any that keep to these rules, and one draw needn't show every extreme that they name: `bigram_ids`: row r of the 2-gram table is held by index r // 2048 of dp. Among the tokens of one device, at most 64 name rows of one holder; in every draw one holder gets exactly 64 from every device. `trigram_ids`: row r of the 3-gram table is held by index r // 2048 of dp. Among the tokens of one device, at most 64 name rows of one holder; in every draw one holder gets exactly 64 from every device.
All inputs are finite; a program needn't handle non-finite values.
Results may differ from the reference program's by a relative error of at most 0.022.
Values may be sent and summed in bfloat16 or wider, within the bound.
A program may use at most 128 MiB of HBM per device.

```python
import math
import jax
import jax.numpy as jnp
from jax import lax

D = 768
H = 12
HD = 64
FF = 2048
G = 192
ROWS_DEV = 2048
SEQ = 1024
NSEQ = 8
TOKENS = 8192
ROWS = 16384
CAP = 64
N_DP = 8
N_TENSOR = 4


def draw_hashed(key):
    per_device = SEQ // N_TENSOR
    devices = N_DP * N_TENSOR
    hot_key, rest_key = jax.random.split(key)
    hottest = jax.random.randint(hot_key, (), 0, N_DP)
    last_owner = N_DP - 1

    def one_block(block_key, leading):
        order_key, shuffle_key, local_key = jax.random.split(block_key, 3)
        ordering = jax.random.permutation(order_key, N_DP)
        ordering = jnp.where(ordering == hottest, ordering[0], ordering).at[0].set(hottest)
        where_last = jnp.argmax(ordering == last_owner)
        swapped = ordering.at[where_last].set(ordering[1]).at[1].set(last_owner)
        moved = leading & (hottest != last_owner)
        ordering = jnp.where(moved, swapped, ordering)
        places = jnp.arange(per_device)
        picked_slot = jnp.where(places < CAP, 0, 1 + (places - CAP) % (N_DP - 1))
        target_place = jnp.where(hottest != last_owner, CAP, 0)
        marker = places == target_place
        shuffle = jax.random.permutation(shuffle_key, per_device)
        owners = ordering[picked_slot][shuffle]
        marker = marker[shuffle]
        within = jax.random.randint(local_key, (per_device,), 0, ROWS_DEV)
        within = jnp.where(leading & marker, ROWS_DEV - 1, within)
        return owners * ROWS_DEV + within
    leading_flags = jnp.arange(devices) == 0
    return jax.vmap(one_block)(jax.random.split(rest_key, devices), leading_flags).reshape(-1).astype(jnp.int32)


def draw_bigram_ids(key, part):
    return draw_hashed(jax.random.fold_in(key, 2))


def draw_trigram_ids(key, part):
    return draw_hashed(jax.random.fold_in(key, 3))


def place_ends(array, rng, low, high):
    place = [jax.random.randint(jax.random.fold_in(rng, axis), (), 0, length) for axis, length in enumerate(array.shape)]
    longest = array.shape.index(max(array.shape))
    next_to = place[:longest] + [(place[longest] + 1) % array.shape[longest]] + place[longest + 1:]
    return array.at[tuple(place)].set(low).at[tuple(next_to)].set(high)


def block_scale(stream_key, extent, cuts, least, largest):
    level, own = 1.0, jax.random.fold_in(stream_key, 6)
    for axis_at, parts in cuts:
        heights = jnp.exp(jax.random.uniform(jax.random.fold_in(own, axis_at), (parts,), jnp.float32, least / len(cuts), largest / len(cuts)))
        level = level * jnp.repeat(heights, extent[axis_at] // parts).reshape([-1 if axis == axis_at else 1 for axis in range(len(extent))])
    return level


def normal_values(own_key, extent, scale, limit, pieces=(), kind=jnp.bfloat16):
    values = jax.random.normal(own_key, extent, jnp.float32) * scale
    if len(pieces) > 0:
        values = block_scale(own_key, extent, pieces, -0.22, 0.18) * values
    return jnp.clip(values, min=-limit, max=limit).astype(kind)


def setup_inputs(seed: int = 0) -> dict:
    key_of = jax.random.split(jax.random.key(seed), 16)
    embedded = normal_values(key_of[0], (TOKENS, D), 1.0, 6.0, ((0, 32),))
    bigram_ids = draw_bigram_ids(jax.random.fold_in(key_of[15], 71), 0)
    trigram_ids = draw_trigram_ids(jax.random.fold_in(key_of[15], 71), 0)
    prefix_lens = place_ends(jax.random.randint(key_of[3], (NSEQ,), SEQ // 10, SEQ // 2 + 1), jax.random.fold_in(key_of[3], 1), SEQ // 10, (SEQ // 2 + 1) - 1).astype(jnp.int32)
    bigram_table = normal_values(key_of[4], (ROWS, G), 1.0, 6.0, ((0, 8),))
    trigram_table = normal_values(key_of[5], (ROWS, G), 1.0, 6.0, ((0, 8),))
    ngram_weight = normal_values(key_of[6], (2 * G, D), (2 * G) ** -0.5, 0.3125)
    first_gain = jnp.clip(1.0 + 0.1 * jax.random.normal(key_of[7], (D,), jnp.float32), 0.5, 1.5)
    attend_weight = normal_values(key_of[8], (D, 3 * D), D ** -0.5, 0.21875, ((1, 4),))
    output_weight = normal_values(key_of[9], (D, D), (D // 16) ** -0.5, 0.875, ((0, 4),))
    second_gain = jnp.clip(1.0 + 0.1 * jax.random.normal(key_of[10], (D,), jnp.float32), 0.5, 1.5)
    gate_weight = normal_values(key_of[11], (D, FF), D ** -0.5, 0.21875, ((1, 4),))
    up_weight = normal_values(key_of[12], (D, FF), D ** -0.5, 0.21875, ((1, 4),))
    down_weight = normal_values(key_of[13], (FF, D), FF ** -0.5, 0.125, ((0, 4),))
    cotangent = normal_values(key_of[14], (TOKENS, D), 1.0, 6.0, ((0, 8),))
    return dict(embedded=embedded, bigram_ids=bigram_ids, trigram_ids=trigram_ids, prefix_lens=prefix_lens, bigram_table=bigram_table, trigram_table=trigram_table, ngram_weight=ngram_weight, first_gain=first_gain, attend_weight=attend_weight, output_weight=output_weight, second_gain=second_gain, gate_weight=gate_weight, up_weight=up_weight, down_weight=down_weight, cotangent=cotangent)


@jax.custom_vjp
def low(v):
    return lax.optimization_barrier(v.astype(jnp.bfloat16)).astype(jnp.float32)

@jax.custom_vjp
def low_back(v):
    return v

def low_keep(v):
    return (low(v), None)

def low_pass(kept, grad):
    return (grad,)

def back_keep(v):
    return (v, None)

def back_low(kept, grad):
    return (low(grad),)
low.defvjp(low_keep, low_pass)
low_back.defvjp(back_keep, back_low)
highest = lax.Precision.HIGHEST

def normed(values_in, gain):
    scaling = lax.rsqrt(lax.optimization_barrier(jnp.mean(values_in * values_in, axis=-1, keepdims=True)) + 1e-05)
    return values_in * scaling * gain

def rotary_tables(length, width):
    halfway = width // 2
    frequency = jnp.exp(jnp.arange(halfway, dtype=jnp.float32) * (-2.0 * math.log(10000.0) / width))
    angles = jnp.arange(length, dtype=jnp.float32)[:, None] * frequency[None, :]
    return (jnp.cos(angles), jnp.sin(angles))

def rotate(values_in, cosine, sines):
    halfway = values_in.shape[-1] // 2
    leading = values_in[..., :halfway]
    trailing = values_in[..., halfway:]
    cosine = cosine[:, None, :]
    sines = sines[:, None, :]
    return jnp.concatenate([leading * cosine - trailing * sines, trailing * cosine + leading * sines], axis=-1)

def block_rows(inputs, prefix, first_gain, attend_weight, output_weight, second_gain, gate_weight, up_weight, down_weight):
    length = inputs.shape[0]
    normed_one = low(normed(inputs, first_gain))
    mixture = low_back(jnp.dot(normed_one, attend_weight, precision=highest))
    mixture = mixture.reshape(length, H, 3, HD)
    cosine, sines = rotary_tables(length, HD)
    queries = low(low_back(rotate(mixture[:, :, 0], cosine, sines)))
    keys = low(low_back(rotate(mixture[:, :, 1], cosine, sines)))
    values = low(mixture[:, :, 2])
    scores = jnp.einsum('qhd,khd->hqk', queries, keys, precision=highest) * HD ** (-0.5)
    position = jnp.arange(length)
    allowed = (position[None, :] <= position[:, None]) | (position[None, :] < prefix)
    scores = low_back(jnp.where(allowed[None], scores, -1000000000.0))
    probs = jax.nn.softmax(scores, axis=-1)
    weights_low = low(probs)
    attended = jnp.einsum('hqk,khd->qhd', weights_low, values, precision=highest)
    attended = low(low_back(attended.reshape(length, D)))
    branch_one = low_back(jnp.dot(attended, output_weight, precision=highest))
    after = inputs + branch_one
    normed_two = low(normed(after, second_gain))
    gate = low_back(jnp.dot(normed_two, gate_weight, precision=highest))
    up_part = low_back(jnp.dot(normed_two, up_weight, precision=highest))
    activity = low(jax.nn.silu(gate) * up_part)
    branch_two = low_back(jnp.dot(activity, down_weight, precision=highest))
    return after + branch_two

def reference(embedded, bigram_ids, trigram_ids, prefix_lens, bigram_table, trigram_table, ngram_weight, first_gain, attend_weight, output_weight, second_gain, gate_weight, up_weight, down_weight, cotangent):
    floats = tuple((item.astype(jnp.float32) for item in (embedded, bigram_table, trigram_table, ngram_weight, first_gain, attend_weight, output_weight, second_gain, gate_weight, up_weight, down_weight)))
    checked = jax.checkpoint(block_rows)

    def forward(embed_rows, bigram_rows, trigram_rows, ngram_mat, gain_one, attend_mat, output_mat, gain_two, gate_mat, up_mat, down_mat):
        ngram_rows = jnp.concatenate([bigram_rows[bigram_ids], trigram_rows[trigram_ids]], axis=1)
        lifted = low_back(jnp.dot(ngram_rows, ngram_mat, precision=highest))
        inputs = embed_rows + lifted
        grouped = inputs.reshape(NSEQ, SEQ, D)

        def one_sequence(carry, item):
            seq_inputs, prefix = item
            return (carry, checked(seq_inputs, prefix, gain_one, attend_mat, output_mat, gain_two, gate_mat, up_mat, down_mat))
        unused, outputs = lax.scan(one_sequence, jnp.zeros((), jnp.float32), (grouped, prefix_lens))
        return outputs.reshape(TOKENS, D)
    result, pullback = jax.vjp(forward, *floats)
    grads = pullback(cotangent.astype(jnp.float32))
    return (result.astype(jnp.bfloat16), grads[0], grads[1], grads[2], grads[3], grads[4], grads[5], grads[6], grads[7], grads[8], grads[9], grads[10])
```

```python
import functools
import math

import jax
import jax.numpy as jnp
from jax import lax
from jax.experimental import pallas as pl
from jax.experimental.pallas import tpu as pltpu
from jax.sharding import PartitionSpec as P

HD = 64


def normed_rows(values_in, gain):
    scaling = lax.rsqrt(jnp.mean(values_in * values_in, axis=-1, keepdims=True) + 1e-05)
    return (values_in * scaling * gain, scaling)


def norm_backward(grad_out, values_in, scaling, gain):
    scaled = grad_out * gain
    gain_grad = jnp.sum(grad_out * values_in * scaling, axis=0)
    row_grad = scaling * scaled - values_in * scaling**3 * jnp.mean(
        scaled * values_in, axis=-1, keepdims=True
    )
    return (row_grad, gain_grad)


def rotary_tables(length, width):
    halfway = width // 2
    frequency = jnp.exp(jnp.arange(halfway, dtype=jnp.float32) * (-2.0 * math.log(10000.0) / width))
    angles = jnp.arange(length, dtype=jnp.float32)[:, None] * frequency[None, :]
    return (jnp.cos(angles), jnp.sin(angles))


def rotate(values_in, cosine, sines):
    halfway = values_in.shape[-1] // 2
    leading = values_in[..., :halfway]
    trailing = values_in[..., halfway:]
    cosine = cosine[:, None, :]
    sines = sines[:, None, :]
    return jnp.concatenate(
        [leading * cosine - trailing * sines, trailing * cosine + leading * sines], axis=-1
    )


def unrotate(grads, cosine, sines):
    halfway = grads.shape[-1] // 2
    leading = grads[..., :halfway]
    trailing = grads[..., halfway:]
    cosine = cosine[:, None, :]
    sines = sines[:, None, :]
    return jnp.concatenate(
        [leading * cosine + trailing * sines, trailing * cosine - leading * sines], axis=-1
    )


def inner(left, right):
    return lax.dot_general(
        left, right, (((0,), (0,)), ((), ())), preferred_element_type=jnp.float32
    )


def reduce_kernel(peers, part_ref, out_ref, mine, pair_in, pair_out, far_in, sems):
    groups = peers // 2
    me = lax.axis_index("dp")
    parity = lax.rem(me, 2)
    place = me // 2
    partner = me + 1 - 2 * parity
    barrier = pltpu.get_barrier_semaphore()
    pl.semaphore_signal(barrier, inc=1, device_id={"dp": partner})
    for step in range(1, groups):
        target = lax.rem(place + step, groups) * 2 + parity
        pl.semaphore_signal(barrier, inc=1, device_id={"dp": target})
    pl.semaphore_wait(barrier, groups)
    near = []
    for step in range(1, groups + 1):
        group = lax.rem(place + step, groups)
        copy = pltpu.make_async_remote_copy(
            src_ref=part_ref.at[group * 2 + 1 - parity],
            dst_ref=pair_in.at[group],
            send_sem=sems.at[0, step - 1],
            recv_sem=sems.at[1, step - 1],
            device_id={"dp": partner},
        )
        copy.start()
        near.append(copy)
    own = pltpu.make_async_copy(part_ref, mine, sems.at[4, 0])
    own.start()
    own.wait()
    far = []
    for step in range(1, groups + 1):
        group = lax.rem(place + step, groups)
        near[step - 1].wait_recv()
        total = mine[group * 2 + parity].astype(jnp.float32) + pair_in[group].astype(jnp.float32)
        if step == groups:
            out_ref[...] = total
            break
        pair_out[step - 1] = total.astype(jnp.bfloat16)
        copy = pltpu.make_async_remote_copy(
            src_ref=pair_out.at[step - 1],
            dst_ref=far_in.at[step - 1],
            send_sem=sems.at[2, step - 1],
            recv_sem=sems.at[3, step - 1],
            device_id={"dp": group * 2 + parity},
        )
        copy.start()
        far.append(copy)
    for step, copy in enumerate(far):
        copy.wait_recv()
        out_ref[...] += far_in[step].astype(jnp.float32)
    for copy in near + far:
        copy.wait_send()


def reduce_over_dp(parts):
    peers, rows, width = parts.shape
    groups = peers // 2
    return pl.pallas_call(
        functools.partial(reduce_kernel, peers),
        out_shape=jax.ShapeDtypeStruct((rows, width), jnp.float32),
        in_specs=[pl.BlockSpec(memory_space=pl.ANY)],
        out_specs=pl.BlockSpec(memory_space=pltpu.VMEM),
        scratch_shapes=[
            pltpu.VMEM((peers, rows, width), jnp.bfloat16),
            pltpu.VMEM((groups, rows, width), jnp.bfloat16),
            pltpu.VMEM((groups - 1, rows, width), jnp.bfloat16),
            pltpu.VMEM((groups - 1, rows, width), jnp.bfloat16),
            pltpu.SemaphoreType.DMA((5, groups)),
        ],
        compiler_params=pltpu.CompilerParams(
            collective_id=0, has_side_effects=True, vmem_limit_bytes=60 << 20
        ),
        name="weight_grads",
    )(parts)


def slot_positions(row_ids, rows_dev, peer_count, capacity):
    owner = row_ids // rows_dev
    onehot = (owner[:, None] == jnp.arange(peer_count)[None, :]).astype(jnp.float32)
    tokens = row_ids.shape[0]
    earlier = (jnp.arange(tokens)[None, :] < jnp.arange(tokens)[:, None]).astype(jnp.float32)
    ranks = jnp.dot(earlier, onehot, precision=lax.Precision.HIGHEST)
    slot = jnp.sum(ranks * onehot, axis=1).astype(jnp.int32)
    return owner * capacity + slot


def shards(
    embedded,
    bigram_ids,
    trigram_ids,
    prefix_lens,
    bigram_table,
    trigram_table,
    ngram_weight,
    first_gain,
    attend_weight,
    output_weight,
    second_gain,
    gate_weight,
    up_weight,
    down_weight,
    cotangent,
):
    peer_count = lax.axis_size("dp")
    split_count = lax.axis_size("tensor")
    local_rows = embedded.shape[0]
    length = local_rows * split_count
    rows_dev = bigram_table.shape[0]
    table_width = bigram_table.shape[1]
    capacity = max(4, 2 * local_rows // peer_count)
    scaling_factor = HD ** (-0.5)
    bigram_slot = slot_positions(bigram_ids, rows_dev, peer_count, capacity)
    trigram_slot = slot_positions(trigram_ids, rows_dev, peer_count, capacity)
    requests = jnp.zeros((2, peer_count * capacity), jnp.int32)
    requests = requests.at[0, bigram_slot].set(bigram_ids % rows_dev + 1)
    requests = requests.at[1, trigram_slot].set(trigram_ids % rows_dev + 1)
    requests = requests.reshape(2, peer_count, capacity)
    asked_rows = lax.all_to_all(requests, "dp", split_axis=1, concat_axis=1, tiled=True)
    picked = jnp.maximum(asked_rows - 1, 0)
    found_rows = jnp.stack([bigram_table[picked[0]], trigram_table[picked[1]]])
    answer = lax.all_to_all(found_rows, "dp", split_axis=1, concat_axis=1, tiled=True)
    fetched, asked_rows = (answer, asked_rows)
    fetched = fetched.reshape(2, peer_count * capacity, table_width)
    ngram_rows = jnp.concatenate([fetched[0][bigram_slot], fetched[1][trigram_slot]], axis=1)
    lifted = jnp.dot(ngram_rows, ngram_weight, preferred_element_type=jnp.float32)
    inputs = embedded.astype(jnp.float32) + lifted
    normed_one, first_scale = normed_rows(inputs, first_gain)
    normed_one_full = lax.all_gather(normed_one.astype(jnp.bfloat16), "tensor", axis=0, tiled=True)
    head_count = attend_weight.shape[1] // (3 * HD)
    mixture = jnp.dot(normed_one_full, attend_weight, preferred_element_type=jnp.float32)
    mixture = mixture.reshape(length, head_count, 3, HD)
    cosine, sines = rotary_tables(length, HD)
    queries = rotate(mixture[:, :, 0], cosine, sines).astype(jnp.bfloat16)
    keys = rotate(mixture[:, :, 1], cosine, sines).astype(jnp.bfloat16)
    values = mixture[:, :, 2].astype(jnp.bfloat16)
    block_size = min(512, length)
    block_count = length // block_size
    prefix = prefix_lens[0]
    key_position = jnp.arange(length)

    def scores_of(query_block, offset):
        products = (
            jnp.einsum("qhd,khd->hqk", query_block, keys, preferred_element_type=jnp.float32)
            * scaling_factor
        )
        query_position = offset + jnp.arange(block_size)
        allowed = (key_position[None, :] <= query_position[:, None]) | (
            key_position[None, :] < prefix
        )
        return jnp.where(allowed[None], products, -1000000000.0)

    def forward_block(position):
        offset = position * block_size
        query_block = lax.dynamic_slice_in_dim(queries, offset, block_size, 0)
        scores = scores_of(query_block, offset)
        highest_score = jnp.max(scores, axis=-1, keepdims=True)
        powers = jnp.exp(scores - highest_score)
        totals = jnp.sum(powers, axis=-1, keepdims=True)
        weights_low = (powers / totals).astype(jnp.bfloat16)
        result = jnp.einsum("hqk,khd->qhd", weights_low, values, preferred_element_type=jnp.float32)
        return (result.astype(jnp.bfloat16), (highest_score + jnp.log(totals))[..., 0])

    attended, log_totals = lax.map(forward_block, jnp.arange(block_count))
    attended = attended.reshape(length, head_count * HD)
    part_rows = attended
    branch_one = lax.psum_scatter(
        jnp.dot(part_rows, output_weight, preferred_element_type=jnp.float32).astype(jnp.bfloat16),
        "tensor",
        scatter_dimension=0,
        tiled=True,
    ).astype(jnp.float32)
    after = inputs + branch_one
    normed_two, second_scale = normed_rows(after, second_gain)
    normed_two_full = lax.all_gather(normed_two.astype(jnp.bfloat16), "tensor", axis=0, tiled=True)
    gate = jnp.dot(normed_two_full, gate_weight, preferred_element_type=jnp.float32)
    up_part = jnp.dot(normed_two_full, up_weight, preferred_element_type=jnp.float32)
    sigmoid_gate = jax.nn.sigmoid(gate)
    activity = (gate * sigmoid_gate * up_part).astype(jnp.bfloat16)
    part_rows = activity
    branch_two = lax.psum_scatter(
        jnp.dot(part_rows, down_weight, preferred_element_type=jnp.float32).astype(jnp.bfloat16),
        "tensor",
        scatter_dimension=0,
        tiled=True,
    ).astype(jnp.float32)
    block_out = (after + branch_two).astype(jnp.bfloat16)
    own_cot = lax.dynamic_slice_in_dim(
        cotangent, lax.axis_index("tensor") * local_rows, local_rows, 0
    ).astype(jnp.float32)
    down_grad = inner(activity, cotangent)
    activity_back = jnp.dot(cotangent, down_weight.T, preferred_element_type=jnp.float32)
    gate_back = (
        activity_back * up_part * sigmoid_gate * (1.0 + gate * (1.0 - sigmoid_gate))
    ).astype(jnp.bfloat16)
    up_back = (activity_back * gate * sigmoid_gate).astype(jnp.bfloat16)
    gate_grad = inner(normed_two_full, gate_back)
    up_grad = inner(normed_two_full, up_back)
    normed_two_back = lax.psum_scatter(
        (
            jnp.dot(gate_back, gate_weight.T, preferred_element_type=jnp.float32)
            + jnp.dot(up_back, up_weight.T, preferred_element_type=jnp.float32)
        ).astype(jnp.bfloat16),
        "tensor",
        scatter_dimension=0,
        tiled=True,
    ).astype(jnp.float32)
    second_row_grad, second_partial = norm_backward(
        normed_two_back, after, second_scale, second_gain
    )
    after_grad = own_cot + second_row_grad
    attn_back_full = lax.all_gather(after_grad.astype(jnp.bfloat16), "tensor", axis=0, tiled=True)
    output_grad = inner(attended, attn_back_full)
    attended_back = jnp.dot(
        attn_back_full, output_weight.T, preferred_element_type=jnp.float32
    ).astype(jnp.bfloat16)
    attended_back = attended_back.reshape(length, head_count, HD)

    def backward_block(carry, item):
        key_sum, value_sum = carry
        position, log_block = item
        offset = position * block_size
        query_block = lax.dynamic_slice_in_dim(queries, offset, block_size, 0)
        grad_block = lax.dynamic_slice_in_dim(attended_back, offset, block_size, 0)
        probs = jnp.exp(scores_of(query_block, offset) - log_block[..., None])
        prob_back = jnp.einsum(
            "qhd,khd->hqk", grad_block, values, preferred_element_type=jnp.float32
        )
        centre = jnp.sum(probs * prob_back, axis=-1, keepdims=True)
        score_back = (probs * (prob_back - centre)).astype(jnp.bfloat16)
        query_grad = (
            jnp.einsum("hqk,khd->qhd", score_back, keys, preferred_element_type=jnp.float32)
            * scaling_factor
        )
        key_sum = (
            key_sum
            + jnp.einsum(
                "hqk,qhd->khd", score_back, query_block, preferred_element_type=jnp.float32
            )
            * scaling_factor
        )
        value_sum = value_sum + jnp.einsum(
            "hqk,qhd->khd",
            probs.astype(jnp.bfloat16),
            grad_block,
            preferred_element_type=jnp.float32,
        )
        return ((key_sum, value_sum), query_grad)

    zero_heads = jnp.zeros((length, head_count, HD), jnp.float32)
    (key_sum, value_sum), query_grads = lax.scan(
        backward_block, (zero_heads, zero_heads), (jnp.arange(block_count), log_totals)
    )
    query_back = (
        query_grads.reshape(length, head_count, HD).astype(jnp.bfloat16).astype(jnp.float32)
    )
    key_back = key_sum.astype(jnp.bfloat16).astype(jnp.float32)
    mixture_back = jnp.stack(
        [unrotate(query_back, cosine, sines), unrotate(key_back, cosine, sines), value_sum], axis=2
    )
    mixture_back = mixture_back.reshape(length, head_count * 3 * HD).astype(jnp.bfloat16)
    attend_grad = inner(normed_one_full, mixture_back)
    part_rows = mixture_back
    normed_one_back = lax.psum_scatter(
        jnp.dot(part_rows, attend_weight.T, preferred_element_type=jnp.float32).astype(
            jnp.bfloat16
        ),
        "tensor",
        scatter_dimension=0,
        tiled=True,
    ).astype(jnp.float32)
    first_row_grad, first_partial = norm_backward(normed_one_back, inputs, first_scale, first_gain)
    embed_grad = after_grad + first_row_grad
    lifted_back = embed_grad.astype(jnp.bfloat16)
    ngram_partial = inner(ngram_rows, lifted_back)
    row_back = jnp.dot(lifted_back, ngram_weight.T, preferred_element_type=jnp.float32)
    outgoing = jnp.zeros((2, peer_count * capacity, table_width), jnp.float32)
    outgoing = outgoing.at[0, bigram_slot].set(row_back[:, :table_width])
    outgoing = outgoing.at[1, trigram_slot].set(row_back[:, table_width:])
    outgoing = outgoing.reshape(2, peer_count, capacity, table_width)
    arrived = lax.all_to_all(
        outgoing.astype(jnp.bfloat16), "dp", split_axis=1, concat_axis=1, tiled=True
    ).astype(outgoing.dtype)
    picked_rows = jnp.maximum(asked_rows - 1, 0)
    bigram_part = (
        jnp.zeros((rows_dev, table_width), jnp.float32)
        .at[picked_rows[0].reshape(-1)]
        .add(arrived[0].reshape(-1, table_width))
    )
    trigram_part = (
        jnp.zeros((rows_dev, table_width), jnp.float32)
        .at[picked_rows[1].reshape(-1)]
        .add(arrived[1].reshape(-1, table_width))
    )
    ngram_group, first_group, second_group = (
        lax.psum_scatter(ngram_partial, "dp", scatter_dimension=1, tiled=True),
        lax.psum_scatter(first_partial, "dp", scatter_dimension=0, tiled=True),
        lax.psum_scatter(second_partial, "dp", scatter_dimension=0, tiled=True),
    )
    width = gate_weight.shape[0]
    if width // peer_count % 16 == 0:
        sides = (attend_grad.shape[1], gate_grad.shape[1], up_grad.shape[1])
        sides += (down_grad.shape[0], output_grad.shape[0])
        parts = jnp.concatenate(
            [
                item.astype(jnp.bfloat16)
                for item in (attend_grad, gate_grad, up_grad, down_grad.T, output_grad.T)
            ],
            axis=1,
        )
        summed = reduce_over_dp(parts.reshape(peer_count, width // peer_count, -1))
        ends = [0]
        for side in sides:
            ends.append(ends[-1] + side)
        attend_sum, gate_sum, up_sum, down_sum, output_sum = (
            summed[:, low:high] for low, high in zip(ends[:-1], ends[1:])
        )
        down_sum, output_sum = down_sum.T, output_sum.T
    else:
        attend_sum, output_sum, gate_sum, up_sum, down_sum = (
            lax.psum_scatter(attend_grad, "dp", scatter_dimension=0, tiled=True),
            lax.psum_scatter(output_grad, "dp", scatter_dimension=1, tiled=True),
            lax.psum_scatter(gate_grad, "dp", scatter_dimension=0, tiled=True),
            lax.psum_scatter(up_grad, "dp", scatter_dimension=0, tiled=True),
            lax.psum_scatter(down_grad, "dp", scatter_dimension=1, tiled=True),
        )
    bigram_grad, trigram_grad, ngram_grad, first_grad, second_grad = (
        lax.psum_scatter(
            bigram_part.astype(jnp.bfloat16), "tensor", scatter_dimension=0, tiled=True
        ).astype(jnp.float32),
        lax.psum_scatter(
            trigram_part.astype(jnp.bfloat16), "tensor", scatter_dimension=0, tiled=True
        ).astype(jnp.float32),
        lax.psum_scatter(
            ngram_group.astype(jnp.bfloat16), "tensor", scatter_dimension=1, tiled=True
        ).astype(jnp.float32),
        lax.psum_scatter(
            first_group.astype(jnp.bfloat16), "tensor", scatter_dimension=0, tiled=True
        ).astype(jnp.float32),
        lax.psum_scatter(
            second_group.astype(jnp.bfloat16), "tensor", scatter_dimension=0, tiled=True
        ).astype(jnp.float32),
    )
    return (
        block_out,
        embed_grad,
        bigram_grad,
        trigram_grad,
        ngram_grad,
        first_grad,
        attend_sum,
        output_sum,
        second_grad,
        gate_sum,
        up_sum,
        down_sum,
    )


def solution(mesh):
    placed = (
        P(("dp", "tensor"), None),
        P(("dp", "tensor")),
        P(("dp", "tensor")),
        P("dp"),
        P("dp", None),
        P("dp", None),
        P(),
        P(),
        P(None, "tensor"),
        P("tensor", None),
        P(),
        P(None, "tensor"),
        P(None, "tensor"),
        P("tensor", None),
        P("dp", None),
    )
    return jax.shard_map(
        shards,
        mesh=mesh,
        in_specs=placed,
        out_specs=(
            P(("dp", "tensor"), None),
            P(("dp", "tensor"), None),
            P(("dp", "tensor"), None),
            P(("dp", "tensor"), None),
            P(None, ("dp", "tensor")),
            P(("dp", "tensor")),
            P("dp", "tensor"),
            P("tensor", "dp"),
            P(("dp", "tensor")),
            P("dp", "tensor"),
            P("dp", "tensor"),
            P("tensor", "dp"),
        ),
        check_vma=False,
    )
```

```python
import functools
import math

import jax
import jax.numpy as jnp
from jax import lax
from jax.experimental import pallas as pl
from jax.experimental.pallas import tpu as pltpu
from jax.sharding import PartitionSpec as P

BF = jnp.bfloat16
F32 = jnp.float32
HD = 64
LANES = 128
PREFIX_MOST = 512
SPLIT = 4
CHUNKS = 4

INPUTS = (
    "embedded", "bigram_ids", "trigram_ids", "prefix", "bigram_table", "trigram_table",
    "ngram_weight", "first_gain", "attend_weight", "output_weight", "second_gain",
    "gate_weight", "up_weight", "down_weight", "cotangent",
)


class Refs:
    def __init__(self, names, refs):
        self.__dict__.update(zip(names, refs, strict=True))


def dot(left, right):
    return jnp.dot(left, right, preferred_element_type=F32)


def dot_right(left, right):
    return lax.dot_general(left, right, (((1,), (1,)), ((), ())), preferred_element_type=F32)


def lane_of(shape):
    return lax.broadcasted_iota(jnp.int32, shape, len(shape) - 1)


def row_of(shape):
    return lax.broadcasted_iota(jnp.int32, shape, 0)


def onehot(test):
    return jnp.where(test, 1.0, 0.0).astype(BF)


def roll64(block):
    return pltpu.roll(block, 64, 1)


def swap_halves(block):
    return jnp.where(lane_of(block.shape) < 32, pltpu.roll(block, 96, 1), pltpu.roll(block, 32, 1))


class Sizes:
    def __init__(self, n, rows, width, heads, units, table_rows, table_width):
        self.n, self.rows, self.width, self.heads, self.units = n, rows, width, heads, units
        self.table_rows, self.table_width = table_rows, table_width
        self.length = rows * SPLIT
        self.keys = [max((i + 1) * rows, min(PREFIX_MOST, rows * SPLIT)) for i in range(SPLIT)]
        self.cap = max(16, 2 * rows // n)
        self.slots = n * self.cap
        self.padded = heads * LANES
        self.chunk = rows // CHUNKS
        self.piece = width // n
        self.groups = n // 2
        self.pair_width = 2 * table_width
        self.small = width // (n * SPLIT)
        self.small_lanes = self.pair_width + LANES
        self.attn_lanes = heads * HD * 4
        self.inside = self.piece % 16 == 0 and self.small % 8 == 0


def make_copy(src, dst, send, recv, **where):
    return pltpu.make_async_remote_copy(
        src_ref=src, dst_ref=dst, send_sem=send, recv_sem=recv, device_id=where
    )


class Gather:
    def __init__(self, z, pos, full, sems):
        self.z, self.pos, self.full, self.sems = z, pos, full, sems

    def piece(self, block, c):
        start = pl.multiple_of(block * self.z.rows + c * self.z.chunk, self.z.chunk)
        return self.full.at[pl.ds(start, self.z.chunk)]

    def copy(self, kind, c, incoming=False):
        p = self.pos
        block = ((p.t, p.t1), (p.t, p.t2), (p.t2, p.t3))[kind][1 if incoming else 0]
        ref = self.piece(block, c)
        target = p.t2 if kind == 1 else p.t1
        return make_copy(
            ref, ref, self.sems.at[c, 2 * kind], self.sems.at[c, 2 * kind + 1], tensor=target
        )

    def send(self, c):
        self.copy(1, c).start()
        self.copy(0, c).start()

    def receive(self, c):
        self.copy(1, c, True).wait_recv()
        self.copy(2, c).start()
        self.copy(0, c, True).wait_recv()
        self.copy(2, c, True).wait_recv()

    def close(self):
        def body(c, carry):
            for kind in range(3):
                self.copy(kind, c).wait_send()
            return carry

        lax.fori_loop(0, CHUNKS, body, 0)


class Scatter:
    def __init__(self, z, pos, part, near, out, far, sems):
        self.z, self.pos, self.part, self.near = z, pos, part, near
        self.out, self.far, self.sems = out, far, sems

    def span(self, c):
        return pl.ds(pl.multiple_of(c * self.z.chunk, self.z.chunk), self.z.chunk)

    def rows(self, block, c):
        start = pl.multiple_of(block * self.z.rows + c * self.z.chunk, self.z.chunk)
        return pl.ds(start, self.z.chunk)

    def near_copy(self, slot, c):
        block = self.pos.t3 if slot else self.pos.t1
        return make_copy(
            self.part.at[self.rows(block, c)],
            self.near.at[slot, self.span(c)],
            self.sems.at[c, 2 * slot],
            self.sems.at[c, 2 * slot + 1],
            tensor=self.pos.t1,
        )

    def far_copy(self, c):
        return make_copy(
            self.out.at[self.span(c)],
            self.far.at[self.span(c)],
            self.sems.at[c, 4],
            self.sems.at[c, 5],
            tensor=self.pos.t2,
        )

    def send(self, c):
        self.near_copy(1, c).start()
        self.near_copy(0, c).start()

    def middle(self, c):
        self.near_copy(1, c).wait_recv()
        own = self.part[self.rows(self.pos.t2, c)].astype(F32)
        self.out[self.span(c)] = (own + self.near[1, self.span(c)].astype(F32)).astype(BF)
        self.far_copy(c).start()

    def finish(self, c):
        self.near_copy(0, c).wait_recv()
        self.far_copy(c).wait_recv()
        own = self.part[self.rows(self.pos.t, c)].astype(F32)
        own = own + self.near[0, self.span(c)].astype(F32)
        return own + self.far[self.span(c)].astype(F32)

    def close(self):
        def body(c, carry):
            self.near_copy(0, c).wait_send()
            self.near_copy(1, c).wait_send()
            self.far_copy(c).wait_send()
            return carry

        lax.fori_loop(0, CHUNKS, body, 0)


class Spread:
    def __init__(self, z, pos, part, pair_in, pair_out, far_in, out, sems):
        self.z, self.pos, self.part, self.pair_in = z, pos, part, pair_in
        self.pair_out, self.far_in, self.out, self.sems = pair_out, far_in, out, sems

    def group(self, step):
        return lax.rem(self.pos.place + step, self.z.groups)

    def rows(self, peer):
        return pl.ds(pl.multiple_of(peer * self.z.piece, self.z.piece), self.z.piece)

    def near_copy(self, step):
        group = self.group(step)
        return make_copy(
            self.part.at[self.rows(group * 2 + 1 - self.pos.parity)],
            self.pair_in.at[step - 1],
            self.sems.at[0, step - 1],
            self.sems.at[1, step - 1],
            dp=self.pos.partner,
        )

    def far_copy(self, step):
        return make_copy(
            self.pair_out.at[step - 1],
            self.far_in.at[step - 1],
            self.sems.at[2, step - 1],
            self.sems.at[3, step - 1],
            dp=self.group(step) * 2 + self.pos.parity,
        )

    def send(self):
        for step in range(1, self.z.groups + 1):
            self.near_copy(step).start()

    def middle(self, step):
        self.near_copy(step).wait_recv()
        own = self.part[self.rows(self.group(step) * 2 + self.pos.parity)].astype(F32)
        total = own + self.pair_in[step - 1].astype(F32)
        if step == self.z.groups:
            self.out[...] = total
        else:
            self.pair_out[step - 1] = total.astype(BF)
            self.far_copy(step).start()

    def finish(self):
        for step in range(1, self.z.groups):
            self.far_copy(step).wait_recv()
            self.out[...] += self.far_in[step - 1].astype(F32)

    def close(self):
        for step in range(1, self.z.groups + 1):
            self.near_copy(step).wait_send()
            if step < self.z.groups:
                self.far_copy(step).wait_send()


class Position:
    def __init__(self, z):
        self.d, self.t = lax.axis_index("dp"), lax.axis_index("tensor")
        core, side = lax.rem(self.t, 2), self.t // 2
        self.t1 = self.t + 1 - 2 * core
        self.t2 = self.t + 2 - 4 * side
        self.t3 = self.t1 + 2 - 4 * side
        self.parity, self.place = lax.rem(self.d, 2), self.d // 2
        self.partner = self.d + 1 - 2 * self.parity


def scratch_of(z):
    n, rows, width, length, chunks = z.n, z.rows, z.width, z.length, CHUNKS
    vmem, dma = pltpu.VMEM, pltpu.SemaphoreType.DMA
    shapes = dict(
        emb=vmem((rows, width), BF),
        ids=vmem((2 * n, 1, rows), jnp.int32),
        own_ids=vmem((2, 1, rows), jnp.int32),
        table_b=vmem((z.table_rows, z.table_width), BF),
        table_t=vmem((z.table_rows, z.table_width), BF),
        nw=vmem((z.pair_width, width), BF),
        gain1=vmem((1, width), F32),
        gain2=vmem((1, width), F32),
        wa=vmem((width, 3 * z.heads * HD), BF),
        wap=vmem((width, 3 * z.padded), BF),
        wo=vmem((z.heads * HD, width), BF),
        wop=vmem((z.padded, width), BF),
        wgu=vmem((width, 2 * z.units), BF),
        wd=vmem((z.units, width), BF),
        cot=vmem((length, width), BF),
        cosine=vmem((length, LANES), F32),
        sines=vmem((length, LANES), F32),
        pick=vmem((2, rows, z.slots), BF),
        pick_t=vmem((2, z.slots, rows), BF),
        lids=vmem((SPLIT, 2, 8, z.slots), jnp.int32),
        rows_out=vmem((z.slots, z.pair_width), BF),
        rows_in=vmem((z.slots, z.pair_width), BF),
        grams=vmem((rows, z.pair_width), BF),
        inputs=vmem((rows, width), F32),
        after=vmem((rows, width), F32),
        aftergrad=vmem((rows, width), F32),
        scale1=vmem((rows, LANES), F32),
        scale2=vmem((rows, LANES), F32),
        n1=vmem((length, width), BF),
        n2=vmem((length, width), BF),
        ab=vmem((length, width), BF),
        q=vmem((length, z.padded), BF),
        k=vmem((length, z.padded), BF),
        v=vmem((length, z.padded), BF),
        probs0=vmem((z.heads, rows, z.keys[0]), BF),
        probs1=vmem((z.heads, rows, z.keys[1]), BF),
        probs2=vmem((z.heads, rows, z.keys[2]), BF),
        probs3=vmem((z.heads, rows, z.keys[3]), BF),
        att=vmem((length, z.padded), BF),
        do=vmem((length, z.padded), BF),
        dk=vmem((z.heads, HD, length), F32),
        dv=vmem((z.heads, HD, length), F32),
        mixb=vmem((length, 3 * z.padded), BF),
        act=vmem((length, z.units), BF),
        gub=vmem((length, 2 * z.units), BF),
        lifted=vmem((rows, width), BF),
        sums=vmem((2, 8, width), F32),
        back_out=vmem((z.slots, z.pair_width), BF),
        back_in=vmem((SPLIT * z.slots, z.pair_width), BF),
        in_sem=dma((16,)),
        id_sem=dma((2,)),
        row_sem=dma((2, n)),
        lid_sem=dma((2, 3)),
        back_sem=dma((2, n)),
        pass_sem=dma((6, n)),
        ag1_sem=dma((chunks, 6)),
        ag2_sem=dma((chunks, 6)),
        ag3_sem=dma((chunks, 6)),
    )
    for k in range(1, 4):
        shapes[f"part{k}"] = vmem((length, width), BF)
        shapes[f"near{k}"] = vmem((2, rows, width), BF)
        shapes[f"send{k}"] = vmem((rows, width), BF)
        shapes[f"far{k}"] = vmem((rows, width), BF)
        shapes[f"rs{k}_sem"] = dma((chunks, 6))
    shapes["rs4_sem"] = dma((chunks, 6))
    if z.inside:
        for name, lanes in (("gu", 2 * z.units), ("dn", z.units), ("at", z.attn_lanes)):
            shapes[f"{name}_part"] = vmem((width, lanes), BF)
            shapes[f"{name}_pair_in"] = vmem((z.groups, z.piece, lanes), BF)
            shapes[f"{name}_pair_out"] = vmem((z.groups - 1, z.piece, lanes), BF)
            shapes[f"{name}_far_in"] = vmem((z.groups - 1, z.piece, lanes), BF)
            shapes[f"{name}_sem"] = dma((4, z.groups))
        small = (n, z.small, z.small_lanes)
        shapes["sm_part"] = vmem((SPLIT, *small), BF)
        shapes["sm_near"] = vmem((2, *small), BF)
        shapes["sm_send"] = vmem(small, BF)
        shapes["sm_far"] = vmem(small, BF)
        shapes["sm_out"] = vmem(small, BF)
        shapes["sm_in"] = vmem(small, BF)
        shapes["sm_sem"] = dma((6,))
        shapes["sp_sem"] = dma((2, n))
    return shapes


def outputs_of(z):
    n, rows, width = z.n, z.rows, z.width
    shapes = dict(
        block_out=((rows, width), BF),
        embed_grad=((rows, width), F32),
        table_grads=((z.table_rows // SPLIT, z.pair_width), F32),
    )
    if z.inside:
        shapes["gu_out"] = ((z.piece, 2 * z.units), F32)
        shapes["dn_out"] = ((z.piece, z.units), F32)
        shapes["at_out"] = ((z.piece, z.attn_lanes), F32)
        shapes["sm_total"] = ((z.small, z.small_lanes), F32)
    else:
        shapes["gu_part"] = ((width, 2 * z.units), BF)
        shapes["dn_part"] = ((width, z.units), BF)
        shapes["at_part"] = ((width, z.attn_lanes), BF)
        shapes["sm_total"] = ((width, z.small_lanes), F32)
    return shapes


def block_kernel(z, names, *refs):
    r = Refs(names, refs)
    p = Position(z)
    n, rows, width, length = z.n, z.rows, z.width, z.length
    cap, slots, units, padded, heads = z.cap, z.slots, z.units, z.padded, z.heads
    gather1 = Gather(z, p, r.n1, r.ag1_sem)
    gather2 = Gather(z, p, r.n2, r.ag2_sem)
    gather3 = Gather(z, p, r.ab, r.ag3_sem)
    scatters = [
        Scatter(
            z, p, getattr(r, f"part{k}"), getattr(r, f"near{k}"), getattr(r, f"send{k}"),
            getattr(r, f"far{k}"), sems,
        )
        for k, sems in ((1, r.rs1_sem), (2, r.rs2_sem), (3, r.rs3_sem), (1, r.rs4_sem))
    ]
    scatter1, scatter2, scatter3, scatter4 = scatters
    spreads = {}
    if z.inside:
        for name in ("gu", "dn", "at"):
            spreads[name] = Spread(
                z, p, getattr(r, f"{name}_part"), getattr(r, f"{name}_pair_in"),
                getattr(r, f"{name}_pair_out"), getattr(r, f"{name}_far_in"),
                getattr(r, f"{name}_out"), getattr(r, f"{name}_sem"),
            )

    def peer(step):
        return lax.rem(p.d + step, n)

    barrier = pltpu.get_barrier_semaphore()
    for step in range(1, n):
        pl.semaphore_signal(barrier, inc=1, device_id={"dp": peer(step)})
    for target in (p.t1, p.t2, p.t3):
        pl.semaphore_signal(barrier, inc=1, device_id={"tensor": target})

    loads = [
        (r.bigram_ids, r.own_ids.at[0]),
        (r.trigram_ids, r.own_ids.at[1]),
        (r.bigram_table, r.table_b),
        (r.trigram_table, r.table_t),
        (r.attend_weight, r.wa),
        (r.output_weight, r.wo),
        (r.embedded, r.emb),
        (r.ngram_weight, r.nw),
        (r.first_gain, r.gain1),
        (r.second_gain, r.gain2),
        (r.gate_weight, r.wgu.at[:, pl.ds(0, units)]),
        (r.up_weight, r.wgu.at[:, pl.ds(units, units)]),
        (r.down_weight, r.wd),
        (r.cotangent, r.cot),
    ]
    loads = [pltpu.make_async_copy(src, dst, r.in_sem.at[i]) for i, (src, dst) in enumerate(loads)]
    for load in loads:
        load.start()

    pl.semaphore_wait(barrier, n - 1 + 3)

    def id_copy(step, k):
        return make_copy(
            (r.bigram_ids, r.trigram_ids)[k],
            r.ids.at[k * n + p.d],
            r.id_sem.at[0],
            r.id_sem.at[1],
            dp=peer(step),
        )

    for step in range(1, n):
        for k in range(2):
            id_copy(step, k).start()

    lane = lane_of((32, LANES))
    low = jnp.where(lane < 32, lane, lane - 32)
    frequency = jnp.exp(low.astype(F32) * (-2.0 * math.log(10000.0) / HD))
    place = row_of((32, LANES)).astype(F32)
    coarse, fine = place * 32.0 * frequency, place * frequency
    cos_coarse, sin_coarse = jnp.cos(coarse), jnp.sin(coarse)
    used = lane < HD
    cos_fine = jnp.where(used, jnp.cos(fine), 0.0)
    sin_fine = jnp.where(used, jnp.sin(fine), 0.0)
    sign = jnp.where(lane < 32, -1.0, 1.0)
    for a in range(length // 32):
        ca, sa = cos_coarse[a : a + 1], sin_coarse[a : a + 1]
        r.cosine[a * 32 : (a + 1) * 32] = ca * cos_fine - sa * sin_fine
        r.sines[a * 32 : (a + 1) * 32] = sign * (sa * cos_fine + ca * sin_fine)

    loads[0].wait()
    loads[1].wait()
    earlier = onehot(row_of((rows, rows)) < lane_of((rows, rows)))
    later = onehot(row_of((rows, rows)) > lane_of((rows, rows)))
    for k in range(2):
        r.ids[k * n + p.d] = r.own_ids[k]
        own = jnp.broadcast_to(r.own_ids[k].astype(F32), (LANES, rows))
        column = own.T
        start = (lane_of((rows, LANES)) * z.table_rows).astype(F32)
        held = (column >= start) & (column < start + z.table_rows)
        ranks = dot(later, onehot(held))
        slot = jnp.where(held, ranks + (lane_of((rows, LANES)) * cap).astype(F32), 0.0)
        slot = jnp.sum(slot, axis=1, keepdims=True)
        r.pick[k] = onehot(slot.astype(jnp.int32) == lane_of((rows, slots)))
        across = jnp.broadcast_to(slot, (rows, LANES)).T[0:1]
        r.pick_t[k] = onehot(across.astype(jnp.int32) == row_of((slots, rows)))

    loads[4].wait()
    low_half = lane_of((width, LANES)) < HD
    for h in range(heads):
        for c in range(3):
            at = (3 * h + c) * HD
            block = r.wa[:, at // LANES * LANES : min(at // LANES * LANES + LANES, 3 * heads * HD)]
            block = block.astype(F32)
            if block.shape[1] < LANES:
                fill = jnp.zeros((width, LANES - block.shape[1]), F32)
                block = jnp.concatenate([block, fill], axis=1)
            if at % LANES:
                block = roll64(block)
            to = c * padded + h * LANES
            r.wap[:, to : to + LANES] = jnp.where(low_half, block, 0.0).astype(BF)
    loads[5].wait()
    for h in range(heads):
        r.wop[h * LANES : h * LANES + HD] = r.wo[h * HD : (h + 1) * HD]
        r.wop[h * LANES + HD : (h + 1) * LANES] = jnp.zeros((HD, width), BF)

    loads[2].wait()
    loads[3].wait()
    all_ids = r.ids.at[pl.ds(0, 2 * (n - 1))]
    all_ids = make_copy(all_ids, all_ids, r.id_sem.at[0], r.id_sem.at[1], dp=peer(1))
    all_ids.wait_recv()
    asked = jnp.concatenate([r.ids[i] for i in range(2 * n)], axis=0)
    first_row = p.d * z.table_rows
    mine = (asked >= first_row) & (asked < first_row + z.table_rows)
    ranks = dot(onehot(mine), earlier)
    tags = jnp.where(mine, ranks, -1.0).astype(jnp.int32)
    local = jnp.where(mine, asked - first_row + 1, 0).astype(F32)
    picked = []
    for k in range(2):
        columns = []
        for i in range(n):
            at = k * n + i
            hit = tags[at : at + 1] == row_of((cap, rows))
            value = jnp.where(hit, local[at : at + 1], 0.0)
            columns.append(jnp.sum(value, axis=1, keepdims=True) - 1.0)
        column = jnp.concatenate(columns, axis=0)
        picked.append(column.astype(jnp.int32))
        across = jnp.broadcast_to(column, (slots, LANES)).T[0:8]
        r.lids[p.t, k] = across.astype(jnp.int32)
    half = slots // 2

    def row_copy(step):
        to = peer(step)
        return make_copy(
            r.rows_out.at[pl.ds(pl.multiple_of(to * cap, cap), cap)],
            r.rows_in.at[pl.ds(pl.multiple_of(p.d * cap, cap), cap)],
            r.row_sem.at[0, 0],
            r.row_sem.at[1, p.d],
            dp=to,
        )

    def row_arrival(step):
        of = peer(step)
        ref = r.rows_in.at[pl.ds(pl.multiple_of(of * cap, cap), cap)]
        return make_copy(ref, ref, r.row_sem.at[0, 0], r.row_sem.at[1, of], dp=of)

    for part in range(2):
        found = []
        for k, table in enumerate((r.table_b, r.table_t)):
            chosen = picked[k][part * half : (part + 1) * half]
            hits = onehot(chosen == lane_of((half, z.table_rows)))
            both = dot(hits, table[...])
            fill = jnp.zeros((half, 2 * LANES - z.table_width), F32)
            found.append((both[:, :LANES], jnp.concatenate([both[:, LANES:], fill], axis=1)))
        low_half = lane_of((half, LANES)) < HD
        rolled = [roll64(block) for block in found[1]]
        span = slice(part * half, (part + 1) * half)
        r.rows_out[span, 0:LANES] = found[0][0].astype(BF)
        middle = jnp.where(low_half, found[0][1], rolled[0])
        r.rows_out[span, LANES : 2 * LANES] = middle.astype(BF)
        r.rows_out[span, 2 * LANES :] = jnp.where(low_half, rolled[0], rolled[1]).astype(BF)
    for step in range(1, n):
        row_copy(n - step).start()
    own_slots = pl.ds(pl.multiple_of(p.d * cap, cap), cap)
    r.rows_in[own_slots] = r.rows_out[own_slots]

    for load in loads[6:10]:
        load.wait()
    for step in range(1, n):
        row_arrival(step).wait_recv()
    fetched = r.rows_in[...]
    low_table = lane_of((rows, z.pair_width)) < z.table_width
    grams = jnp.where(low_table, dot(r.pick[0], fetched), dot(r.pick[1], fetched)).astype(BF)
    r.grams[...] = grams
    inputs = r.emb[...].astype(F32) + dot(grams, r.nw[...])
    r.inputs[...] = inputs
    scale = lax.rsqrt(jnp.mean(inputs * inputs, axis=1, keepdims=True) + 1e-05)
    r.scale1[...] = jnp.broadcast_to(scale, (rows, LANES))
    own_rows = pl.ds(pl.multiple_of(p.t * rows, rows), rows)
    r.n1[own_rows] = (inputs * scale * r.gain1[...]).astype(BF)
    for c in range(CHUNKS):
        gather1.send(c)

    def lid_copy(i, incoming=False):
        target = (p.t1, p.t2, p.t3)[i]
        ref = r.lids.at[target if incoming else p.t]
        return make_copy(ref, ref, r.lid_sem.at[0, i], r.lid_sem.at[1, i], tensor=target)

    for i in range(3):
        lid_copy(i).start()

    def spans(c):
        return [
            pl.ds(pl.multiple_of(b * rows + c * z.chunk, z.chunk), z.chunk) for b in range(SPLIT)
        ]

    def take(ref, c, *rest):
        return jnp.concatenate([ref[(span, *rest)] for span in spans(c)], axis=0)

    def put(ref, c, value, *rest):
        for b, span in enumerate(spans(c)):
            ref[(span, *rest)] = value[b * z.chunk : (b + 1) * z.chunk]

    def project(c, carry):
        gather1.receive(c)
        mixture = dot(take(r.n1, c), r.wap[...])
        cosine, sines = take(r.cosine, c), take(r.sines, c)
        for h in range(heads):
            for i, (ref, factor) in enumerate(((r.q, HD**-0.5), (r.k, 1.0))):
                at = i * padded + h * LANES
                block = mixture[:, at : at + LANES]
                turned = (block * cosine + swap_halves(block) * sines).astype(BF)
                if factor != 1.0:
                    turned = (turned.astype(F32) * factor).astype(BF)
                put(ref, c, turned, slice(h * LANES, (h + 1) * LANES))
        put(r.v, c, mixture[:, 2 * padded :].astype(BF))
        return carry

    lax.fori_loop(0, CHUNKS, project, 0)

    prefix = r.prefix[0]
    probs = (r.probs0, r.probs1, r.probs2, r.probs3)
    blocks = [(i * rows, z.keys[i], probs[i]) for i in range(SPLIT)]

    def head_lanes(h):
        return pl.ds(pl.multiple_of(h * LANES, LANES), LANES)

    def attend(first, keys, kept):
        span = slice(first, first + rows)

        def one_head(h, carry):
            at = head_lanes(h)
            scores = dot_right(r.q[span, at], r.k[0:keys, at])
            key = lane_of((rows, keys))
            allowed = (key <= row_of((rows, keys)) + first) | (key < prefix)
            scores = jnp.where(allowed, scores, -1000000000.0)
            powers = jnp.exp(scores - jnp.max(scores, axis=1, keepdims=True))
            inverse = 1.0 / jnp.sum(powers, axis=1, keepdims=True)
            weights = (powers * inverse).astype(BF)
            kept[h] = weights
            r.att[span, at] = dot(weights, r.v[0:keys, at]).astype(BF)
            return carry

        lax.fori_loop(0, heads, one_head, 0)
        r.part1[span] = dot(r.att[span], r.wop[...]).astype(BF)

    for block in blocks:
        attend(*block)
    for c in range(CHUNKS):
        scatter1.send(c)
    for c in range(CHUNKS):
        scatter1.middle(c)

    for load in loads[10:]:
        load.wait()

    def second_norm(c, carry):
        span = scatter1.span(c)
        after = r.inputs[span] + scatter1.finish(c)
        r.after[span] = after
        scale = lax.rsqrt(jnp.mean(after * after, axis=1, keepdims=True) + 1e-05)
        r.scale2[span] = jnp.broadcast_to(scale, (z.chunk, LANES))
        own = scatter1.rows(p.t, c)
        r.n2[own] = (after * scale * r.gain2[...]).astype(BF)
        gather2.send(c)
        return carry

    lax.fori_loop(0, CHUNKS, second_norm, 0)

    def feed_forward(c, carry):
        gather2.receive(c)
        both = dot(take(r.n2, c), r.wgu[...])
        act_back = dot_right(take(r.cot, c), r.wd[...])
        gate, up = both[:, :units], both[:, units:]
        s = 1.0 / (1.0 + jnp.exp(-gate))
        silu = gate * s
        put(r.act, c, (silu * up).astype(BF))
        gate_back = (act_back * up * s * (1.0 + gate * (1.0 - s))).astype(BF)
        up_back = (act_back * silu).astype(BF)
        put(r.gub, c, gate_back, slice(0, units))
        put(r.gub, c, up_back, slice(units, 2 * units))
        back = dot_right(gate_back, r.wgu[:, 0:units]) + dot_right(up_back, r.wgu[:, units:])
        put(r.part3, c, back.astype(BF))
        scatter3.send(c)
        return carry

    lax.fori_loop(0, CHUNKS, feed_forward, 0)
    for c in range(CHUNKS):
        scatter3.middle(c)

    tile = 2 * LANES

    def gate_up_tile(j, carry):
        at = pl.ds(pl.multiple_of(j * tile, tile), tile)
        r.gu_part[at] = dot(r.n2[:, at].T, r.gub[...]).astype(BF)
        return carry

    lax.fori_loop(0, width // tile, gate_up_tile, 0)
    if z.inside:
        spreads["gu"].send()

    r.sums[...] = jnp.zeros_like(r.sums)

    def norm_back(grad, values, scale, gain):
        scaled = grad * gain
        mean = jnp.mean(scaled * values, axis=1, keepdims=True)
        total = jnp.sum(grad * values * scale, axis=0, keepdims=True)
        return scale * scaled - values * (scale * scale * scale * mean), total

    def second_back(c, carry):
        span = scatter3.span(c)
        grad = scatter3.finish(c)
        row_grad, total = norm_back(grad, r.after[span], r.scale2[span, 0:1], r.gain2[...])
        r.sums[1, 0:1] += total
        own = scatter3.rows(p.t, c)
        after_grad = r.cot[own].astype(F32) + row_grad
        r.aftergrad[span] = after_grad
        r.ab[own] = after_grad.astype(BF)
        gather3.send(c)
        return carry

    lax.fori_loop(0, CHUNKS, second_back, 0)

    def branch_two(c, carry):
        put(r.part2, c, dot(take(r.act, c), r.wd[...]).astype(BF))
        scatter2.send(c)
        return carry

    lax.fori_loop(0, CHUNKS, branch_two, 0)
    for c in range(CHUNKS):
        scatter2.middle(c)

    def down_tile(j, carry):
        at = pl.ds(pl.multiple_of(j * tile, tile), tile)
        r.dn_part[at] = dot(r.cot[:, at].T, r.act[...]).astype(BF)
        return carry

    lax.fori_loop(0, width // tile, down_tile, 0)
    if z.inside:
        spreads["dn"].send()

    def attended_back(c, carry):
        gather3.receive(c)
        put(r.do, c, dot_right(take(r.ab, c), r.wop[...]).astype(BF))
        return carry

    lax.fori_loop(0, CHUNKS, attended_back, 0)
    r.dk[...] = jnp.zeros_like(r.dk)
    r.dv[...] = jnp.zeros_like(r.dv)

    def unrotate(grads, span):
        grads = grads.astype(BF).astype(F32)
        turned = grads * r.cosine[span] - swap_halves(grads) * r.sines[span]
        return turned.astype(BF)

    def attend_back(first, keys, kept):
        span = slice(first, first + rows)

        def one_head(h, carry):
            at = head_lanes(h)
            do, q = r.do[span, at], r.q[span, at]
            weights = kept[h]
            prob_back = dot_right(do, r.v[0:keys, at])
            centre = jnp.sum(do.astype(F32) * r.att[span, at].astype(F32), axis=1, keepdims=True)
            score_back = (weights.astype(F32) * (prob_back - centre)).astype(BF)
            query_back = dot(score_back, r.k[0:keys, at]) * HD**-0.5
            r.mixb[span, at] = unrotate(query_back, span)
            r.dk[h, :, 0:keys] += dot(q.T[:HD], score_back)
            r.dv[h, :, 0:keys] += dot(do.T[:HD], weights)
            return carry

        lax.fori_loop(0, heads, one_head, 0)

    for block in blocks:
        attend_back(*block)

    def block_out(c, carry):
        span = scatter2.span(c)
        r.block_out[span] = (r.after[span] + scatter2.finish(c)).astype(BF)
        return carry

    lax.fori_loop(0, CHUNKS, block_out, 0)

    def upright(block):
        return jnp.concatenate([block, jnp.zeros_like(block)], axis=0).T

    scatter1.close()
    for h in range(heads):
        for i in range(SPLIT):
            span = slice(i * rows, (i + 1) * rows)
            at = padded + h * LANES
            r.mixb[span, at : at + LANES] = unrotate(upright(r.dk[h, :, span]), span)
            at = 2 * padded + h * LANES
            r.mixb[span, at : at + LANES] = upright(r.dv[h, :, span]).astype(BF)

    def first_norm_part(c, carry):
        put(r.part1, c, dot_right(take(r.mixb, c), r.wap[...]).astype(BF))
        scatter4.send(c)
        return carry

    lax.fori_loop(0, CHUNKS, first_norm_part, 0)
    for c in range(CHUNKS):
        scatter4.middle(c)
    if z.inside:
        for step in range(1, z.groups + 1):
            spreads["gu"].middle(step)

    def attend_tile(j, carry):
        at = pl.ds(pl.multiple_of(j * tile, tile), tile)
        grad = dot(r.n1[:, at].T, r.mixb[...])
        outer = dot(r.ab[:, at].T, r.att[...])
        parts = []
        for h in range(heads):
            for c in range(3):
                start = c * padded + h * LANES
                parts.append(grad[:, start : start + LANES])
        for h in range(heads):
            parts.append(outer[:, h * LANES : (h + 1) * LANES])
        for g in range(len(parts) // 2):
            both = parts[2 * g] + roll64(parts[2 * g + 1])
            r.at_part[at, g * LANES : (g + 1) * LANES] = both.astype(BF)
        return carry

    lax.fori_loop(0, width // tile, attend_tile, 0)
    if z.inside:
        spreads["at"].send()

    def first_back(c, carry):
        span = scatter4.span(c)
        grad = scatter4.finish(c)
        row_grad, total = norm_back(grad, r.inputs[span], r.scale1[span, 0:1], r.gain1[...])
        r.sums[0, 0:1] += total
        embed_grad = r.aftergrad[span] + row_grad
        r.embed_grad[span] = embed_grad
        r.lifted[span] = embed_grad.astype(BF)
        return carry

    lax.fori_loop(0, CHUNKS, first_back, 0)

    row_back = dot_right(r.lifted[...], r.nw[...]).astype(BF)
    low_table = lane_of((slots, z.pair_width)) < z.table_width
    outgoing = jnp.where(low_table, dot(r.pick_t[0], row_back), dot(r.pick_t[1], row_back))
    r.back_out[...] = outgoing.astype(BF)

    def back_slots(block, of):
        return r.back_in.at[pl.ds(pl.multiple_of(block * slots + of * cap, cap), cap)]

    def back_copy(step, incoming=False):
        to = peer(step)
        src = r.back_out.at[pl.ds(pl.multiple_of(to * cap, cap), cap)]
        dst = back_slots(p.t, to if incoming else p.d)
        recv = r.back_sem.at[1, to if incoming else p.d]
        return make_copy(src, dst, r.back_sem.at[0, 0], recv, dp=to)

    def pass_copy(kind, of, incoming=False):
        block = ((p.t, p.t1), (p.t, p.t2), (p.t2, p.t3))[kind][1 if incoming else 0]
        ref = back_slots(block, of)
        target = p.t2 if kind == 1 else p.t1
        return make_copy(
            ref, ref, r.pass_sem.at[2 * kind, of], r.pass_sem.at[2 * kind + 1, of], tensor=target
        )

    for step in range(1, n):
        back_copy(n - step).start()
    own_block = pl.ds(pl.multiple_of(p.t * slots + p.d * cap, cap), cap)
    r.back_in[own_block] = r.back_out[own_slots]

    gains = jnp.concatenate(
        [r.sums[0, 0:1], r.sums[1, 0:1], jnp.zeros((LANES - 2, width), F32)], axis=0
    )
    small = jnp.concatenate([dot(r.lifted[...].T, r.grams[...]), gains.T], axis=1)
    if z.inside:
        for j in range(n * SPLIT):
            value = small[j * z.small : (j + 1) * z.small].astype(BF)
            r.sm_part[j % SPLIT, j // SPLIT] = value

        def small_near(slot):
            block = p.t3 if slot else p.t1
            return make_copy(
                r.sm_part.at[block],
                r.sm_near.at[slot],
                r.sm_sem.at[2 * slot],
                r.sm_sem.at[2 * slot + 1],
                tensor=p.t1,
            )

        small_far = make_copy(r.sm_send, r.sm_far, r.sm_sem.at[4], r.sm_sem.at[5], tensor=p.t2)

        def small_copy(step, incoming=False):
            to = peer(step)
            at = to if incoming else p.d
            return make_copy(
                r.sm_out.at[to], r.sm_in.at[at], r.sp_sem.at[0, 0], r.sp_sem.at[1, at], dp=to
            )

        small_near(1).start()
        small_near(0).start()
        small_near(1).wait_recv()
        r.sm_send[...] = (r.sm_part[p.t2].astype(F32) + r.sm_near[1].astype(F32)).astype(BF)
        small_far.start()
    else:
        r.sm_total[...] = small

    pass_copy(0, p.d).start()
    pass_copy(1, p.d).start()
    for step in range(1, n):
        back_copy(step, True).wait_recv()
        pass_copy(1, peer(step)).start()
        pass_copy(0, peer(step)).start()
    if z.inside:
        small_near(0).wait_recv()
        small_far.wait_recv()
        total = r.sm_part[p.t].astype(F32) + r.sm_near[0].astype(F32) + r.sm_far[...].astype(F32)
        r.sm_out[...] = total.astype(BF)
        for step in range(1, n):
            small_copy(step).start()
        r.sm_in[p.d] = r.sm_out[p.d]
        for name in ("dn", "at"):
            for step in range(1, z.groups + 1):
                spreads[name].middle(step)
    for step in range(n):
        of = peer(step)
        pass_copy(1, of, True).wait_recv()
        pass_copy(2, of).start()
    for step in range(n):
        of = peer(step)
        pass_copy(0, of, True).wait_recv()
        pass_copy(2, of, True).wait_recv()
    for i in range(3):
        lid_copy(i, True).wait_recv()
    kept = z.table_rows // SPLIT
    low_table = lane_of((kept, z.pair_width)) < z.table_width

    def add_rows(b, carry):
        block = pl.ds(pl.multiple_of(b * slots, slots), slots)
        arrived = r.back_in[block]
        wanted = row_of((kept, slots)) + p.t * kept
        sums = [dot(onehot(r.lids[b, k][0:1] == wanted), arrived) for k in range(2)]
        r.table_grads[...] += jnp.where(low_table, sums[0], sums[1])
        return carry

    r.table_grads[...] = jnp.zeros_like(r.table_grads)
    lax.fori_loop(0, SPLIT, add_rows, 0)

    if z.inside:
        for step in range(1, n):
            small_copy(step, True).wait_recv()
        r.sm_total[...] = jnp.sum(r.sm_in[...].astype(F32), axis=0)
        for spread in spreads.values():
            spread.finish()

    all_ids.wait_send()
    shared = [(r.rows_out, r.row_sem, cap), (r.back_out, r.back_sem, cap)]
    if z.inside:
        shared.append((r.sm_out, r.sp_sem, 1))
    for ref, sems, each in shared:
        ref = ref.at[pl.ds(0, (n - 1) * each)]
        make_copy(ref, ref, sems.at[0, 0], sems.at[1, 0], dp=peer(1)).wait_send()
    for i in range(3):
        lid_copy(i).wait_send()
    for gather in (gather1, gather2, gather3):
        gather.close()
    for scatter in scatters[1:]:
        scatter.close()
    for spread in spreads.values():
        spread.close()
    if z.inside:
        small_near(0).wait_send()
        small_near(1).wait_send()
        small_far.wait_send()
    for step in range(n):
        for kind in range(3):
            pass_copy(kind, peer(step)).wait_send()


def shards(
    embedded,
    bigram_ids,
    trigram_ids,
    prefix_lens,
    bigram_table,
    trigram_table,
    ngram_weight,
    first_gain,
    attend_weight,
    output_weight,
    second_gain,
    gate_weight,
    up_weight,
    down_weight,
    cotangent,
):
    n = lax.axis_size("dp")
    rows, width = embedded.shape
    table_rows, table_width = bigram_table.shape
    heads, units = attend_weight.shape[1] // (3 * HD), gate_weight.shape[1]
    z = Sizes(n, rows, width, heads, units, table_rows, table_width)
    scratch, outs = scratch_of(z), outputs_of(z)
    names = (*INPUTS, *outs, *scratch)
    anywhere = pl.BlockSpec(memory_space=pl.ANY)
    in_specs = [anywhere] * len(INPUTS)
    in_specs[3] = pl.BlockSpec(memory_space=pltpu.SMEM)
    got = pl.pallas_call(
        functools.partial(block_kernel, z, names),
        out_shape=[jax.ShapeDtypeStruct(*item) for item in outs.values()],
        in_specs=in_specs,
        out_specs=[pl.BlockSpec(memory_space=pltpu.VMEM)] * len(outs),
        scratch_shapes=list(scratch.values()),
        compiler_params=pltpu.CompilerParams(
            collective_id=0, has_side_effects=True, vmem_limit_bytes=67043328
        ),
        name="block",
    )(
        embedded,
        bigram_ids.reshape(1, rows),
        trigram_ids.reshape(1, rows),
        prefix_lens,
        bigram_table,
        trigram_table,
        ngram_weight,
        first_gain.reshape(1, width),
        attend_weight,
        output_weight,
        second_gain.reshape(1, width),
        gate_weight,
        up_weight,
        down_weight,
        cotangent,
    )
    got = dict(zip(outs, got, strict=True))
    tables = got["table_grads"]
    small = got["sm_total"]
    if z.inside:
        gate_up, down, attn = got["gu_out"], got["dn_out"], got["at_out"]
    else:
        gate_up, down, attn = (
            lax.psum_scatter(got[name].astype(F32), "dp", scatter_dimension=0, tiled=True)
            for name in ("gu_part", "dn_part", "at_part")
        )
        small = lax.psum_scatter(small, ("dp", "tensor"), scatter_dimension=0, tiled=True)
    side = 3 * heads * HD
    return (
        got["block_out"],
        got["embed_grad"],
        tables[:, :table_width],
        tables[:, table_width:],
        small[:, : 2 * table_width].T,
        small[:, 2 * table_width],
        attn[:, :side],
        attn[:, side:].T,
        small[:, 2 * table_width + 1],
        gate_up[:, :units],
        gate_up[:, units:],
        down.T,
    )


def solution(mesh):
    placed = (
        P(("dp", "tensor"), None),
        P(("dp", "tensor")),
        P(("dp", "tensor")),
        P("dp"),
        P("dp", None),
        P("dp", None),
        P(),
        P(),
        P(None, "tensor"),
        P("tensor", None),
        P(),
        P(None, "tensor"),
        P(None, "tensor"),
        P("tensor", None),
        P("dp", None),
    )
    return jax.shard_map(
        shards,
        mesh=mesh,
        in_specs=placed,
        out_specs=(
            P(("dp", "tensor"), None),
            P(("dp", "tensor"), None),
            P(("dp", "tensor"), None),
            P(("dp", "tensor"), None),
            P(None, ("dp", "tensor")),
            P(("dp", "tensor")),
            P("dp", "tensor"),
            P("tensor", "dp"),
            P(("dp", "tensor")),
            P("dp", "tensor"),
            P("dp", "tensor"),
            P("tensor", "dp"),
        ),
        check_vma=False,
    )
```

```python
import functools
import math

import jax
import jax.numpy as jnp
from jax import lax
from jax.experimental import pallas as pl
from jax.experimental.pallas import tpu as pltpu
from jax.sharding import PartitionSpec as P

BF = jnp.bfloat16
F32 = jnp.float32
HD = 64
LANES = 128
PREFIX_MOST = 512
SPLIT = 4
CHUNKS = 4

INPUTS = (
    "embedded", "bigram_ids", "trigram_ids", "prefix", "bigram_table", "trigram_table",
    "ngram_weight", "first_gain", "attend_weight", "output_weight", "second_gain",
    "gate_weight", "up_weight", "down_weight", "cotangent",
)


class Refs:
    def __init__(self, names, refs):
        self.__dict__.update(zip(names, refs, strict=True))


def dot(left, right):
    return jnp.dot(left, right, preferred_element_type=F32)


def dot_right(left, right):
    return lax.dot_general(left, right, (((1,), (1,)), ((), ())), preferred_element_type=F32)


def lane_of(shape):
    return lax.broadcasted_iota(jnp.int32, shape, len(shape) - 1)


def row_of(shape):
    return lax.broadcasted_iota(jnp.int32, shape, 0)


def onehot(test):
    return jnp.where(test, 1.0, 0.0).astype(BF)


def roll64(block):
    return pltpu.roll(block, 64, 1)


def swap_halves(block):
    return jnp.where(lane_of(block.shape) < 32, pltpu.roll(block, 96, 1), pltpu.roll(block, 32, 1))


class Sizes:
    def __init__(self, n, rows, width, heads, units, table_rows, table_width):
        self.n, self.rows, self.width, self.heads, self.units = n, rows, width, heads, units
        self.table_rows, self.table_width = table_rows, table_width
        self.length = rows * SPLIT
        self.keys = [max((i + 1) * rows, min(PREFIX_MOST, rows * SPLIT)) for i in range(SPLIT)]
        self.cap = max(16, 2 * rows // n)
        self.slots = n * self.cap
        self.padded = heads * LANES
        self.chunk = rows // CHUNKS
        self.piece = width // n
        self.groups = n // 2
        self.pair_width = 2 * table_width
        self.small = width // (n * SPLIT)
        self.small_lanes = self.pair_width + LANES
        self.attn_lanes = 4 * HD
        self.inside = self.piece % 16 == 0 and self.small % 8 == 0


def make_copy(src, dst, send, recv, **where):
    return pltpu.make_async_remote_copy(
        src_ref=src, dst_ref=dst, send_sem=send, recv_sem=recv, device_id=where
    )


class Gather:
    def __init__(self, z, pos, full, sems):
        self.z, self.pos, self.full, self.sems = z, pos, full, sems

    def piece(self, block, c):
        start = pl.multiple_of(block * self.z.rows + c * self.z.chunk, self.z.chunk)
        return self.full.at[pl.ds(start, self.z.chunk)]

    def copy(self, kind, c, incoming=False):
        p = self.pos
        block = ((p.t, p.t1), (p.t, p.t2), (p.t2, p.t3))[kind][1 if incoming else 0]
        ref = self.piece(block, c)
        target = p.t2 if kind == 1 else p.t1
        return make_copy(
            ref, ref, self.sems.at[c, 2 * kind], self.sems.at[c, 2 * kind + 1], tensor=target
        )

    def send(self, c):
        self.copy(1, c).start()
        self.copy(0, c).start()

    def receive(self, c):
        self.copy(1, c, True).wait_recv()
        self.copy(2, c).start()
        self.copy(0, c, True).wait_recv()
        self.copy(2, c, True).wait_recv()

    def close(self):
        def body(c, carry):
            for kind in range(3):
                self.copy(kind, c).wait_send()
            return carry

        lax.fori_loop(0, CHUNKS, body, 0)


class Scatter:
    def __init__(self, z, pos, part, near, out, far, sems):
        self.z, self.pos, self.part, self.near = z, pos, part, near
        self.out, self.far, self.sems = out, far, sems

    def span(self, c):
        return pl.ds(pl.multiple_of(c * self.z.chunk, self.z.chunk), self.z.chunk)

    def rows(self, block, c):
        start = pl.multiple_of(block * self.z.rows + c * self.z.chunk, self.z.chunk)
        return pl.ds(start, self.z.chunk)

    def near_copy(self, slot, c):
        block = self.pos.t3 if slot else self.pos.t1
        return make_copy(
            self.part.at[self.rows(block, c)],
            self.near.at[slot, self.span(c)],
            self.sems.at[c, 2 * slot],
            self.sems.at[c, 2 * slot + 1],
            tensor=self.pos.t1,
        )

    def far_copy(self, c):
        return make_copy(
            self.out.at[self.span(c)],
            self.far.at[self.span(c)],
            self.sems.at[c, 4],
            self.sems.at[c, 5],
            tensor=self.pos.t2,
        )

    def send(self, c):
        self.near_copy(1, c).start()
        self.near_copy(0, c).start()

    def middle(self, c):
        self.near_copy(1, c).wait_recv()
        own = self.part[self.rows(self.pos.t2, c)].astype(F32)
        self.out[self.span(c)] = (own + self.near[1, self.span(c)].astype(F32)).astype(BF)
        self.far_copy(c).start()

    def finish(self, c):
        self.near_copy(0, c).wait_recv()
        self.far_copy(c).wait_recv()
        own = self.part[self.rows(self.pos.t, c)].astype(F32)
        own = own + self.near[0, self.span(c)].astype(F32)
        return own + self.far[self.span(c)].astype(F32)

    def close(self):
        def body(c, carry):
            self.near_copy(0, c).wait_send()
            self.near_copy(1, c).wait_send()
            self.far_copy(c).wait_send()
            return carry

        lax.fori_loop(0, CHUNKS, body, 0)


class Spread:
    def __init__(self, z, pos, part, pair_in, pair_out, far_in, out, sems):
        self.z, self.pos, self.part, self.pair_in = z, pos, part, pair_in
        self.pair_out, self.far_in, self.out, self.sems = pair_out, far_in, out, sems

    def group(self, step):
        return lax.rem(self.pos.place + step, self.z.groups)

    def rows(self, peer):
        return pl.ds(pl.multiple_of(peer * self.z.piece, self.z.piece), self.z.piece)

    def near_copy(self, step):
        group = self.group(step)
        return make_copy(
            self.part.at[self.rows(group * 2 + 1 - self.pos.parity)],
            self.pair_in.at[step - 1],
            self.sems.at[0, step - 1],
            self.sems.at[1, step - 1],
            dp=self.pos.partner,
        )

    def far_copy(self, step):
        return make_copy(
            self.pair_out.at[step - 1],
            self.far_in.at[step - 1],
            self.sems.at[2, step - 1],
            self.sems.at[3, step - 1],
            dp=self.group(step) * 2 + self.pos.parity,
        )

    def send(self):
        for step in range(1, self.z.groups + 1):
            self.near_copy(step).start()

    def middle(self, step):
        self.near_copy(step).wait_recv()
        own = self.part[self.rows(self.group(step) * 2 + self.pos.parity)].astype(F32)
        total = own + self.pair_in[step - 1].astype(F32)
        if step == self.z.groups:
            self.out[...] = total
        else:
            self.pair_out[step - 1] = total.astype(BF)
            self.far_copy(step).start()

    def finish(self):
        for step in range(1, self.z.groups):
            self.far_copy(step).wait_recv()
            self.out[...] += self.far_in[step - 1].astype(F32)

    def close(self):
        for step in range(1, self.z.groups + 1):
            self.near_copy(step).wait_send()
            if step < self.z.groups:
                self.far_copy(step).wait_send()


class Position:
    def __init__(self, z):
        self.d, self.t = lax.axis_index("dp"), lax.axis_index("tensor")
        core, side = lax.rem(self.t, 2), self.t // 2
        self.t1 = self.t + 1 - 2 * core
        self.t2 = self.t + 2 - 4 * side
        self.t3 = self.t1 + 2 - 4 * side
        self.parity, self.place = lax.rem(self.d, 2), self.d // 2
        self.partner = self.d + 1 - 2 * self.parity


def scratch_of(z):
    n, rows, width, length, chunks = z.n, z.rows, z.width, z.length, CHUNKS
    vmem, dma = pltpu.VMEM, pltpu.SemaphoreType.DMA
    shapes = dict(
        emb=vmem((rows, width), BF),
        ids=vmem((2 * n, 1, rows), jnp.int32),
        own_ids=vmem((2, 1, rows), jnp.int32),
        table_b=vmem((z.table_width, z.table_rows), BF),
        table_t=vmem((z.table_width, z.table_rows), BF),
        nw=vmem((z.pair_width, width), BF),
        gain1=vmem((width,), F32),
        gain2=vmem((width,), F32),
        wap=vmem((3 * z.padded, width), BF),
        wop=vmem((z.padded, width), BF),
        wgu=vmem((width, 2 * z.units), BF),
        wd=vmem((z.units, width), BF),
        cot=vmem((length, width), BF),
        cosine=vmem((length, LANES), F32),
        sines=vmem((length, LANES), F32),
        pick=vmem((2, rows, z.slots), BF),
        pick_t=vmem((2, z.slots, rows), BF),
        lids=vmem((SPLIT, 2, 8, z.slots), jnp.int32),
        rows_out=vmem((z.slots, z.pair_width), BF),
        rows_in=vmem((z.slots, z.pair_width), BF),
        grams=vmem((rows, z.pair_width), BF),
        inputs=vmem((rows, width), F32),
        after=vmem((rows, width), F32),
        aftergrad=vmem((rows, width), F32),
        scale1=vmem((rows, LANES), F32),
        scale2=vmem((rows, LANES), F32),
        n1=vmem((length, width), BF),
        n2=vmem((length, width), BF),
        ab=vmem((length, width), BF),
        q=vmem((length, z.padded), BF),
        k=vmem((length, z.padded), BF),
        v=vmem((length, z.padded), BF),
        probs0=vmem((z.heads, rows, z.keys[0]), BF),
        probs1=vmem((z.heads, rows, z.keys[1]), BF),
        probs2=vmem((z.heads, rows, z.keys[2]), BF),
        probs3=vmem((z.heads, rows, z.keys[3]), BF),
        att=vmem((length, z.padded), BF),
        do=vmem((length, z.padded), BF),
        dk=vmem((HD, length), F32),
        dv=vmem((HD, length), F32),
        n1t=vmem((width, length), BF),
        abt=vmem((width, length), BF),
        mixb=vmem((length, 3 * z.padded), BF),
        act=vmem((length, z.units), BF),
        gub=vmem((length, 2 * z.units), BF),
        lifted=vmem((rows, width), BF),
        sums=vmem((2, 8, width), F32),
        back_out=vmem((z.slots, z.pair_width), BF),
        back_in=vmem((SPLIT * z.slots, z.pair_width), BF),
        in_sem=dma((12 + 4 * z.heads,)),
        id_sem=dma((2,)),
        row_sem=dma((2, n)),
        lid_sem=dma((2, 3)),
        back_sem=dma((2, n)),
        pass_sem=dma((6, n)),
        ag1_sem=dma((chunks, 6)),
        ag2_sem=dma((chunks, 6)),
        ag3_sem=dma((chunks, 6)),
    )
    for k in range(1, 4):
        shapes[f"part{k}"] = vmem((length, width), BF)
        shapes[f"near{k}"] = vmem((2, rows, width), BF)
        shapes[f"send{k}"] = vmem((rows, width), BF)
        shapes[f"far{k}"] = vmem((rows, width), BF)
        shapes[f"rs{k}_sem"] = dma((chunks, 6))
    shapes["rs4_sem"] = dma((chunks, 6))
    if z.inside:
        heads = [(f"at{h}", z.attn_lanes) for h in range(z.heads)]
        for name, lanes in (("gu", 2 * z.units), ("dn", z.units), *heads):
            shapes[f"{name}_part"] = vmem((width, lanes), BF)
            shapes[f"{name}_pair_in"] = vmem((z.groups, z.piece, lanes), BF)
            shapes[f"{name}_pair_out"] = vmem((z.groups - 1, z.piece, lanes), BF)
            shapes[f"{name}_far_in"] = vmem((z.groups - 1, z.piece, lanes), BF)
            shapes[f"{name}_sem"] = dma((4, z.groups))
        small = (n, z.small, z.small_lanes)
        shapes["sm_part"] = vmem((SPLIT, *small), BF)
        shapes["sm_near"] = vmem((2, *small), BF)
        shapes["sm_send"] = vmem(small, BF)
        shapes["sm_far"] = vmem(small, BF)
        shapes["sm_out"] = vmem(small, BF)
        shapes["sm_in"] = vmem(small, BF)
        shapes["sm_sem"] = dma((6,))
        shapes["sp_sem"] = dma((2, n))
    return shapes


def outputs_of(z):
    n, rows, width = z.n, z.rows, z.width
    shapes = dict(
        block_out=((rows, width), BF),
        embed_grad=((rows, width), F32),
        table_grads=((z.table_rows // SPLIT, z.pair_width), F32),
    )
    if z.inside:
        shapes["gu_out"] = ((z.piece, 2 * z.units), F32)
        shapes["dn_out"] = ((z.piece, z.units), F32)
        for h in range(z.heads):
            shapes[f"at{h}_out"] = ((z.piece, z.attn_lanes), F32)
        shapes["sm_total"] = ((z.small, z.small_lanes), F32)
    else:
        shapes["gu_part"] = ((width, 2 * z.units), BF)
        shapes["dn_part"] = ((width, z.units), BF)
        for h in range(z.heads):
            shapes[f"at{h}_part"] = ((width, z.attn_lanes), BF)
        shapes["sm_total"] = ((width, z.small_lanes), F32)
    return shapes


def block_kernel(z, names, *refs):
    r = Refs(names, refs)
    p = Position(z)
    n, rows, width, length = z.n, z.rows, z.width, z.length
    cap, slots, units, padded, heads = z.cap, z.slots, z.units, z.padded, z.heads
    gather1 = Gather(z, p, r.n1, r.ag1_sem)
    gather2 = Gather(z, p, r.n2, r.ag2_sem)
    gather3 = Gather(z, p, r.ab, r.ag3_sem)
    scatters = [
        Scatter(
            z, p, getattr(r, f"part{k}"), getattr(r, f"near{k}"), getattr(r, f"send{k}"),
            getattr(r, f"far{k}"), sems,
        )
        for k, sems in ((1, r.rs1_sem), (2, r.rs2_sem), (3, r.rs3_sem), (1, r.rs4_sem))
    ]
    scatter1, scatter2, scatter3, scatter4 = scatters
    spreads = {}
    if z.inside:
        for name in ("gu", "dn", *(f"at{h}" for h in range(heads))):
            spreads[name] = Spread(
                z, p, getattr(r, f"{name}_part"), getattr(r, f"{name}_pair_in"),
                getattr(r, f"{name}_pair_out"), getattr(r, f"{name}_far_in"),
                getattr(r, f"{name}_out"), getattr(r, f"{name}_sem"),
            )

    def peer(step):
        return lax.rem(p.d + step, n)

    barrier = pltpu.get_barrier_semaphore()
    for step in range(1, n):
        pl.semaphore_signal(barrier, inc=1, device_id={"dp": peer(step)})
    for target in (p.t1, p.t2, p.t3):
        pl.semaphore_signal(barrier, inc=1, device_id={"tensor": target})

    loads = [
        (r.bigram_ids, r.own_ids.at[0]),
        (r.trigram_ids, r.own_ids.at[1]),
        (r.bigram_table, r.table_b),
        (r.trigram_table, r.table_t),
        (r.embedded, r.emb),
        (r.ngram_weight, r.nw),
        (r.first_gain, r.gain1),
        (r.second_gain, r.gain2),
        (r.gate_weight, r.wgu.at[:, pl.ds(0, units)]),
        (r.up_weight, r.wgu.at[:, pl.ds(units, units)]),
        (r.down_weight, r.wd),
        (r.cotangent, r.cot),
    ]
    for h in range(heads):
        for c in range(3):
            src = r.attend_weight.at[pl.ds((3 * h + c) * HD, HD)]
            loads.append((src, r.wap.at[pl.ds(c * padded + h * LANES, HD)]))
        src = r.output_weight.at[pl.ds(h * HD, HD)]
        loads.append((src, r.wop.at[pl.ds(h * LANES, HD)]))
    loads = [pltpu.make_async_copy(src, dst, r.in_sem.at[i]) for i, (src, dst) in enumerate(loads)]
    for load in loads:
        load.start()

    pl.semaphore_wait(barrier, n - 1 + 3)

    def id_copy(step, k):
        return make_copy(
            (r.bigram_ids, r.trigram_ids)[k],
            r.ids.at[k * n + p.d],
            r.id_sem.at[0],
            r.id_sem.at[1],
            dp=peer(step),
        )

    for step in range(1, n):
        for k in range(2):
            id_copy(step, k).start()

    lane = lane_of((32, LANES))
    low = jnp.where(lane < 32, lane, lane - 32)
    frequency = jnp.exp(low.astype(F32) * (-2.0 * math.log(10000.0) / HD))
    place = row_of((32, LANES)).astype(F32)
    coarse, fine = place * 32.0 * frequency, place * frequency
    cos_coarse, sin_coarse = jnp.cos(coarse), jnp.sin(coarse)
    used = lane < HD
    cos_fine = jnp.where(used, jnp.cos(fine), 0.0)
    sin_fine = jnp.where(used, jnp.sin(fine), 0.0)
    sign = jnp.where(lane < 32, -1.0, 1.0)
    for a in range(length // 32):
        ca, sa = cos_coarse[a : a + 1], sin_coarse[a : a + 1]
        r.cosine[a * 32 : (a + 1) * 32] = ca * cos_fine - sa * sin_fine
        r.sines[a * 32 : (a + 1) * 32] = sign * (sa * cos_fine + ca * sin_fine)

    loads[0].wait()
    loads[1].wait()
    earlier = onehot(row_of((rows, rows)) < lane_of((rows, rows)))
    later = onehot(row_of((rows, rows)) > lane_of((rows, rows)))
    for k in range(2):
        r.ids[k * n + p.d] = r.own_ids[k]
        own = jnp.broadcast_to(r.own_ids[k].astype(F32), (LANES, rows))
        column = own.T
        start = (lane_of((rows, LANES)) * z.table_rows).astype(F32)
        held = (column >= start) & (column < start + z.table_rows)
        ranks = dot(later, onehot(held))
        slot = jnp.where(held, ranks + (lane_of((rows, LANES)) * cap).astype(F32), 0.0)
        slot = jnp.sum(slot, axis=1, keepdims=True)
        r.pick[k] = onehot(slot.astype(jnp.int32) == lane_of((rows, slots)))
        across = jnp.broadcast_to(slot, (rows, LANES)).T[0:1]
        r.pick_t[k] = onehot(across.astype(jnp.int32) == row_of((slots, rows)))

    for h in range(heads):
        empty = jnp.zeros((LANES - HD, width), BF)
        for c in range(3):
            at = c * padded + h * LANES + HD
            r.wap[at : at + LANES - HD] = empty
        r.wop[h * LANES + HD : (h + 1) * LANES] = empty

    loads[2].wait()
    loads[3].wait()
    all_ids = r.ids.at[pl.ds(0, 2 * (n - 1))]
    all_ids = make_copy(all_ids, all_ids, r.id_sem.at[0], r.id_sem.at[1], dp=peer(1))
    all_ids.wait_recv()
    asked = jnp.concatenate([r.ids[i] for i in range(2 * n)], axis=0)
    first_row = p.d * z.table_rows
    mine = (asked >= first_row) & (asked < first_row + z.table_rows)
    ranks = dot(onehot(mine), earlier)
    tags = jnp.where(mine, ranks, -1.0).astype(jnp.int32)
    local = jnp.where(mine, asked - first_row + 1, 0).astype(F32)
    picked = []
    for k in range(2):
        columns = []
        for i in range(n):
            at = k * n + i
            hit = tags[at : at + 1] == row_of((cap, rows))
            value = jnp.where(hit, local[at : at + 1], 0.0)
            columns.append(jnp.sum(value, axis=1, keepdims=True) - 1.0)
        column = jnp.concatenate(columns, axis=0)
        picked.append(column.astype(jnp.int32))
        across = jnp.broadcast_to(column, (slots, LANES)).T[0:8]
        r.lids[p.t, k] = across.astype(jnp.int32)
    half = slots // 2

    def row_copy(step):
        to = peer(step)
        return make_copy(
            r.rows_out.at[pl.ds(pl.multiple_of(to * cap, cap), cap)],
            r.rows_in.at[pl.ds(pl.multiple_of(p.d * cap, cap), cap)],
            r.row_sem.at[0, 0],
            r.row_sem.at[1, p.d],
            dp=to,
        )

    def row_arrival(step):
        of = peer(step)
        ref = r.rows_in.at[pl.ds(pl.multiple_of(of * cap, cap), cap)]
        return make_copy(ref, ref, r.row_sem.at[0, 0], r.row_sem.at[1, of], dp=of)

    for part in range(2):
        found = []
        for k, table in enumerate((r.table_b, r.table_t)):
            chosen = picked[k][part * half : (part + 1) * half]
            hits = onehot(chosen == lane_of((half, z.table_rows)))
            both = dot_right(hits, table[...])
            fill = jnp.zeros((half, 2 * LANES - z.table_width), F32)
            found.append((both[:, :LANES], jnp.concatenate([both[:, LANES:], fill], axis=1)))
        low_half = lane_of((half, LANES)) < HD
        rolled = [roll64(block) for block in found[1]]
        span = slice(part * half, (part + 1) * half)
        r.rows_out[span, 0:LANES] = found[0][0].astype(BF)
        middle = jnp.where(low_half, found[0][1], rolled[0])
        r.rows_out[span, LANES : 2 * LANES] = middle.astype(BF)
        r.rows_out[span, 2 * LANES :] = jnp.where(low_half, rolled[0], rolled[1]).astype(BF)
    for step in range(1, n):
        row_copy(n - step).start()
    own_slots = pl.ds(pl.multiple_of(p.d * cap, cap), cap)
    r.rows_in[own_slots] = r.rows_out[own_slots]

    for load in loads[4:8]:
        load.wait()
    for step in range(1, n):
        row_arrival(step).wait_recv()
    fetched = r.rows_in[...]
    low_table = lane_of((rows, z.pair_width)) < z.table_width
    grams = jnp.where(low_table, dot(r.pick[0], fetched), dot(r.pick[1], fetched)).astype(BF)
    r.grams[...] = grams
    inputs = r.emb[...].astype(F32) + dot(grams, r.nw[...])
    r.inputs[...] = inputs
    scale = lax.rsqrt(jnp.mean(inputs * inputs, axis=1, keepdims=True) + 1e-05)
    r.scale1[...] = jnp.broadcast_to(scale, (rows, LANES))
    own_rows = pl.ds(pl.multiple_of(p.t * rows, rows), rows)
    r.n1[own_rows] = (inputs * scale * r.gain1[...][None, :]).astype(BF)
    for c in range(CHUNKS):
        gather1.send(c)

    def lid_copy(i, incoming=False):
        target = (p.t1, p.t2, p.t3)[i]
        ref = r.lids.at[target if incoming else p.t]
        return make_copy(ref, ref, r.lid_sem.at[0, i], r.lid_sem.at[1, i], tensor=target)

    for i in range(3):
        lid_copy(i).start()

    def spans(c):
        return [
            pl.ds(pl.multiple_of(b * rows + c * z.chunk, z.chunk), z.chunk) for b in range(SPLIT)
        ]

    def take(ref, c, *rest):
        return jnp.concatenate([ref[(span, *rest)] for span in spans(c)], axis=0)

    def put(ref, c, value, *rest):
        for b, span in enumerate(spans(c)):
            ref[(span, *rest)] = value[b * z.chunk : (b + 1) * z.chunk]

    for load in loads[8:]:
        load.wait()

    def project(c, carry):
        gather1.receive(c)
        mixture = dot_right(take(r.n1, c), r.wap[...])
        cosine, sines = take(r.cosine, c), take(r.sines, c)
        for h in range(heads):
            for i, (ref, factor) in enumerate(((r.q, HD**-0.5), (r.k, 1.0))):
                at = i * padded + h * LANES
                block = mixture[:, at : at + LANES]
                turned = (block * cosine + swap_halves(block) * sines).astype(BF)
                if factor != 1.0:
                    turned = (turned.astype(F32) * factor).astype(BF)
                put(ref, c, turned, slice(h * LANES, (h + 1) * LANES))
        put(r.v, c, mixture[:, 2 * padded :].astype(BF))
        return carry

    lax.fori_loop(0, CHUNKS, project, 0)

    prefix = r.prefix[0]
    probs = (r.probs0, r.probs1, r.probs2, r.probs3)
    blocks = [(i * rows, z.keys[i], probs[i]) for i in range(SPLIT)]

    def head_lanes(h):
        return pl.ds(pl.multiple_of(h * LANES, LANES), LANES)

    def attend(first, keys, kept):
        span = slice(first, first + rows)

        def one_head(h, carry):
            at = head_lanes(h)
            scores = dot_right(r.q[span, at], r.k[0:keys, at])
            key = lane_of((rows, keys))
            allowed = (key <= row_of((rows, keys)) + first) | (key < prefix)
            scores = jnp.where(allowed, scores, -1000000000.0)
            powers = jnp.exp(scores - jnp.max(scores, axis=1, keepdims=True))
            inverse = 1.0 / jnp.sum(powers, axis=1, keepdims=True)
            weights = (powers * inverse).astype(BF)
            kept[h] = weights
            r.att[span, at] = dot(weights, r.v[0:keys, at]).astype(BF)
            return carry

        lax.fori_loop(0, heads, one_head, 0)
        r.part1[span] = dot(r.att[span], r.wop[...]).astype(BF)

    for block in blocks:
        attend(*block)
    for c in range(CHUNKS):
        scatter1.send(c)
    for c in range(CHUNKS):
        scatter1.middle(c)

    def second_norm(c, carry):
        span = scatter1.span(c)
        after = r.inputs[span] + scatter1.finish(c)
        r.after[span] = after
        scale = lax.rsqrt(jnp.mean(after * after, axis=1, keepdims=True) + 1e-05)
        r.scale2[span] = jnp.broadcast_to(scale, (z.chunk, LANES))
        own = scatter1.rows(p.t, c)
        r.n2[own] = (after * scale * r.gain2[...][None, :]).astype(BF)
        gather2.send(c)
        return carry

    lax.fori_loop(0, CHUNKS, second_norm, 0)

    def feed_forward(c, carry):
        gather2.receive(c)
        both = dot(take(r.n2, c), r.wgu[...])
        act_back = dot_right(take(r.cot, c), r.wd[...])
        gate, up = both[:, :units], both[:, units:]
        s = 1.0 / (1.0 + jnp.exp(-gate))
        silu = gate * s
        put(r.act, c, (silu * up).astype(BF))
        gate_back = (act_back * up * s * (1.0 + gate * (1.0 - s))).astype(BF)
        up_back = (act_back * silu).astype(BF)
        put(r.gub, c, gate_back, slice(0, units))
        put(r.gub, c, up_back, slice(units, 2 * units))
        back = dot_right(gate_back, r.wgu[:, 0:units]) + dot_right(up_back, r.wgu[:, units:])
        put(r.part3, c, back.astype(BF))
        scatter3.send(c)
        return carry

    lax.fori_loop(0, CHUNKS, feed_forward, 0)
    for c in range(CHUNKS):
        scatter3.middle(c)

    tile = 2 * LANES

    def gate_up_tile(j, carry):
        at = pl.ds(pl.multiple_of(j * tile, tile), tile)
        r.gu_part[at] = dot(r.n2[:, at].T, r.gub[...]).astype(BF)
        return carry

    lax.fori_loop(0, width // tile, gate_up_tile, 0)
    if z.inside:
        spreads["gu"].send()

    r.sums[...] = jnp.zeros_like(r.sums)

    def norm_back(grad, values, scale, gain):
        scaled = grad * gain
        mean = jnp.mean(scaled * values, axis=1, keepdims=True)
        total = jnp.sum(grad * values * scale, axis=0, keepdims=True)
        return scale * scaled - values * (scale * scale * scale * mean), total

    def second_back(c, carry):
        span = scatter3.span(c)
        grad = scatter3.finish(c)
        row_grad, total = norm_back(grad, r.after[span], r.scale2[span, 0:1], r.gain2[...][None, :])
        r.sums[1, 0:1] += total
        own = scatter3.rows(p.t, c)
        after_grad = r.cot[own].astype(F32) + row_grad
        r.aftergrad[span] = after_grad
        r.ab[own] = after_grad.astype(BF)
        gather3.send(c)
        return carry

    lax.fori_loop(0, CHUNKS, second_back, 0)

    def branch_two(c, carry):
        put(r.part2, c, dot(take(r.act, c), r.wd[...]).astype(BF))
        scatter2.send(c)
        return carry

    lax.fori_loop(0, CHUNKS, branch_two, 0)
    for c in range(CHUNKS):
        scatter2.middle(c)

    def down_tile(j, carry):
        at = pl.ds(pl.multiple_of(j * tile, tile), tile)
        r.dn_part[at] = dot(r.cot[:, at].T, r.act[...]).astype(BF)
        return carry

    lax.fori_loop(0, width // tile, down_tile, 0)
    if z.inside:
        spreads["dn"].send()

    def attended_back(c, carry):
        gather3.receive(c)
        put(r.do, c, dot_right(take(r.ab, c), r.wop[...]).astype(BF))
        return carry

    lax.fori_loop(0, CHUNKS, attended_back, 0)

    def unrotate(grads, span):
        grads = grads.astype(BF).astype(F32)
        turned = grads * r.cosine[span] - swap_halves(grads) * r.sines[span]
        return turned.astype(BF)

    def upright(block):
        return jnp.concatenate([block, jnp.zeros_like(block)], axis=0).T

    def attend_back(h, first, keys, kept, whole):
        span, at = slice(first, first + rows), slice(h * LANES, (h + 1) * LANES)
        do, q = r.do[span, at], r.q[span, at]
        weights = kept[h]
        prob_back = dot_right(do, r.v[0:keys, at])
        centre = jnp.sum(do.astype(F32) * r.att[span, at].astype(F32), axis=1, keepdims=True)
        score_back = (weights.astype(F32) * (prob_back - centre)).astype(BF)
        query_back = dot(score_back, r.k[0:keys, at]) * HD**-0.5
        r.mixb[span, at] = unrotate(query_back, span)
        key_back, value_back = dot(q.T[:HD], score_back), dot(do.T[:HD], weights)
        if whole:
            r.dk[...] = key_back
            r.dv[...] = value_back
        else:
            r.dk[:, 0:keys] += key_back
            r.dv[:, 0:keys] += value_back

    def turned_tile(j, carry):
        at = pl.ds(pl.multiple_of(j * tile, tile), tile)
        r.n1t[at] = r.n1[:, at].T
        r.abt[at] = r.ab[:, at].T
        return carry

    lax.fori_loop(0, width // tile, turned_tile, 0)

    def head_tiles(h):
        part = getattr(r, f"at{h}_part")
        lanes = [slice(c * padded + h * LANES, c * padded + (h + 1) * LANES) for c in range(3)]

        def head_tile(j, carry):
            at = pl.ds(pl.multiple_of(j * tile, tile), tile)
            mixed = jnp.concatenate([r.mixb[:, span] for span in lanes], axis=1)
            grad = dot(r.n1t[at], mixed)
            outer = dot(r.abt[at], r.att[:, h * LANES : (h + 1) * LANES])
            first = grad[:, :LANES] + roll64(grad[:, LANES : 2 * LANES])
            second = grad[:, 2 * LANES :] + roll64(outer)
            part[at, 0:LANES] = first.astype(BF)
            part[at, LANES:] = second.astype(BF)
            return carry

        lax.fori_loop(0, width // tile, head_tile, 0)

    waiting = [("gu", i) for i in range(1, z.groups + 1)] + [("dn", i) for i in range(1, z.groups + 1)]

    def pair_sums(count):
        for name, step in waiting[:count]:
            if z.inside:
                spreads[name].middle(step)
        del waiting[:count]

    pair_sums(2 * z.groups // 4)
    for h in range(heads):
        for i in reversed(range(SPLIT)):
            first, keys, kept = blocks[i]
            attend_back(h, first, keys, kept, i == SPLIT - 1)
            pair_sums(1)
        for i in range(SPLIT):
            span = slice(i * rows, (i + 1) * rows)
            at = padded + h * LANES
            r.mixb[span, at : at + LANES] = unrotate(upright(r.dk[:, span]), span)
            at = 2 * padded + h * LANES
            r.mixb[span, at : at + LANES] = upright(r.dv[:, span]).astype(BF)
        if h < heads - 1:
            head_tiles(h)
            if z.inside:
                spreads[f"at{h}"].send()
                waiting.extend((f"at{h}", i) for i in range(1, z.groups + 1))
    scatter1.close()

    def first_norm_part(c, carry):
        put(r.part1, c, dot(take(r.mixb, c), r.wap[...]).astype(BF))
        scatter4.send(c)
        return carry

    lax.fori_loop(0, CHUNKS, first_norm_part, 0)
    for c in range(CHUNKS):
        scatter4.middle(c)
    head_tiles(heads - 1)
    if z.inside:
        spreads[f"at{heads - 1}"].send()
    pair_sums(len(waiting))

    def block_out(c, carry):
        span = scatter2.span(c)
        r.block_out[span] = (r.after[span] + scatter2.finish(c)).astype(BF)
        return carry

    lax.fori_loop(0, CHUNKS, block_out, 0)

    def first_back(c, carry):
        span = scatter4.span(c)
        grad = scatter4.finish(c)
        row_grad, total = norm_back(grad, r.inputs[span], r.scale1[span, 0:1], r.gain1[...][None, :])
        r.sums[0, 0:1] += total
        embed_grad = r.aftergrad[span] + row_grad
        r.embed_grad[span] = embed_grad
        r.lifted[span] = embed_grad.astype(BF)
        return carry

    lax.fori_loop(0, CHUNKS, first_back, 0)

    row_back = dot_right(r.lifted[...], r.nw[...]).astype(BF)
    low_table = lane_of((slots, z.pair_width)) < z.table_width
    outgoing = jnp.where(low_table, dot(r.pick_t[0], row_back), dot(r.pick_t[1], row_back))
    r.back_out[...] = outgoing.astype(BF)

    def back_slots(block, of):
        return r.back_in.at[pl.ds(pl.multiple_of(block * slots + of * cap, cap), cap)]

    def back_copy(step, incoming=False):
        to = peer(step)
        src = r.back_out.at[pl.ds(pl.multiple_of(to * cap, cap), cap)]
        dst = back_slots(p.t, to if incoming else p.d)
        recv = r.back_sem.at[1, to if incoming else p.d]
        return make_copy(src, dst, r.back_sem.at[0, 0], recv, dp=to)

    def pass_copy(kind, of, incoming=False):
        block = ((p.t, p.t1), (p.t, p.t2), (p.t2, p.t3))[kind][1 if incoming else 0]
        ref = back_slots(block, of)
        target = p.t2 if kind == 1 else p.t1
        return make_copy(
            ref, ref, r.pass_sem.at[2 * kind, of], r.pass_sem.at[2 * kind + 1, of], tensor=target
        )

    for step in range(1, n):
        back_copy(n - step).start()
    own_block = pl.ds(pl.multiple_of(p.t * slots + p.d * cap, cap), cap)
    r.back_in[own_block] = r.back_out[own_slots]

    gains = jnp.concatenate(
        [r.sums[0, 0:1], r.sums[1, 0:1], jnp.zeros((LANES - 2, width), F32)], axis=0
    )
    small = jnp.concatenate([dot(r.lifted[...].T, r.grams[...]), gains.T], axis=1)
    if z.inside:
        for j in range(n * SPLIT):
            value = small[j * z.small : (j + 1) * z.small].astype(BF)
            r.sm_part[j % SPLIT, j // SPLIT] = value

        def small_near(slot):
            block = p.t3 if slot else p.t1
            return make_copy(
                r.sm_part.at[block],
                r.sm_near.at[slot],
                r.sm_sem.at[2 * slot],
                r.sm_sem.at[2 * slot + 1],
                tensor=p.t1,
            )

        small_far = make_copy(r.sm_send, r.sm_far, r.sm_sem.at[4], r.sm_sem.at[5], tensor=p.t2)

        def small_copy(step, incoming=False):
            to = peer(step)
            at = to if incoming else p.d
            return make_copy(
                r.sm_out.at[to], r.sm_in.at[at], r.sp_sem.at[0, 0], r.sp_sem.at[1, at], dp=to
            )

        small_near(1).start()
        small_near(0).start()
        small_near(1).wait_recv()
        r.sm_send[...] = (r.sm_part[p.t2].astype(F32) + r.sm_near[1].astype(F32)).astype(BF)
        small_far.start()
    else:
        r.sm_total[...] = small

    pass_copy(0, p.d).start()
    pass_copy(1, p.d).start()
    for step in range(1, n):
        back_copy(step, True).wait_recv()
        pass_copy(1, peer(step)).start()
        pass_copy(0, peer(step)).start()
    if z.inside:
        small_near(0).wait_recv()
        small_far.wait_recv()
        total = r.sm_part[p.t].astype(F32) + r.sm_near[0].astype(F32) + r.sm_far[...].astype(F32)
        r.sm_out[...] = total.astype(BF)
        for step in range(1, n):
            small_copy(step).start()
        r.sm_in[p.d] = r.sm_out[p.d]
        for step in range(1, z.groups + 1):
            spreads[f"at{heads - 1}"].middle(step)
    for step in range(n):
        of = peer(step)
        pass_copy(1, of, True).wait_recv()
        pass_copy(2, of).start()
    for i in range(3):
        lid_copy(i, True).wait_recv()
    kept = z.table_rows // SPLIT
    low_table = lane_of((kept, LANES)) < HD
    wanted = row_of((kept, slots)) + p.t * kept

    def add_rows(b, fresh=False):
        block = pl.ds(pl.multiple_of(b * slots, slots), slots)
        hits = [onehot(r.lids[b, k][0:1] == wanted) for k in range(2)]
        left = dot(hits[0], r.back_in[block, 0 : 2 * LANES])
        right = dot(hits[1], r.back_in[block, LANES : 3 * LANES])
        sums = (left[:, :LANES], jnp.where(low_table, left[:, LANES:], right[:, :LANES]), right[:, LANES:])
        for g, value in enumerate(sums):
            at = slice(g * LANES, (g + 1) * LANES)
            r.table_grads[:, at] = value if fresh else r.table_grads[:, at] + value

    add_rows(p.t, True)
    for step in range(n):
        pass_copy(0, peer(step), True).wait_recv()
    add_rows(p.t1)
    add_rows(p.t2)
    for step in range(n):
        pass_copy(2, peer(step), True).wait_recv()
    add_rows(p.t3)

    if z.inside:
        for step in range(1, n):
            small_copy(step, True).wait_recv()
        r.sm_total[...] = jnp.sum(r.sm_in[...].astype(F32), axis=0)
        for spread in spreads.values():
            spread.finish()

    all_ids.wait_send()
    shared = [(r.rows_out, r.row_sem, cap), (r.back_out, r.back_sem, cap)]
    if z.inside:
        shared.append((r.sm_out, r.sp_sem, 1))
    for ref, sems, each in shared:
        ref = ref.at[pl.ds(0, (n - 1) * each)]
        make_copy(ref, ref, sems.at[0, 0], sems.at[1, 0], dp=peer(1)).wait_send()
    for i in range(3):
        lid_copy(i).wait_send()
    for gather in (gather1, gather2, gather3):
        gather.close()
    for scatter in scatters[1:]:
        scatter.close()
    for spread in spreads.values():
        spread.close()
    if z.inside:
        small_near(0).wait_send()
        small_near(1).wait_send()
        small_far.wait_send()
    for step in range(n):
        for kind in range(3):
            pass_copy(kind, peer(step)).wait_send()


def finish_kernel(z, names, *refs):
    r = Refs(names, refs)
    r.block[...] = r.block_out[...]
    r.embed[...] = r.embed_grad[...]
    r.bigram[...] = r.table_grads[:, : 2 * LANES].T[: z.table_width]
    r.trigram[...] = r.table_grads[:, LANES:].T[2 * LANES - z.table_width :]
    r.ngram[...] = r.sm_total[:, : z.pair_width]
    gains = r.sm_total[:, z.pair_width :]
    r.first[...] = gains[:, 0:1].T
    r.second[...] = gains[:, 1:2].T
    r.gate[...] = r.gu_out[:, : z.units]
    r.up[...] = r.gu_out[:, z.units :]
    r.down[...] = r.dn_out[...]
    side = 3 * HD
    for h in range(z.heads):
        sums = getattr(r, f"at{h}_out")[...]
        r.attend[:, h * side : (h + 1) * side] = sums[:, :side]
        r.output[h * HD : (h + 1) * HD] = sums[:, LANES:].T[HD:]


def finish_outputs(z, got):
    kept = z.table_rows // SPLIT
    outs = dict(
        block=((z.rows, z.width), BF),
        embed=((z.rows, z.width), F32),
        bigram=((z.table_width, kept), F32),
        trigram=((z.table_width, kept), F32),
        ngram=((z.small, z.pair_width), F32),
        first=((1, z.small), F32),
        attend=((z.piece, 3 * HD * z.heads), F32),
        output=((HD * z.heads, z.piece), F32),
        second=((1, z.small), F32),
        gate=((z.piece, z.units), F32),
        up=((z.piece, z.units), F32),
        down=((z.piece, z.units), F32),
    )
    done = pl.pallas_call(
        functools.partial(finish_kernel, z, (*got, *outs)),
        out_shape=[jax.ShapeDtypeStruct(*item) for item in outs.values()],
        in_specs=[pl.BlockSpec(memory_space=pltpu.VMEM)] * len(got),
        out_specs=[pl.BlockSpec(memory_space=pltpu.VMEM)] * len(outs),
        name="finish",
    )(*got.values())
    done = dict(zip(outs, done, strict=True))
    for name in ("bigram", "trigram", "ngram", "down"):
        done[name] = done[name].T
    for name in ("first", "second"):
        done[name] = done[name].reshape(z.small)
    return tuple(done.values())


def shards(
    embedded,
    bigram_ids,
    trigram_ids,
    prefix_lens,
    bigram_table,
    trigram_table,
    ngram_weight,
    first_gain,
    attend_weight,
    output_weight,
    second_gain,
    gate_weight,
    up_weight,
    down_weight,
    cotangent,
):
    n = lax.axis_size("dp")
    rows, width = embedded.shape
    table_rows, table_width = bigram_table.shape
    heads, units = attend_weight.shape[1] // (3 * HD), gate_weight.shape[1]
    z = Sizes(n, rows, width, heads, units, table_rows, table_width)
    scratch, outs = scratch_of(z), outputs_of(z)
    names = (*INPUTS, *outs, *scratch)
    anywhere = pl.BlockSpec(memory_space=pl.ANY)
    in_specs = [anywhere] * len(INPUTS)
    in_specs[3] = pl.BlockSpec(memory_space=pltpu.SMEM)
    got = pl.pallas_call(
        functools.partial(block_kernel, z, names),
        out_shape=[jax.ShapeDtypeStruct(*item) for item in outs.values()],
        in_specs=in_specs,
        out_specs=[pl.BlockSpec(memory_space=pltpu.VMEM)] * len(outs),
        scratch_shapes=list(scratch.values()),
        compiler_params=pltpu.CompilerParams(
            collective_id=0, has_side_effects=True, vmem_limit_bytes=67043328
        ),
        name="block",
    )(
        embedded,
        bigram_ids.reshape(1, rows),
        trigram_ids.reshape(1, rows),
        prefix_lens,
        bigram_table.T,
        trigram_table.T,
        ngram_weight,
        first_gain,
        attend_weight.T,
        output_weight,
        second_gain,
        gate_weight,
        up_weight,
        down_weight,
        cotangent,
    )
    got = dict(zip(outs, got, strict=True))
    if not z.inside:

        def summed(part, axes):
            return lax.psum_scatter(part, axes, scatter_dimension=0, tiled=True)

        for name in ("gu", "dn", *(f"at{h}" for h in range(heads))):
            got[f"{name}_out"] = summed(got.pop(f"{name}_part").astype(F32), "dp")
        got["sm_total"] = summed(got["sm_total"], ("dp", "tensor"))
    return finish_outputs(z, got)


def solution(mesh):
    placed = (
        P(("dp", "tensor"), None),
        P(("dp", "tensor")),
        P(("dp", "tensor")),
        P("dp"),
        P("dp", None),
        P("dp", None),
        P(),
        P(),
        P(None, "tensor"),
        P("tensor", None),
        P(),
        P(None, "tensor"),
        P(None, "tensor"),
        P("tensor", None),
        P("dp", None),
    )
    return jax.shard_map(
        shards,
        mesh=mesh,
        in_specs=placed,
        out_specs=(
            P(("dp", "tensor"), None),
            P(("dp", "tensor"), None),
            P(("dp", "tensor"), None),
            P(("dp", "tensor"), None),
            P(None, ("dp", "tensor")),
            P(("dp", "tensor")),
            P("dp", "tensor"),
            P("tensor", "dp"),
            P(("dp", "tensor")),
            P("dp", "tensor"),
            P("dp", "tensor"),
            P("tensor", "dp"),
        ),
        check_vma=False,
    )
```

```python
import functools
import math

import jax
import jax.numpy as jnp
from jax import lax
from jax.experimental import pallas as pl
from jax.experimental.pallas import tpu as pltpu
from jax.sharding import PartitionSpec as P

BF = jnp.bfloat16
F32 = jnp.float32
HD = 64
LANES = 128
PREFIX_MOST = 512
SPLIT = 4
CHUNKS = 4

INPUTS = (
    "embedded", "bigram_ids", "trigram_ids", "prefix", "bigram_table", "trigram_table",
    "ngram_weight", "first_gain", "attend_weight", "output_weight", "second_gain",
    "gate_weight", "up_weight", "down_weight", "cotangent",
)


class Refs:
    def __init__(self, names, refs):
        self.__dict__.update(zip(names, refs, strict=True))


def dot(left, right):
    return jnp.dot(left, right, preferred_element_type=F32)


def dot_right(left, right):
    return lax.dot_general(left, right, (((1,), (1,)), ((), ())), preferred_element_type=F32)


def lane_of(shape):
    return lax.broadcasted_iota(jnp.int32, shape, len(shape) - 1)


def row_of(shape):
    return lax.broadcasted_iota(jnp.int32, shape, 0)


def onehot(test):
    return jnp.where(test, 1.0, 0.0).astype(BF)


def roll64(block):
    return pltpu.roll(block, 64, 1)


def swap_halves(block):
    return jnp.where(lane_of(block.shape) < 32, pltpu.roll(block, 96, 1), pltpu.roll(block, 32, 1))


class Sizes:
    def __init__(self, n, rows, width, heads, units, table_rows, table_width):
        self.n, self.rows, self.width, self.heads, self.units = n, rows, width, heads, units
        self.table_rows, self.table_width = table_rows, table_width
        self.length = rows * SPLIT
        self.keys = [max((i + 1) * rows, min(PREFIX_MOST, rows * SPLIT)) for i in range(SPLIT)]
        self.cap = max(16, 2 * rows // n)
        self.slots = n * self.cap
        self.padded = heads * LANES
        self.chunk = rows // CHUNKS
        self.piece = width // n
        self.pair_width = 2 * table_width
        self.small = width // (n * SPLIT)
        self.small_lanes = self.pair_width + LANES
        self.attn_lanes = 4 * HD
        self.inside = n == 8 and self.piece % 16 == 0 and self.small % 8 == 0


def make_copy(src, dst, send, recv, **where):
    return pltpu.make_async_remote_copy(
        src_ref=src, dst_ref=dst, send_sem=send, recv_sem=recv, device_id=where
    )


class Gather:
    def __init__(self, z, pos, full, sems):
        self.z, self.pos, self.full, self.sems = z, pos, full, sems

    def piece(self, block, c):
        start = pl.multiple_of(block * self.z.rows + c * self.z.chunk, self.z.chunk)
        return self.full.at[pl.ds(start, self.z.chunk)]

    def copy(self, kind, c, incoming=False):
        p = self.pos
        block = ((p.t, p.t1), (p.t, p.t2), (p.t2, p.t3))[kind][1 if incoming else 0]
        ref = self.piece(block, c)
        target = p.t2 if kind == 1 else p.t1
        return make_copy(
            ref, ref, self.sems.at[c, 2 * kind], self.sems.at[c, 2 * kind + 1], tensor=target
        )

    def send(self, c):
        self.copy(1, c).start()
        self.copy(0, c).start()

    def receive(self, c):
        self.copy(1, c, True).wait_recv()
        self.copy(2, c).start()
        self.copy(0, c, True).wait_recv()
        self.copy(2, c, True).wait_recv()

    def close(self):
        def body(c, carry):
            for kind in range(3):
                self.copy(kind, c).wait_send()
            return carry

        lax.fori_loop(0, CHUNKS, body, 0)


class Scatter:
    def __init__(self, z, pos, part, near, out, far, sems):
        self.z, self.pos, self.part, self.near = z, pos, part, near
        self.out, self.far, self.sems = out, far, sems

    def span(self, c):
        return pl.ds(pl.multiple_of(c * self.z.chunk, self.z.chunk), self.z.chunk)

    def rows(self, block, c):
        start = pl.multiple_of(block * self.z.rows + c * self.z.chunk, self.z.chunk)
        return pl.ds(start, self.z.chunk)

    def near_copy(self, slot, c):
        block = self.pos.t1 + slot * (self.pos.t3 - self.pos.t1)
        return make_copy(
            self.part.at[self.rows(block, c)],
            self.near.at[slot, self.span(c)],
            self.sems.at[c, 2 * slot],
            self.sems.at[c, 2 * slot + 1],
            tensor=self.pos.t1,
        )

    def far_copy(self, c):
        return make_copy(
            self.out.at[self.span(c)],
            self.far.at[self.span(c)],
            self.sems.at[c, 4],
            self.sems.at[c, 5],
            tensor=self.pos.t2,
        )

    def send(self, c):
        self.near_copy(1, c).start()
        self.near_copy(0, c).start()

    def middle(self, c):
        self.near_copy(1, c).wait_recv()
        own = self.part[self.rows(self.pos.t2, c)].astype(F32)
        self.out[self.span(c)] = (own + self.near[1, self.span(c)].astype(F32)).astype(BF)
        self.far_copy(c).start()

    def finish(self, c):
        self.near_copy(0, c).wait_recv()
        self.far_copy(c).wait_recv()
        own = self.part[self.rows(self.pos.t, c)].astype(F32)
        own = own + self.near[0, self.span(c)].astype(F32)
        return own + self.far[self.span(c)].astype(F32)

    def close(self):
        def body(c, carry):
            self.near_copy(0, c).wait_send()
            self.near_copy(1, c).wait_send()
            self.far_copy(c).wait_send()
            return carry

        lax.fori_loop(0, CHUNKS, body, 0)


class Spread:
    STEPS = 4

    def __init__(self, z, pos, part, pair_in, next_out, next_in, out, sems):
        self.z, self.pos, self.part, self.pair_in = z, pos, part, pair_in
        self.next_out, self.next_in, self.out, self.sems = next_out, next_in, out, sems
        near = pos.place + 1 - 2 * lax.rem(pos.place, 2)
        far = lax.rem(pos.place + 2, 4)
        both = lax.rem(near + 2, 4)
        self.order = (both, near, far, pos.place)

    def rows(self, peer):
        return pl.ds(pl.multiple_of(peer * self.z.piece, self.z.piece), self.z.piece)

    def pair_copy(self, step):
        return make_copy(
            self.part.at[self.rows(self.order[step] * 2 + 1 - self.pos.parity)],
            self.pair_in.at[step],
            self.sems.at[0, step],
            self.sems.at[1, step],
            dp=self.pos.partner,
        )

    def next_copy(self, step):
        place = self.order[1] if step < 2 else self.order[2]
        return make_copy(
            self.next_out.at[step],
            self.next_in.at[step],
            self.sems.at[2, step],
            self.sems.at[3, step],
            dp=place * 2 + self.pos.parity,
        )

    def send(self):
        for step in range(4):
            self.pair_copy(step).start()

    def middle(self, step):
        self.pair_copy(step).wait_recv()
        own = self.part[self.rows(self.order[step] * 2 + self.pos.parity)].astype(F32)
        total = own + self.pair_in[step].astype(F32)
        if step >= 2:
            self.next_copy(step - 2).wait_recv()
            total = total + self.next_in[step - 2].astype(F32)
        if step == 3:
            self.out[...] = total
        else:
            self.next_out[step] = total.astype(BF)
            self.next_copy(step).start()

    def finish(self):
        self.next_copy(2).wait_recv()
        self.out[...] += self.next_in[2].astype(F32)

    def close(self):
        for step in range(4):
            self.pair_copy(step).wait_send()
            if step < 3:
                self.next_copy(step).wait_send()


class Position:
    def __init__(self, z):
        self.d, self.t = lax.axis_index("dp"), lax.axis_index("tensor")
        core, side = lax.rem(self.t, 2), self.t // 2
        self.t1 = self.t + 1 - 2 * core
        self.t2 = self.t + 2 - 4 * side
        self.t3 = self.t1 + 2 - 4 * side
        self.parity, self.place = lax.rem(self.d, 2), self.d // 2
        self.partner = self.d + 1 - 2 * self.parity


def scratch_of(z):
    n, rows, width, length, chunks = z.n, z.rows, z.width, z.length, CHUNKS
    vmem, dma = pltpu.VMEM, pltpu.SemaphoreType.DMA
    shapes = dict(
        emb=vmem((rows, width), BF),
        ids=vmem((2 * n, 1, rows), jnp.int32),
        own_ids=vmem((2, 1, rows), jnp.int32),
        table_b=vmem((z.table_width, z.table_rows), BF),
        table_t=vmem((z.table_width, z.table_rows), BF),
        nw=vmem((z.pair_width, width), BF),
        gain1=vmem((width,), F32),
        gain2=vmem((width,), F32),
        wap=vmem((3 * z.padded, width), BF),
        wop=vmem((z.padded, width), BF),
        wgu=vmem((width, 2 * z.units), BF),
        wd=vmem((z.units, width), BF),
        cot=vmem((length, width), BF),
        cosine=vmem((length, LANES), F32),
        sines=vmem((length, LANES), F32),
        pick=vmem((2, rows, z.slots), BF),
        pick_t=vmem((2, z.slots, rows), BF),
        lids=vmem((SPLIT, 2, 8, z.slots), jnp.int32),
        rows_out=vmem((z.slots, z.pair_width), BF),
        rows_in=vmem((z.slots, z.pair_width), BF),
        grams=vmem((rows, z.pair_width), BF),
        inputs=vmem((rows, width), F32),
        after=vmem((rows, width), F32),
        aftergrad=vmem((rows, width), F32),
        inverse=vmem((length, LANES), F32),
        scale1=vmem((rows, LANES), F32),
        scale2=vmem((rows, LANES), F32),
        n1=vmem((length, width), BF),
        n2=vmem((length, width), BF),
        ab=vmem((length, width), BF),
        q=vmem((length, z.padded), BF),
        k=vmem((length, z.padded), BF),
        v=vmem((length, z.padded), BF),
        probs0=vmem((z.heads, rows, z.keys[0]), BF),
        probs1=vmem((z.heads, rows, z.keys[1]), BF),
        probs2=vmem((z.heads, rows, z.keys[2]), BF),
        probs3=vmem((z.heads, rows, z.keys[3]), BF),
        att=vmem((length, z.padded), BF),
        do=vmem((length, z.padded), BF),
        dk=vmem((HD, length), F32),
        dv=vmem((HD, length), F32),
        mixb=vmem((length, 3 * z.padded), BF),
        act=vmem((length, z.units), BF),
        gub=vmem((max(length, width), 2 * z.units), BF),
        lifted=vmem((rows, width), BF),
        sums=vmem((2, 8, width), F32),
        back_out=vmem((z.slots, z.pair_width), BF),
        back_in=vmem((SPLIT * z.slots, z.pair_width), BF),
        in_sem=dma((12 + 4 * z.heads,)),
        id_sem=dma((2,)),
        row_sem=dma((2, n)),
        lid_sem=dma((2, 3)),
        back_sem=dma((2, n)),
        pass_sem=dma((6, n)),
        ag1_sem=dma((chunks, 6)),
        ag2_sem=dma((chunks, 6)),
        ag3_sem=dma((chunks, 6)),
    )
    for k in range(1, 4):
        shapes[f"part{k}"] = vmem((length, width), BF)
        shapes[f"near{k}"] = vmem((2, rows, width), BF)
        shapes[f"send{k}"] = vmem((rows, width), BF)
        shapes[f"far{k}"] = vmem((rows, width), BF)
        shapes[f"rs{k}_sem"] = dma((chunks, 6))
    shapes["rs4_sem"] = dma((chunks, 6))
    if z.inside:
        heads = [(f"at{h}", z.attn_lanes) for h in range(z.heads)]
        for name, lanes in (("gu", 2 * z.units), ("dn", z.units), *heads):
            shapes[f"{name}_part"] = vmem((width, lanes), BF)
            shapes[f"{name}_pair_in"] = vmem((4, z.piece, lanes), BF)
            shapes[f"{name}_next_out"] = vmem((3, z.piece, lanes), BF)
            shapes[f"{name}_next_in"] = vmem((3, z.piece, lanes), BF)
            shapes[f"{name}_sem"] = dma((4, 4))
        small = (n, z.small, z.small_lanes)
        shapes["sm_part"] = vmem((SPLIT, *small), BF)
        shapes["sm_near"] = vmem((2, *small), BF)
        shapes["sm_send"] = vmem(small, BF)
        shapes["sm_far"] = vmem(small, BF)
        shapes["sm_out"] = vmem(small, BF)
        shapes["sm_in"] = vmem(small, BF)
        shapes["sm_sem"] = dma((6,))
        shapes["sp_sem"] = dma((2, n))
    return shapes


def outputs_of(z):
    n, rows, width = z.n, z.rows, z.width
    shapes = dict(
        block_out=((rows, width), BF),
        embed_grad=((rows, width), F32),
        table_grads=((z.table_rows // SPLIT, z.pair_width), F32),
    )
    if z.inside:
        shapes["gu_out"] = ((z.piece, 2 * z.units), F32)
        shapes["dn_out"] = ((z.piece, z.units), F32)
        for h in range(z.heads):
            shapes[f"at{h}_out"] = ((z.piece, z.attn_lanes), F32)
        shapes["sm_total"] = ((z.small, z.small_lanes), F32)
    else:
        shapes["gu_part"] = ((width, 2 * z.units), BF)
        shapes["dn_part"] = ((width, z.units), BF)
        for h in range(z.heads):
            shapes[f"at{h}_part"] = ((width, z.attn_lanes), BF)
        shapes["sm_total"] = ((width, z.small_lanes), F32)
    return shapes


def block_kernel(z, names, *refs):
    r = Refs(names, refs)
    p = Position(z)
    n, rows, width, length = z.n, z.rows, z.width, z.length
    cap, slots, units, padded, heads = z.cap, z.slots, z.units, z.padded, z.heads
    gather1 = Gather(z, p, r.n1, r.ag1_sem)
    gather2 = Gather(z, p, r.n2, r.ag2_sem)
    gather3 = Gather(z, p, r.ab, r.ag3_sem)
    scatters = [
        Scatter(
            z, p, getattr(r, f"part{k}"), getattr(r, f"near{k}"), getattr(r, f"send{k}"),
            getattr(r, f"far{k}"), sems,
        )
        for k, sems in ((1, r.rs1_sem), (2, r.rs2_sem), (3, r.rs3_sem), (1, r.rs4_sem))
    ]
    scatter1, scatter2, scatter3, scatter4 = scatters
    spreads = {}
    if z.inside:
        for name in ("gu", "dn", *(f"at{h}" for h in range(heads))):
            spreads[name] = Spread(
                z, p, getattr(r, f"{name}_part"), getattr(r, f"{name}_pair_in"),
                getattr(r, f"{name}_next_out"), getattr(r, f"{name}_next_in"),
                getattr(r, f"{name}_out"), getattr(r, f"{name}_sem"),
            )

    def peer(step):
        return lax.rem(p.d + step, n)

    barrier = pltpu.get_barrier_semaphore()
    for step in range(1, n):
        pl.semaphore_signal(barrier, inc=1, device_id={"dp": peer(step)})
    for target in (p.t1, p.t2, p.t3):
        pl.semaphore_signal(barrier, inc=1, device_id={"tensor": target})

    loads = [
        (r.bigram_ids, r.own_ids.at[0]),
        (r.trigram_ids, r.own_ids.at[1]),
        (r.bigram_table, r.table_b),
        (r.trigram_table, r.table_t),
        (r.embedded, r.emb),
        (r.ngram_weight, r.nw),
        (r.first_gain, r.gain1),
        (r.second_gain, r.gain2),
        (r.gate_weight, r.wgu.at[:, pl.ds(0, units)]),
        (r.up_weight, r.wgu.at[:, pl.ds(units, units)]),
        (r.down_weight, r.wd),
        (r.cotangent, r.cot),
    ]
    for h in range(heads):
        for c in range(3):
            src = r.attend_weight.at[pl.ds((3 * h + c) * HD, HD)]
            loads.append((src, r.wap.at[pl.ds(c * padded + h * LANES, HD)]))
        src = r.output_weight.at[pl.ds(h * HD, HD)]
        loads.append((src, r.wop.at[pl.ds(h * LANES, HD)]))
    loads = [pltpu.make_async_copy(src, dst, r.in_sem.at[i]) for i, (src, dst) in enumerate(loads)]
    for load in loads:
        load.start()

    pl.semaphore_wait(barrier, n - 1 + 3)

    def id_copy(step, k):
        return make_copy(
            (r.bigram_ids, r.trigram_ids)[k],
            r.ids.at[k * n + p.d],
            r.id_sem.at[0],
            r.id_sem.at[1],
            dp=peer(step),
        )

    for step in range(1, n):
        for k in range(2):
            id_copy(step, k).start()

    lane = lane_of((32, LANES))
    low = jnp.where(lane < 32, lane, lane - 32)
    frequency = jnp.exp(low.astype(F32) * (-2.0 * math.log(10000.0) / HD))
    place = row_of((32, LANES)).astype(F32)
    coarse, fine = place * 32.0 * frequency, place * frequency
    cos_coarse, sin_coarse = jnp.cos(coarse), jnp.sin(coarse)
    used = lane < HD
    cos_fine = jnp.where(used, jnp.cos(fine), 0.0)
    sin_fine = jnp.where(used, jnp.sin(fine), 0.0)
    sign = jnp.where(lane < 32, -1.0, 1.0)
    for a in range(length // 32):
        ca, sa = cos_coarse[a : a + 1], sin_coarse[a : a + 1]
        r.cosine[a * 32 : (a + 1) * 32] = ca * cos_fine - sa * sin_fine
        r.sines[a * 32 : (a + 1) * 32] = sign * (sa * cos_fine + ca * sin_fine)

    loads[0].wait()
    loads[1].wait()
    earlier = onehot(row_of((rows, rows)) < lane_of((rows, rows)))
    later = onehot(row_of((rows, rows)) > lane_of((rows, rows)))
    for k in range(2):
        r.ids[k * n + p.d] = r.own_ids[k]
        own = jnp.broadcast_to(r.own_ids[k].astype(F32), (LANES, rows))
        column = own.T
        start = (lane_of((rows, LANES)) * z.table_rows).astype(F32)
        held = (column >= start) & (column < start + z.table_rows)
        ranks = dot(later, onehot(held))
        slot = jnp.where(held, ranks + (lane_of((rows, LANES)) * cap).astype(F32), 0.0)
        slot = jnp.sum(slot, axis=1, keepdims=True)
        r.pick[k] = onehot(slot.astype(jnp.int32) == lane_of((rows, slots)))
        across = jnp.broadcast_to(slot, (rows, LANES)).T[0:1]
        r.pick_t[k] = onehot(across.astype(jnp.int32) == row_of((slots, rows)))

    for h in range(heads):
        empty = jnp.zeros((LANES - HD, width), BF)
        for c in range(3):
            at = c * padded + h * LANES + HD
            r.wap[at : at + LANES - HD] = empty
        r.wop[h * LANES + HD : (h + 1) * LANES] = empty

    loads[2].wait()
    loads[3].wait()
    all_ids = r.ids.at[pl.ds(0, 2 * (n - 1))]
    all_ids = make_copy(all_ids, all_ids, r.id_sem.at[0], r.id_sem.at[1], dp=peer(1))
    all_ids.wait_recv()
    asked = jnp.concatenate([r.ids[i] for i in range(2 * n)], axis=0)
    first_row = p.d * z.table_rows
    mine = (asked >= first_row) & (asked < first_row + z.table_rows)
    ranks = dot(onehot(mine), earlier)
    tags = jnp.where(mine, ranks, -1.0).astype(jnp.int32)
    local = jnp.where(mine, asked - first_row + 1, 0).astype(F32)
    picked = []
    for k in range(2):
        columns = []
        for i in range(n):
            at = k * n + i
            hit = tags[at : at + 1] == row_of((cap, rows))
            value = jnp.where(hit, local[at : at + 1], 0.0)
            columns.append(jnp.sum(value, axis=1, keepdims=True) - 1.0)
        column = jnp.concatenate(columns, axis=0)
        picked.append(column.astype(jnp.int32))
        across = jnp.broadcast_to(column, (slots, LANES)).T[0:8]
        r.lids[p.t, k] = across.astype(jnp.int32)
    half = slots // 2

    def row_copy(step):
        to = peer(step)
        return make_copy(
            r.rows_out.at[pl.ds(pl.multiple_of(to * cap, cap), cap)],
            r.rows_in.at[pl.ds(pl.multiple_of(p.d * cap, cap), cap)],
            r.row_sem.at[0, 0],
            r.row_sem.at[1, p.d],
            dp=to,
        )

    def row_arrival(step):
        of = peer(step)
        ref = r.rows_in.at[pl.ds(pl.multiple_of(of * cap, cap), cap)]
        return make_copy(ref, ref, r.row_sem.at[0, 0], r.row_sem.at[1, of], dp=of)

    for part in range(2):
        found = []
        for k, table in enumerate((r.table_b, r.table_t)):
            chosen = picked[k][part * half : (part + 1) * half]
            hits = onehot(chosen == lane_of((half, z.table_rows)))
            both = dot_right(hits, table[...])
            fill = jnp.zeros((half, 2 * LANES - z.table_width), F32)
            found.append((both[:, :LANES], jnp.concatenate([both[:, LANES:], fill], axis=1)))
        low_half = lane_of((half, LANES)) < HD
        rolled = [roll64(block) for block in found[1]]
        span = slice(part * half, (part + 1) * half)
        r.rows_out[span, 0:LANES] = found[0][0].astype(BF)
        middle = jnp.where(low_half, found[0][1], rolled[0])
        r.rows_out[span, LANES : 2 * LANES] = middle.astype(BF)
        r.rows_out[span, 2 * LANES :] = jnp.where(low_half, rolled[0], rolled[1]).astype(BF)
    for step in range(1, n):
        row_copy(n - step).start()
    own_slots = pl.ds(pl.multiple_of(p.d * cap, cap), cap)
    r.rows_in[own_slots] = r.rows_out[own_slots]

    for load in loads[4:8]:
        load.wait()
    for step in range(1, n):
        row_arrival(step).wait_recv()
    fetched = r.rows_in[...]
    low_table = lane_of((rows, z.pair_width)) < z.table_width
    grams = jnp.where(low_table, dot(r.pick[0], fetched), dot(r.pick[1], fetched)).astype(BF)
    r.grams[...] = grams
    inputs = r.emb[...].astype(F32) + dot(grams, r.nw[...])
    r.inputs[...] = inputs
    scale = lax.rsqrt(jnp.mean(inputs * inputs, axis=1, keepdims=True) + 1e-05)
    r.scale1[...] = jnp.broadcast_to(scale, (rows, LANES))
    own_rows = pl.ds(pl.multiple_of(p.t * rows, rows), rows)
    r.n1[own_rows] = (inputs * scale * r.gain1[...][None, :]).astype(BF)
    for c in range(CHUNKS):
        gather1.send(c)

    def lid_copy(i, incoming=False):
        target = (p.t1, p.t2, p.t3)[i]
        ref = r.lids.at[target if incoming else p.t]
        return make_copy(ref, ref, r.lid_sem.at[0, i], r.lid_sem.at[1, i], tensor=target)

    for i in range(3):
        lid_copy(i).start()

    def spans(c):
        return [
            pl.ds(pl.multiple_of(b * rows + c * z.chunk, z.chunk), z.chunk) for b in range(SPLIT)
        ]

    def take(ref, c, *rest):
        return jnp.concatenate([ref[(span, *rest)] for span in spans(c)], axis=0)

    def put(ref, c, value, *rest):
        for b, span in enumerate(spans(c)):
            ref[(span, *rest)] = value[b * z.chunk : (b + 1) * z.chunk]

    for load in loads[8:]:
        load.wait()

    def project(c, carry):
        gather1.receive(c)
        mixture = dot_right(take(r.n1, c), r.wap[...])
        cosine, sines = take(r.cosine, c), take(r.sines, c)
        for h in range(heads):
            for i, ref in enumerate((r.q, r.k)):
                at = i * padded + h * LANES
                block = mixture[:, at : at + LANES]
                turned = block * cosine + swap_halves(block) * sines
                if i == 0:
                    turned = turned * (HD**-0.5 * math.log2(math.e))
                put(ref, c, turned.astype(BF), slice(h * LANES, (h + 1) * LANES))
            at = 2 * padded + h * LANES
            block = mixture[:, at : at + LANES]
            block = jnp.where(lane_of(block.shape) == HD, 1.0, block)
            put(r.v, c, block.astype(BF), slice(h * LANES, (h + 1) * LANES))
        return carry

    lax.fori_loop(0, CHUNKS, project, 0)

    prefix = r.prefix[0]
    probs = (r.probs0, r.probs1, r.probs2, r.probs3)
    blocks = [(i * rows, z.keys[i], probs[i]) for i in range(SPLIT)]

    def head_lanes(h):
        return pl.ds(pl.multiple_of(h * LANES, LANES), LANES)

    def attend(first, keys, kept):
        span = slice(first, first + rows)
        lane = lane_of((rows, LANES))
        row, column = row_of((rows, rows)), lane_of((rows, rows))

        def one_head(h, inverses):
            at = head_lanes(h)
            query = r.q[span, at]
            tiles = []
            for start in range(0, keys, rows):
                scores = dot_right(query, r.k[start : start + rows, at])
                allowed = None
                if start == first:
                    allowed = column <= row
                if start + rows > first + 1 and start < PREFIX_MOST:
                    in_prefix = column < prefix - start
                    allowed = in_prefix if allowed is None else allowed | in_prefix
                if allowed is not None:
                    scores = jnp.where(allowed, scores, -1000000000.0)
                tiles.append(scores)
            highest = functools.reduce(jnp.maximum, tiles)
            highest = jnp.max(highest, axis=1, keepdims=True)
            total = jnp.zeros((rows, LANES), F32)
            for j, scores in enumerate(tiles):
                weights = jnp.exp2(scores - highest).astype(BF)
                kept[h, :, j * rows : (j + 1) * rows] = weights
                total = total + dot(weights, r.v[j * rows : (j + 1) * rows, at])
            inverse = 1.0 / total[:, HD : HD + 1]
            r.att[span, at] = jnp.where(lane < HD, total * inverse, 0.0).astype(BF)
            return jnp.where(lane == h, inverse, inverses)

        r.inverse[span] = lax.fori_loop(0, heads, one_head, jnp.zeros((rows, LANES), F32))
        r.part1[span] = dot(r.att[span], r.wop[...]).astype(BF)

    def attend_step(step, carry):
        core, side = lax.rem(p.t, 2), p.t // 2
        side = side + (1 - step // 2) * (1 - 2 * side)
        core = core + (1 - lax.rem(step, 2)) * (1 - 2 * core)
        wanted = 2 * side + core
        for i, block in enumerate(blocks):

            @pl.when(wanted == i)
            def _(block=block):
                attend(*block)

        @pl.when(lax.rem(step, 2) == 0)
        def _():
            for c in range(CHUNKS):
                scatter1.near_copy(1 - step // 2, c).start()

        @pl.when(step == 1)
        def _():
            for c in range(CHUNKS):
                scatter1.middle(c)

        return carry

    lax.fori_loop(0, SPLIT, attend_step, 0)

    waiting = []

    def spread(name):
        if z.inside:
            spreads[name].send()
            waiting.extend((name, step) for step in range(Spread.STEPS))

    def pair_sums(count):
        for name, step in waiting[:count]:
            spreads[name].middle(step)
        del waiting[:count]

    def second_norm(c, carry):
        span = scatter1.span(c)
        after = r.inputs[span] + scatter1.finish(c)
        r.after[span] = after
        scale = lax.rsqrt(jnp.mean(after * after, axis=1, keepdims=True) + 1e-05)
        r.scale2[span] = jnp.broadcast_to(scale, (z.chunk, LANES))
        own = scatter1.rows(p.t, c)
        r.n2[own] = (after * scale * r.gain2[...][None, :]).astype(BF)
        gather2.send(c)
        return carry

    lax.fori_loop(0, CHUNKS, second_norm, 0)

    def feed_forward(c, carry):
        gather2.receive(c)
        both = dot(take(r.n2, c), r.wgu[...])
        act_back = dot_right(take(r.cot, c), r.wd[...])
        gate, up = both[:, :units], both[:, units:]
        s = 1.0 / (1.0 + jnp.exp(-gate))
        silu = gate * s
        put(r.act, c, (silu * up).astype(BF))
        gate_back = (act_back * up * s * (1.0 + gate * (1.0 - s))).astype(BF)
        up_back = (act_back * silu).astype(BF)
        put(r.gub, c, gate_back, slice(0, units))
        put(r.gub, c, up_back, slice(units, 2 * units))
        back = dot_right(gate_back, r.wgu[:, 0:units]) + dot_right(up_back, r.wgu[:, units:])
        put(r.part3, c, back.astype(BF))
        scatter3.send(c)

        @pl.when(c > 0)
        def _():
            scatter3.middle(c - 1)

        return carry

    lax.fori_loop(0, CHUNKS, feed_forward, 0)
    scatter3.middle(CHUNKS - 1)

    tile = 2 * LANES

    def gate_up_tile(j, carry):
        at = pl.ds(pl.multiple_of(j * tile, tile), tile)
        r.gu_part[at] = dot(r.n2[:, at].T, r.gub[0:length]).astype(BF)
        return carry

    lax.fori_loop(0, width // tile, gate_up_tile, 0)
    spread("gu")

    r.sums[...] = jnp.zeros_like(r.sums)

    def norm_back(grad, values, scale, gain):
        scaled = grad * gain
        mean = jnp.mean(scaled * values, axis=1, keepdims=True)
        total = jnp.sum(grad * values * scale, axis=0, keepdims=True)
        return scale * scaled - values * (scale * scale * scale * mean), total

    def second_back(c, carry):
        span = scatter3.span(c)
        grad = scatter3.finish(c)
        row_grad, total = norm_back(grad, r.after[span], r.scale2[span, 0:1], r.gain2[...][None, :])
        r.sums[1, 0:1] += total
        own = scatter3.rows(p.t, c)
        after_grad = r.cot[own].astype(F32) + row_grad
        r.aftergrad[span] = after_grad
        r.ab[own] = after_grad.astype(BF)
        gather3.send(c)
        return carry

    lax.fori_loop(0, CHUNKS, second_back, 0)

    def branch_two(c, carry):
        put(r.part2, c, dot(take(r.act, c), r.wd[...]).astype(BF))
        scatter2.send(c)
        return carry

    lax.fori_loop(0, CHUNKS, branch_two, 0)
    for c in range(CHUNKS):
        scatter2.middle(c)

    def down_tile(j, carry):
        at = pl.ds(pl.multiple_of(j * tile, tile), tile)
        r.dn_part[at] = dot(r.cot[:, at].T, r.act[...]).astype(BF)
        return carry

    lax.fori_loop(0, width // tile, down_tile, 0)
    spread("dn")
    pair_sums(2)

    def attended_back(c, carry):
        gather3.receive(c)
        back = dot_right(take(r.ab, c), r.wop[...])
        inverse = take(r.inverse, c)
        for h in range(heads):
            at = slice(h * LANES, (h + 1) * LANES)
            put(r.do, c, (back[:, at] * inverse[:, h : h + 1]).astype(BF), at)
        return carry

    lax.fori_loop(0, CHUNKS, attended_back, 0)

    def unrotate(grads, span):
        grads = grads.astype(BF).astype(F32)
        turned = grads * r.cosine[span] - swap_halves(grads) * r.sines[span]
        return turned.astype(BF)

    def upright(block):
        return jnp.concatenate([block, jnp.zeros_like(block)], axis=0).T

    def attend_back(h, first, keys, kept, whole):
        span, at = slice(first, first + rows), slice(h * LANES, (h + 1) * LANES)
        do, q = r.do[span, at], r.q[span, at]
        weights = kept[h]
        prob_back = dot_right(do, r.v[0:keys, at])
        centre = jnp.sum(do.astype(F32) * r.att[span, at].astype(F32), axis=1, keepdims=True)
        score_back = (weights.astype(F32) * (prob_back - centre)).astype(BF)
        query_back = dot(score_back, r.k[0:keys, at]) * HD**-0.5
        r.mixb[span, at] = unrotate(query_back, span)
        key_back, value_back = dot(q.T[:HD], score_back), dot(do.T[:HD], weights)
        if whole:
            r.dk[...] = key_back
            r.dv[...] = value_back
        else:
            r.dk[:, 0:keys] += key_back
            r.dv[:, 0:keys] += value_back

    n1_turned, ab_turned = r.gub.at[0:width], r.wgu

    def turned_tile(j, carry):
        at = pl.ds(pl.multiple_of(j * tile, tile), tile)
        n1_turned[at] = r.n1[:, at].T
        ab_turned[at] = r.ab[:, at].T
        return carry

    lax.fori_loop(0, width // tile, turned_tile, 0)

    def head_tiles(h):
        part = getattr(r, f"at{h}_part")
        lanes = [slice(c * padded + h * LANES, c * padded + (h + 1) * LANES) for c in range(3)]

        def head_tile(j, carry):
            at = pl.ds(pl.multiple_of(j * tile, tile), tile)
            mixed = jnp.concatenate([r.mixb[:, span] for span in lanes], axis=1)
            grad = dot(n1_turned[at], mixed)
            outer = dot(ab_turned[at], r.att[:, h * LANES : (h + 1) * LANES])
            first = grad[:, :LANES] + roll64(grad[:, LANES : 2 * LANES])
            second = grad[:, 2 * LANES :] + roll64(outer)
            part[at, 0:LANES] = first.astype(BF)
            part[at, LANES:] = second.astype(BF)
            return carry

        lax.fori_loop(0, width // tile, head_tile, 0)

    pair_sums(1)
    for h in range(heads):
        for i in reversed(range(SPLIT)):
            first, keys, kept = blocks[i]
            attend_back(h, first, keys, kept, i == SPLIT - 1)
        for i in range(SPLIT):
            span = slice(i * rows, (i + 1) * rows)
            at = padded + h * LANES
            key_back = upright(r.dk[:, span]) * math.log(2.0)
            r.mixb[span, at : at + LANES] = unrotate(key_back, span)
            at = 2 * padded + h * LANES
            r.mixb[span, at : at + LANES] = upright(r.dv[:, span]).astype(BF)
        if h < heads - 1:
            head_tiles(h)
            spread(f"at{h}")
            pair_sums(h + 1)
    scatter1.close()

    def first_norm_part(c, carry):
        put(r.part1, c, dot(take(r.mixb, c), r.wap[...]).astype(BF))
        scatter4.send(c)

        @pl.when(c > 0)
        def _():
            scatter4.middle(c - 1)

        return carry

    lax.fori_loop(0, CHUNKS, first_norm_part, 0)
    scatter4.middle(CHUNKS - 1)
    head_tiles(heads - 1)
    spread(f"at{heads - 1}")
    pair_sums(max(0, len(waiting) - Spread.STEPS - 2))

    def block_out(c, carry):
        span = scatter2.span(c)
        r.block_out[span] = (r.after[span] + scatter2.finish(c)).astype(BF)
        return carry

    lax.fori_loop(0, CHUNKS, block_out, 0)

    def first_back(c, carry):
        span = scatter4.span(c)
        grad = scatter4.finish(c)
        row_grad, total = norm_back(grad, r.inputs[span], r.scale1[span, 0:1], r.gain1[...][None, :])
        r.sums[0, 0:1] += total
        embed_grad = r.aftergrad[span] + row_grad
        r.embed_grad[span] = embed_grad
        r.lifted[span] = embed_grad.astype(BF)
        return carry

    lax.fori_loop(0, CHUNKS, first_back, 0)

    row_back = dot_right(r.lifted[...], r.nw[...]).astype(BF)
    low_table = lane_of((slots, z.pair_width)) < z.table_width
    outgoing = jnp.where(low_table, dot(r.pick_t[0], row_back), dot(r.pick_t[1], row_back))
    r.back_out[...] = outgoing.astype(BF)

    def back_slots(block, of):
        return r.back_in.at[pl.ds(pl.multiple_of(block * slots + of * cap, cap), cap)]

    def back_copy(step, incoming=False):
        to = peer(step)
        src = r.back_out.at[pl.ds(pl.multiple_of(to * cap, cap), cap)]
        dst = back_slots(p.t, to if incoming else p.d)
        recv = r.back_sem.at[1, to if incoming else p.d]
        return make_copy(src, dst, r.back_sem.at[0, 0], recv, dp=to)

    def pass_copy(kind, of, incoming=False):
        block = ((p.t, p.t1), (p.t, p.t2), (p.t2, p.t3))[kind][1 if incoming else 0]
        ref = back_slots(block, of)
        target = p.t2 if kind == 1 else p.t1
        return make_copy(
            ref, ref, r.pass_sem.at[2 * kind, of], r.pass_sem.at[2 * kind + 1, of], tensor=target
        )

    for step in range(1, n):
        back_copy(n - step).start()
    own_block = pl.ds(pl.multiple_of(p.t * slots + p.d * cap, cap), cap)
    r.back_in[own_block] = r.back_out[own_slots]

    gains = jnp.concatenate(
        [r.sums[0, 0:1], r.sums[1, 0:1], jnp.zeros((LANES - 2, width), F32)], axis=0
    )
    small = jnp.concatenate([dot(r.lifted[...].T, r.grams[...]), gains.T], axis=1)
    if z.inside:
        for j in range(n * SPLIT):
            value = small[j * z.small : (j + 1) * z.small].astype(BF)
            r.sm_part[j % SPLIT, j // SPLIT] = value

        def small_near(slot):
            block = p.t3 if slot else p.t1
            return make_copy(
                r.sm_part.at[block],
                r.sm_near.at[slot],
                r.sm_sem.at[2 * slot],
                r.sm_sem.at[2 * slot + 1],
                tensor=p.t1,
            )

        small_far = make_copy(r.sm_send, r.sm_far, r.sm_sem.at[4], r.sm_sem.at[5], tensor=p.t2)

        def small_copy(step, incoming=False):
            to = peer(step)
            at = to if incoming else p.d
            return make_copy(
                r.sm_out.at[to], r.sm_in.at[at], r.sp_sem.at[0, 0], r.sp_sem.at[1, at], dp=to
            )

        small_near(1).start()
        small_near(0).start()
        small_near(1).wait_recv()
        r.sm_send[...] = (r.sm_part[p.t2].astype(F32) + r.sm_near[1].astype(F32)).astype(BF)
        small_far.start()
    else:
        r.sm_total[...] = small

    pass_copy(0, p.d).start()
    pass_copy(1, p.d).start()
    for step in range(1, n):
        back_copy(step, True).wait_recv()
        pass_copy(1, peer(step)).start()
        pass_copy(0, peer(step)).start()
    if z.inside:
        small_near(0).wait_recv()
        small_far.wait_recv()
        total = r.sm_part[p.t].astype(F32) + r.sm_near[0].astype(F32) + r.sm_far[...].astype(F32)
        r.sm_out[...] = total.astype(BF)
        for step in range(1, n):
            small_copy(step).start()
        r.sm_in[p.d] = r.sm_out[p.d]
        pair_sums(len(waiting))
    for step in range(n):
        of = peer(step)
        pass_copy(1, of, True).wait_recv()
        pass_copy(2, of).start()
    for i in range(3):
        lid_copy(i, True).wait_recv()
    kept = z.table_rows // SPLIT
    low_table = lane_of((kept, LANES)) < HD
    wanted = row_of((kept, slots)) + p.t * kept

    def add_rows(b, fresh=False):
        block = pl.ds(pl.multiple_of(b * slots, slots), slots)
        hits = [onehot(r.lids[b, k][0:1] == wanted) for k in range(2)]
        left = dot(hits[0], r.back_in[block, 0 : 2 * LANES])
        right = dot(hits[1], r.back_in[block, LANES : 3 * LANES])
        sums = (left[:, :LANES], jnp.where(low_table, left[:, LANES:], right[:, :LANES]), right[:, LANES:])
        for g, value in enumerate(sums):
            at = slice(g * LANES, (g + 1) * LANES)
            r.table_grads[:, at] = value if fresh else r.table_grads[:, at] + value

    add_rows(p.t, True)
    for step in range(n):
        pass_copy(0, peer(step), True).wait_recv()
    add_rows(p.t1)
    add_rows(p.t2)
    for step in range(n):
        pass_copy(2, peer(step), True).wait_recv()
    add_rows(p.t3)

    if z.inside:
        for step in range(1, n):
            small_copy(step, True).wait_recv()
        r.sm_total[...] = jnp.sum(r.sm_in[...].astype(F32), axis=0)
        for spread in spreads.values():
            spread.finish()

    all_ids.wait_send()
    shared = [(r.rows_out, r.row_sem, cap), (r.back_out, r.back_sem, cap)]
    if z.inside:
        shared.append((r.sm_out, r.sp_sem, 1))
    for ref, sems, each in shared:
        ref = ref.at[pl.ds(0, (n - 1) * each)]
        make_copy(ref, ref, sems.at[0, 0], sems.at[1, 0], dp=peer(1)).wait_send()
    for i in range(3):
        lid_copy(i).wait_send()
    for gather in (gather1, gather2, gather3):
        gather.close()
    for scatter in scatters[1:]:
        scatter.close()
    for spread in spreads.values():
        spread.close()
    if z.inside:
        small_near(0).wait_send()
        small_near(1).wait_send()
        small_far.wait_send()
    for step in range(n):
        for kind in range(3):
            pass_copy(kind, peer(step)).wait_send()


def finish_kernel(z, names, *refs):
    r = Refs(names, refs)
    r.block[...] = r.block_out[...]
    r.embed[...] = r.embed_grad[...]
    r.bigram[...] = r.table_grads[:, : 2 * LANES].T[: z.table_width]
    r.trigram[...] = r.table_grads[:, LANES:].T[2 * LANES - z.table_width :]
    r.ngram[...] = r.sm_total[:, : z.pair_width]
    gains = r.sm_total[:, z.pair_width :]
    r.first[...] = gains[:, 0:1].T
    r.second[...] = gains[:, 1:2].T
    r.gate[...] = r.gu_out[:, : z.units]
    r.up[...] = r.gu_out[:, z.units :]
    r.down[...] = r.dn_out[...]
    side = 3 * HD
    for h in range(z.heads):
        sums = getattr(r, f"at{h}_out")[...]
        r.attend[:, h * side : (h + 1) * side] = sums[:, :side]
        r.output[h * HD : (h + 1) * HD] = sums[:, LANES:].T[HD:]


def finish_outputs(z, got):
    kept = z.table_rows // SPLIT
    outs = dict(
        block=((z.rows, z.width), BF),
        embed=((z.rows, z.width), F32),
        bigram=((z.table_width, kept), F32),
        trigram=((z.table_width, kept), F32),
        ngram=((z.small, z.pair_width), F32),
        first=((1, z.small), F32),
        attend=((z.piece, 3 * HD * z.heads), F32),
        output=((HD * z.heads, z.piece), F32),
        second=((1, z.small), F32),
        gate=((z.piece, z.units), F32),
        up=((z.piece, z.units), F32),
        down=((z.piece, z.units), F32),
    )
    done = pl.pallas_call(
        functools.partial(finish_kernel, z, (*got, *outs)),
        out_shape=[jax.ShapeDtypeStruct(*item) for item in outs.values()],
        in_specs=[pl.BlockSpec(memory_space=pltpu.VMEM)] * len(got),
        out_specs=[pl.BlockSpec(memory_space=pltpu.VMEM)] * len(outs),
        name="finish",
    )(*got.values())
    done = dict(zip(outs, done, strict=True))
    for name in ("bigram", "trigram", "ngram", "down"):
        done[name] = done[name].T
    for name in ("first", "second"):
        done[name] = done[name].reshape(z.small)
    return tuple(done.values())


def shards(
    embedded,
    bigram_ids,
    trigram_ids,
    prefix_lens,
    bigram_table,
    trigram_table,
    ngram_weight,
    first_gain,
    attend_weight,
    output_weight,
    second_gain,
    gate_weight,
    up_weight,
    down_weight,
    cotangent,
):
    n = lax.axis_size("dp")
    rows, width = embedded.shape
    table_rows, table_width = bigram_table.shape
    heads, units = attend_weight.shape[1] // (3 * HD), gate_weight.shape[1]
    z = Sizes(n, rows, width, heads, units, table_rows, table_width)
    scratch, outs = scratch_of(z), outputs_of(z)
    names = (*INPUTS, *outs, *scratch)
    anywhere = pl.BlockSpec(memory_space=pl.ANY)
    in_specs = [anywhere] * len(INPUTS)
    in_specs[3] = pl.BlockSpec(memory_space=pltpu.SMEM)
    got = pl.pallas_call(
        functools.partial(block_kernel, z, names),
        out_shape=[jax.ShapeDtypeStruct(*item) for item in outs.values()],
        in_specs=in_specs,
        out_specs=[pl.BlockSpec(memory_space=pltpu.VMEM)] * len(outs),
        scratch_shapes=list(scratch.values()),
        compiler_params=pltpu.CompilerParams(
            collective_id=0, has_side_effects=True, vmem_limit_bytes=67043328
        ),
        name="block",
    )(
        embedded,
        bigram_ids.reshape(1, rows),
        trigram_ids.reshape(1, rows),
        prefix_lens,
        bigram_table.T,
        trigram_table.T,
        ngram_weight,
        first_gain,
        attend_weight.T,
        output_weight,
        second_gain,
        gate_weight,
        up_weight,
        down_weight,
        cotangent,
    )
    got = dict(zip(outs, got, strict=True))
    if not z.inside:

        def summed(part, axes):
            return lax.psum_scatter(part, axes, scatter_dimension=0, tiled=True)

        for name in ("gu", "dn", *(f"at{h}" for h in range(heads))):
            got[f"{name}_out"] = summed(got.pop(f"{name}_part").astype(F32), "dp")
        got["sm_total"] = summed(got["sm_total"], ("dp", "tensor"))
    return finish_outputs(z, got)


def solution(mesh):
    placed = (
        P(("dp", "tensor"), None),
        P(("dp", "tensor")),
        P(("dp", "tensor")),
        P("dp"),
        P("dp", None),
        P("dp", None),
        P(),
        P(),
        P(None, "tensor"),
        P("tensor", None),
        P(),
        P(None, "tensor"),
        P(None, "tensor"),
        P("tensor", None),
        P("dp", None),
    )
    return jax.shard_map(
        shards,
        mesh=mesh,
        in_specs=placed,
        out_specs=(
            P(("dp", "tensor"), None),
            P(("dp", "tensor"), None),
            P(("dp", "tensor"), None),
            P(("dp", "tensor"), None),
            P(None, ("dp", "tensor")),
            P(("dp", "tensor")),
            P("dp", "tensor"),
            P("tensor", "dp"),
            P(("dp", "tensor")),
            P("dp", "tensor"),
            P("dp", "tensor"),
            P("tensor", "dp"),
        ),
        check_vma=False,
    )
```

```python
import functools
import math

import jax
import jax.numpy as jnp
from jax import lax
from jax.experimental import pallas as pl
from jax.experimental.pallas import tpu as pltpu
from jax.sharding import PartitionSpec as P

BF = jnp.bfloat16
F32 = jnp.float32
HD = 64
LANES = 128
PREFIX_MOST = 512
SPLIT = 4
CHUNKS = 4

INPUTS = (
    "embedded", "bigram_ids", "trigram_ids", "prefix", "bigram_table", "trigram_table",
    "ngram_weight", "first_gain", "attend_weight", "output_weight", "second_gain",
    "gate_weight", "up_weight", "down_weight", "cotangent",
)


class Refs:
    def __init__(self, names, refs):
        self.__dict__.update(zip(names, refs, strict=True))


def dot(left, right):
    return jnp.dot(left, right, preferred_element_type=F32)


def dot_right(left, right):
    return lax.dot_general(left, right, (((1,), (1,)), ((), ())), preferred_element_type=F32)


def lane_of(shape):
    return lax.broadcasted_iota(jnp.int32, shape, len(shape) - 1)


def row_of(shape):
    return lax.broadcasted_iota(jnp.int32, shape, 0)


def onehot(test):
    return jnp.where(test, 1.0, 0.0).astype(BF)


def roll64(block):
    return pltpu.roll(block, 64, 1)


def swap_halves(block):
    return jnp.where(lane_of(block.shape) < 32, pltpu.roll(block, 96, 1), pltpu.roll(block, 32, 1))


class Sizes:
    def __init__(self, n, rows, width, heads, units, table_rows, table_width):
        self.n, self.rows, self.width, self.heads, self.units = n, rows, width, heads, units
        self.table_rows, self.table_width = table_rows, table_width
        self.length = rows * SPLIT
        self.keys = [max((i + 1) * rows, min(PREFIX_MOST, rows * SPLIT)) for i in range(SPLIT)]
        self.cap = max(16, 2 * rows // n)
        self.slots = n * self.cap
        self.padded = heads * LANES
        self.chunk = rows // CHUNKS
        self.piece = width // n
        self.pair_width = 2 * table_width
        self.small = width // (n * SPLIT)
        self.small_lanes = self.pair_width + LANES
        self.attn_lanes = 4 * HD
        self.inside = n == 8 and self.piece % 16 == 0 and self.small % 8 == 0


def make_copy(src, dst, send, recv, **where):
    return pltpu.make_async_remote_copy(
        src_ref=src, dst_ref=dst, send_sem=send, recv_sem=recv, device_id=where
    )


class Gather:
    def __init__(self, z, pos, full, sems):
        self.z, self.pos, self.full, self.sems = z, pos, full, sems

    def piece(self, block, c):
        start = pl.multiple_of(block * self.z.rows + c * self.z.chunk, self.z.chunk)
        return self.full.at[pl.ds(start, self.z.chunk)]

    def copy(self, kind, c, incoming=False):
        p = self.pos
        block = ((p.t, p.t1), (p.t, p.t2), (p.t2, p.t3))[kind][1 if incoming else 0]
        ref = self.piece(block, c)
        target = p.t2 if kind == 1 else p.t1
        return make_copy(
            ref, ref, self.sems.at[c, 2 * kind], self.sems.at[c, 2 * kind + 1], tensor=target
        )

    def send(self, c):
        self.copy(1, c).start()
        self.copy(0, c).start()

    def receive(self, c):
        self.copy(1, c, True).wait_recv()
        self.copy(2, c).start()
        self.copy(0, c, True).wait_recv()
        self.copy(2, c, True).wait_recv()

    def close(self):
        def body(c, carry):
            for kind in range(3):
                self.copy(kind, c).wait_send()
            return carry

        lax.fori_loop(0, CHUNKS, body, 0)


class Scatter:
    def __init__(self, z, pos, part, near, out, far, sems):
        self.z, self.pos, self.part, self.near = z, pos, part, near
        self.out, self.far, self.sems = out, far, sems

    def span(self, c):
        return pl.ds(pl.multiple_of(c * self.z.chunk, self.z.chunk), self.z.chunk)

    def rows(self, block, c):
        start = pl.multiple_of(block * self.z.rows + c * self.z.chunk, self.z.chunk)
        return pl.ds(start, self.z.chunk)

    def near_copy(self, slot, c):
        block = self.pos.t1 + slot * (self.pos.t3 - self.pos.t1)
        return make_copy(
            self.part.at[self.rows(block, c)],
            self.near.at[slot, self.span(c)],
            self.sems.at[c, 2 * slot],
            self.sems.at[c, 2 * slot + 1],
            tensor=self.pos.t1,
        )

    def far_copy(self, c):
        return make_copy(
            self.out.at[self.span(c)],
            self.far.at[self.span(c)],
            self.sems.at[c, 4],
            self.sems.at[c, 5],
            tensor=self.pos.t2,
        )

    def send(self, c):
        self.near_copy(1, c).start()
        self.near_copy(0, c).start()

    def middle(self, c):
        self.near_copy(1, c).wait_recv()
        own = self.part[self.rows(self.pos.t2, c)].astype(F32)
        self.out[self.span(c)] = (own + self.near[1, self.span(c)].astype(F32)).astype(BF)
        self.far_copy(c).start()

    def finish(self, c):
        self.near_copy(0, c).wait_recv()
        self.far_copy(c).wait_recv()
        own = self.part[self.rows(self.pos.t, c)].astype(F32)
        own = own + self.near[0, self.span(c)].astype(F32)
        return own + self.far[self.span(c)].astype(F32)

    def close(self):
        def body(c, carry):
            self.near_copy(0, c).wait_send()
            self.near_copy(1, c).wait_send()
            self.far_copy(c).wait_send()
            return carry

        lax.fori_loop(0, CHUNKS, body, 0)


class Spread:
    STEPS = 4

    def __init__(self, z, pos, part, pair_in, next_out, next_in, out, sems):
        self.z, self.pos, self.part, self.pair_in = z, pos, part, pair_in
        self.next_out, self.next_in, self.out, self.sems = next_out, next_in, out, sems
        near = pos.place + 1 - 2 * lax.rem(pos.place, 2)
        far = lax.rem(pos.place + 2, 4)
        both = lax.rem(near + 2, 4)
        self.order = (both, near, far, pos.place)

    def rows(self, peer):
        return pl.ds(pl.multiple_of(peer * self.z.piece, self.z.piece), self.z.piece)

    def pair_copy(self, step):
        return make_copy(
            self.part.at[self.rows(self.order[step] * 2 + 1 - self.pos.parity)],
            self.pair_in.at[step],
            self.sems.at[0, step],
            self.sems.at[1, step],
            dp=self.pos.partner,
        )

    def next_copy(self, step):
        place = self.order[1] if step < 2 else self.order[2]
        return make_copy(
            self.next_out.at[step],
            self.next_in.at[step],
            self.sems.at[2, step],
            self.sems.at[3, step],
            dp=place * 2 + self.pos.parity,
        )

    def send(self):
        for step in range(4):
            self.pair_copy(step).start()

    def middle(self, step):
        self.pair_copy(step).wait_recv()
        own = self.part[self.rows(self.order[step] * 2 + self.pos.parity)].astype(F32)
        total = own + self.pair_in[step].astype(F32)
        if step >= 2:
            self.next_copy(step - 2).wait_recv()
            total = total + self.next_in[step - 2].astype(F32)
        if step == 3:
            self.out[...] = total
        else:
            self.next_out[step] = total.astype(BF)
            self.next_copy(step).start()

    def finish(self):
        self.next_copy(2).wait_recv()
        self.out[...] += self.next_in[2].astype(F32)

    def close(self):
        for step in range(4):
            self.pair_copy(step).wait_send()
            if step < 3:
                self.next_copy(step).wait_send()


class Position:
    def __init__(self, z):
        self.d, self.t = lax.axis_index("dp"), lax.axis_index("tensor")
        core, side = lax.rem(self.t, 2), self.t // 2
        self.t1 = self.t + 1 - 2 * core
        self.t2 = self.t + 2 - 4 * side
        self.t3 = self.t1 + 2 - 4 * side
        self.parity, self.place = lax.rem(self.d, 2), self.d // 2
        self.partner = self.d + 1 - 2 * self.parity


def scratch_of(z):
    n, rows, width, length, chunks = z.n, z.rows, z.width, z.length, CHUNKS
    vmem, dma = pltpu.VMEM, pltpu.SemaphoreType.DMA
    shapes = dict(
        emb=vmem((rows, width), BF),
        ids=vmem((2 * n, 1, rows), jnp.int32),
        own_ids=vmem((2, 1, rows), jnp.int32),
        pick=vmem((2, rows, z.slots), BF),
        table_b=vmem((z.table_width, z.table_rows), BF),
        table_t=vmem((z.table_width, z.table_rows), BF),
        nw=vmem((z.pair_width, width), BF),
        gain1=vmem((width,), F32),
        gain2=vmem((width,), F32),
        wap=vmem((3 * z.padded, width), BF),
        wop=vmem((z.padded, width), BF),
        wgu=vmem((width, 2 * z.units), BF),
        wd=vmem((z.units, width), BF),
        cot=vmem((length, width), BF),
        cosine=vmem((length, LANES), F32),
        sines=vmem((length, LANES), F32),
        pick_t=vmem((2, z.slots, rows), BF),
        lids=vmem((SPLIT, 2, 8, z.slots), jnp.int32),
        rows_out=vmem((z.slots, z.pair_width), BF),
        rows_in=vmem((z.slots, z.pair_width), BF),
        grams=vmem((rows, z.pair_width), BF),
        inputs=vmem((rows, width), F32),
        after=vmem((rows, width), F32),
        aftergrad=vmem((rows, width), F32),
        inverse=vmem((length, LANES), F32),
        scale1=vmem((rows, LANES), F32),
        scale2=vmem((rows, LANES), F32),
        n1=vmem((length, width), BF),
        n2=vmem((length, width), BF),
        ab=vmem((length, width), BF),
        q=vmem((length, z.padded), BF),
        k=vmem((length, z.padded), BF),
        v=vmem((length, z.padded), BF),
        probs0=vmem((z.heads, rows, z.keys[0]), BF),
        probs1=vmem((z.heads, rows, z.keys[1]), BF),
        probs2=vmem((z.heads, rows, z.keys[2]), BF),
        probs3=vmem((z.heads, rows, z.keys[3]), BF),
        att=vmem((length, z.padded), BF),
        do=vmem((length, z.padded), BF),
        dk=vmem((HD, length), F32),
        dv=vmem((HD, length), F32),
        mixb=vmem((length, 3 * z.padded), BF),
        act=vmem((length, z.units), BF),
        gub=vmem((max(length, width), 2 * z.units), BF),
        lifted=vmem((rows, width), BF),
        sums=vmem((2, 8, width), F32),
        back_out=vmem((z.slots, z.pair_width), BF),
        back_in=vmem((SPLIT * z.slots, z.pair_width), BF),
        in_sem=dma((12 + 4 * z.heads,)),
        id_sem=dma((2,)),
        row_sem=dma((2, n)),
        lid_sem=dma((2, 3)),
        back_sem=dma((2, 2 * n)),
        pass_sem=dma((6, 2 * n)),
        ag1_sem=dma((chunks, 6)),
        ag2_sem=dma((chunks, 6)),
        ag3_sem=dma((chunks, 6)),
    )
    for k in range(1, 4):
        shapes[f"part{k}"] = vmem((length, width), BF)
        shapes[f"near{k}"] = vmem((2, rows, width), BF)
        shapes[f"send{k}"] = vmem((rows, width), BF)
        shapes[f"far{k}"] = vmem((rows, width), BF)
        shapes[f"rs{k}_sem"] = dma((chunks, 6))
    shapes["rs4_sem"] = dma((chunks, 6))
    if z.inside:
        heads = [(f"at{h}", z.attn_lanes) for h in range(z.heads)]
        for name, lanes in (("gu", 2 * z.units), ("dn", z.units), *heads):
            shapes[f"{name}_part"] = vmem((width, lanes), BF)
            shapes[f"{name}_pair_in"] = vmem((4, z.piece, lanes), BF)
            shapes[f"{name}_next_out"] = vmem((3, z.piece, lanes), BF)
            shapes[f"{name}_next_in"] = vmem((3, z.piece, lanes), BF)
            shapes[f"{name}_sem"] = dma((4, 4))
        small = (n, z.small, z.small_lanes)
        shapes["sm_part"] = vmem((SPLIT, *small), BF)
        shapes["sm_near"] = vmem((2, *small), BF)
        shapes["sm_send"] = vmem(small, BF)
        shapes["sm_far"] = vmem(small, BF)
        shapes["sm_out"] = vmem(small, BF)
        shapes["sm_in"] = vmem(small, BF)
        shapes["sm_sem"] = dma((6,))
        shapes["sp_sem"] = dma((2, n))
    return shapes


def outputs_of(z):
    n, rows, width = z.n, z.rows, z.width
    shapes = dict(
        block_out=((rows, width), BF),
        embed_grad=((rows, width), F32),
        table_grads=((z.table_rows // SPLIT, z.pair_width), F32),
    )
    if z.inside:
        shapes["gu_out"] = ((z.piece, 2 * z.units), F32)
        shapes["dn_out"] = ((z.piece, z.units), F32)
        for h in range(z.heads):
            shapes[f"at{h}_out"] = ((z.piece, z.attn_lanes), F32)
        shapes["sm_total"] = ((z.small, z.small_lanes), F32)
    else:
        shapes["gu_part"] = ((width, 2 * z.units), BF)
        shapes["dn_part"] = ((width, z.units), BF)
        for h in range(z.heads):
            shapes[f"at{h}_part"] = ((width, z.attn_lanes), BF)
        shapes["sm_total"] = ((width, z.small_lanes), F32)
    return shapes


def block_kernel(z, names, *refs):
    r = Refs(names, refs)
    p = Position(z)
    n, rows, width, length = z.n, z.rows, z.width, z.length
    cap, slots, units, padded, heads = z.cap, z.slots, z.units, z.padded, z.heads
    gather1 = Gather(z, p, r.n1, r.ag1_sem)
    gather2 = Gather(z, p, r.n2, r.ag2_sem)
    gather3 = Gather(z, p, r.ab, r.ag3_sem)
    scatters = [
        Scatter(
            z, p, getattr(r, f"part{k}"), getattr(r, f"near{k}"), getattr(r, f"send{k}"),
            getattr(r, f"far{k}"), sems,
        )
        for k, sems in ((1, r.rs1_sem), (2, r.rs2_sem), (3, r.rs3_sem), (1, r.rs4_sem))
    ]
    scatter1, scatter2, scatter3, scatter4 = scatters
    spreads = {}
    if z.inside:
        for name in ("gu", "dn", *(f"at{h}" for h in range(heads))):
            spreads[name] = Spread(
                z, p, getattr(r, f"{name}_part"), getattr(r, f"{name}_pair_in"),
                getattr(r, f"{name}_next_out"), getattr(r, f"{name}_next_in"),
                getattr(r, f"{name}_out"), getattr(r, f"{name}_sem"),
            )

    def peer(step):
        return lax.rem(p.d + step, n)

    barrier = pltpu.get_barrier_semaphore()
    for step in range(1, n):
        pl.semaphore_signal(barrier, inc=1, device_id={"dp": peer(step)})
    for target in (p.t1, p.t2, p.t3):
        pl.semaphore_signal(barrier, inc=1, device_id={"tensor": target})

    loads = [
        (r.bigram_ids, r.own_ids.at[0]),
        (r.trigram_ids, r.own_ids.at[1]),
        (r.bigram_table, r.table_b),
        (r.trigram_table, r.table_t),
        (r.embedded, r.emb),
        (r.ngram_weight, r.nw),
        (r.first_gain, r.gain1),
        (r.second_gain, r.gain2),
        (r.gate_weight, r.wgu.at[:, pl.ds(0, units)]),
        (r.up_weight, r.wgu.at[:, pl.ds(units, units)]),
        (r.down_weight, r.wd),
        (r.cotangent, r.cot),
    ]
    for h in range(heads):
        for c in range(3):
            src = r.attend_weight.at[pl.ds((3 * h + c) * HD, HD)]
            loads.append((src, r.wap.at[pl.ds(c * padded + h * LANES, HD)]))
        src = r.output_weight.at[pl.ds(h * HD, HD)]
        loads.append((src, r.wop.at[pl.ds(h * LANES, HD)]))
    loads = [pltpu.make_async_copy(src, dst, r.in_sem.at[i]) for i, (src, dst) in enumerate(loads)]
    for load in loads[:4]:
        load.start()

    pl.semaphore_wait(barrier, n - 1 + 3)

    def id_copy(step, k):
        return make_copy(
            (r.bigram_ids, r.trigram_ids)[k],
            r.ids.at[k * n + p.d],
            r.id_sem.at[0],
            r.id_sem.at[1],
            dp=peer(step),
        )

    for step in range(1, n):
        for k in range(2):
            id_copy(step, k).start()
    for load in loads[4:]:
        load.start()

    lane = lane_of((32, LANES))
    low = jnp.where(lane < 32, lane, lane - 32)
    frequency = jnp.exp(low.astype(F32) * (-2.0 * math.log(10000.0) / HD))
    place = row_of((32, LANES)).astype(F32)
    coarse, fine = place * 32.0 * frequency, place * frequency
    cos_coarse, sin_coarse = jnp.cos(coarse), jnp.sin(coarse)
    used = lane < HD
    cos_fine = jnp.where(used, jnp.cos(fine), 0.0)
    sin_fine = jnp.where(used, jnp.sin(fine), 0.0)
    sign = jnp.where(lane < 32, -1.0, 1.0)
    for a in range(length // 32):
        ca, sa = cos_coarse[a : a + 1], sin_coarse[a : a + 1]
        r.cosine[a * 32 : (a + 1) * 32] = ca * cos_fine - sa * sin_fine
        r.sines[a * 32 : (a + 1) * 32] = sign * (sa * cos_fine + ca * sin_fine)

    loads[0].wait()
    loads[1].wait()
    earlier = onehot(row_of((rows, rows)) < lane_of((rows, rows)))
    later = onehot(row_of((rows, rows)) > lane_of((rows, rows)))
    lane = lane_of((rows, LANES))
    start, half_cap = (lane * z.table_rows).astype(F32), cap // 2
    for k in range(2):
        r.ids[k * n + p.d] = r.own_ids[k]
        column = jnp.broadcast_to(r.own_ids[k].astype(F32), (LANES, rows)).T
        held = (column >= start) & (column < start + z.table_rows)
        ranks = dot(later, onehot(held))
        slot = jnp.where(held, ranks + (lane * cap).astype(F32), 0.0)
        slot = jnp.sum(slot, axis=1, keepdims=True)
        r.pick[k] = onehot(slot.astype(jnp.int32) == lane_of((rows, slots)))
        second = jnp.where(ranks >= half_cap, float((n - 1) * half_cap), 0.0)
        slot = jnp.where(held, ranks + (lane * half_cap).astype(F32) + second, 0.0)
        slot = jnp.sum(slot, axis=1, keepdims=True)
        across = jnp.broadcast_to(slot, (rows, LANES)).T[0:1]
        r.pick_t[k] = onehot(across.astype(jnp.int32) == row_of((slots, rows)))

    for h in range(heads):
        empty = jnp.zeros((LANES - HD, width), BF)
        for c in range(3):
            at = c * padded + h * LANES + HD
            r.wap[at : at + LANES - HD] = empty
        r.wop[h * LANES + HD : (h + 1) * LANES] = empty

    loads[2].wait()
    loads[3].wait()
    all_ids = r.ids.at[pl.ds(0, 2 * (n - 1))]
    all_ids = make_copy(all_ids, all_ids, r.id_sem.at[0], r.id_sem.at[1], dp=peer(1))
    all_ids.wait_recv()
    asked = jnp.concatenate([r.ids[i] for i in range(2 * n)], axis=0)
    first_row = p.d * z.table_rows
    mine = (asked >= first_row) & (asked < first_row + z.table_rows)
    ranks = dot(onehot(mine), earlier)
    tags = jnp.where(mine, ranks, -1.0).astype(jnp.int32)
    local = jnp.where(mine, asked - first_row + 1, 0).astype(F32)
    picked = []
    for k in range(2):
        columns = []
        for i in range(n):
            at = k * n + i
            hit = tags[at : at + 1] == row_of((cap, rows))
            value = jnp.where(hit, local[at : at + 1], 0.0)
            columns.append(jnp.sum(value, axis=1, keepdims=True) - 1.0)
        picked.append(jnp.concatenate(columns, axis=0).astype(jnp.int32))
        columns = [item[:half_cap] for item in columns] + [item[half_cap:] for item in columns]
        column = jnp.concatenate(columns, axis=0)
        across = jnp.broadcast_to(column, (slots, LANES)).T[0:8]
        r.lids[p.t, k] = across.astype(jnp.int32)
    half = slots // 2

    def row_copy(step):
        to = peer(step)
        return make_copy(
            r.rows_out.at[pl.ds(pl.multiple_of(to * cap, cap), cap)],
            r.rows_in.at[pl.ds(pl.multiple_of(p.d * cap, cap), cap)],
            r.row_sem.at[0, 0],
            r.row_sem.at[1, p.d],
            dp=to,
        )

    def row_arrival(step):
        of = peer(step)
        ref = r.rows_in.at[pl.ds(pl.multiple_of(of * cap, cap), cap)]
        return make_copy(ref, ref, r.row_sem.at[0, 0], r.row_sem.at[1, of], dp=of)

    for part in range(2):
        found = []
        for k, table in enumerate((r.table_b, r.table_t)):
            chosen = picked[k][part * half : (part + 1) * half]
            hits = onehot(chosen == lane_of((half, z.table_rows)))
            both = dot_right(hits, table[...])
            fill = jnp.zeros((half, 2 * LANES - z.table_width), F32)
            found.append((both[:, :LANES], jnp.concatenate([both[:, LANES:], fill], axis=1)))
        low_half = lane_of((half, LANES)) < HD
        rolled = [roll64(block) for block in found[1]]
        span = slice(part * half, (part + 1) * half)
        r.rows_out[span, 0:LANES] = found[0][0].astype(BF)
        middle = jnp.where(low_half, found[0][1], rolled[0])
        r.rows_out[span, LANES : 2 * LANES] = middle.astype(BF)
        r.rows_out[span, 2 * LANES :] = jnp.where(low_half, rolled[0], rolled[1]).astype(BF)
    for step in range(1, n):
        row_copy(n - step).start()
    own_slots = pl.ds(pl.multiple_of(p.d * cap, cap), cap)
    r.rows_in[own_slots] = r.rows_out[own_slots]

    for load in loads[4:8]:
        load.wait()
    for step in range(1, n):
        row_arrival(step).wait_recv()
    fetched = r.rows_in[...]
    low_table = lane_of((rows, z.pair_width)) < z.table_width
    grams = jnp.where(low_table, dot(r.pick[0], fetched), dot(r.pick[1], fetched)).astype(BF)
    r.grams[...] = grams
    inputs = r.emb[...].astype(F32) + dot(grams, r.nw[...])
    r.inputs[...] = inputs
    scale = lax.rsqrt(jnp.mean(inputs * inputs, axis=1, keepdims=True) + 1e-05)
    r.scale1[...] = jnp.broadcast_to(scale, (rows, LANES))
    own_rows = pl.ds(pl.multiple_of(p.t * rows, rows), rows)
    r.n1[own_rows] = (inputs * scale * r.gain1[...][None, :]).astype(BF)
    for c in range(CHUNKS):
        gather1.send(c)

    def lid_copy(i, incoming=False):
        target = (p.t1, p.t2, p.t3)[i]
        ref = r.lids.at[target if incoming else p.t]
        return make_copy(ref, ref, r.lid_sem.at[0, i], r.lid_sem.at[1, i], tensor=target)

    for i in range(3):
        lid_copy(i).start()

    def spans(c):
        return [
            pl.ds(pl.multiple_of(b * rows + c * z.chunk, z.chunk), z.chunk) for b in range(SPLIT)
        ]

    def take(ref, c, *rest):
        return jnp.concatenate([ref[(span, *rest)] for span in spans(c)], axis=0)

    def put(ref, c, value, *rest):
        for b, span in enumerate(spans(c)):
            ref[(span, *rest)] = value[b * z.chunk : (b + 1) * z.chunk]

    for load in loads[8:]:
        load.wait()

    def project(c, carry):
        gather1.receive(c)
        mixture = dot_right(take(r.n1, c), r.wap[...])
        cosine, sines = take(r.cosine, c), take(r.sines, c)
        for h in range(heads):
            for i, ref in enumerate((r.q, r.k)):
                at = i * padded + h * LANES
                block = mixture[:, at : at + LANES]
                turned = block * cosine + swap_halves(block) * sines
                if i == 0:
                    turned = turned * (HD**-0.5 * math.log2(math.e))
                put(ref, c, turned.astype(BF), slice(h * LANES, (h + 1) * LANES))
            at = 2 * padded + h * LANES
            block = mixture[:, at : at + LANES]
            block = jnp.where(lane_of(block.shape) == HD, 1.0, block)
            put(r.v, c, block.astype(BF), slice(h * LANES, (h + 1) * LANES))
        return carry

    lax.fori_loop(0, CHUNKS, project, 0)

    prefix = r.prefix[0]
    probs = (r.probs0, r.probs1, r.probs2, r.probs3)
    blocks = [(i * rows, z.keys[i], probs[i]) for i in range(SPLIT)]

    def attend(first, keys, kept):
        span = slice(first, first + rows)
        lane = lane_of((rows, LANES))
        row, column = row_of((rows, rows)), lane_of((rows, rows))

        def score_tiles(h):
            at = slice(h * LANES, (h + 1) * LANES)
            tiles = []
            for start in range(0, keys, rows):
                scores = dot_right(r.q[span, at], r.k[start : start + rows, at])
                allowed = None
                if start == first:
                    allowed = column <= row
                if start + rows > first + 1 and start < PREFIX_MOST:
                    in_prefix = column < prefix - start
                    allowed = in_prefix if allowed is None else allowed | in_prefix
                if allowed is not None:
                    scores = jnp.where(allowed, scores, -1000000000.0)
                tiles.append(scores)
            return tiles

        inverses = jnp.zeros((rows, LANES), F32)
        every = [score_tiles(h) for h in range(heads)]
        tops = [jnp.max(functools.reduce(jnp.maximum, tiles), axis=1, keepdims=True) for tiles in every]
        totals = []
        for h in range(heads):
            at = slice(h * LANES, (h + 1) * LANES)
            total = jnp.zeros((rows, LANES), F32)
            for j, scores in enumerate(every[h]):
                weights = jnp.exp2(scores - tops[h]).astype(BF)
                kept[h, :, j * rows : (j + 1) * rows] = weights
                total = total + dot(weights, r.v[j * rows : (j + 1) * rows, at])
            totals.append(total)
        for h, total in enumerate(totals):
            at = slice(h * LANES, (h + 1) * LANES)
            inverse = 1.0 / total[:, HD : HD + 1]
            r.att[span, at] = jnp.where(lane < HD, total * inverse, 0.0).astype(BF)
            inverses = jnp.where(lane == h, inverse, inverses)
        r.inverse[span] = inverses
        r.part1[span] = dot(r.att[span], r.wop[...]).astype(BF)

    def attend_step(step, carry):
        core, side = lax.rem(p.t, 2), p.t // 2
        side = side + (1 - step // 2) * (1 - 2 * side)
        core = core + (1 - lax.rem(step, 2)) * (1 - 2 * core)
        wanted = 2 * side + core
        for i, block in enumerate(blocks):

            @pl.when(wanted == i)
            def _(block=block):
                attend(*block)

        @pl.when(lax.rem(step, 2) == 0)
        def _():
            for c in range(CHUNKS):
                scatter1.near_copy(1 - step // 2, c).start()

        @pl.when(step == 1)
        def _():
            for c in range(CHUNKS):
                scatter1.middle(c)

        return carry

    lax.fori_loop(0, SPLIT, attend_step, 0)

    waiting = []

    def spread(name):
        if z.inside:
            spreads[name].send()
            waiting.extend((name, step) for step in range(Spread.STEPS))

    def pair_sums(count):
        for name, step in waiting[:count]:
            spreads[name].middle(step)
        del waiting[:count]

    def second_norm(c, carry):
        span = scatter1.span(c)
        after = r.inputs[span] + scatter1.finish(c)
        r.after[span] = after
        scale = lax.rsqrt(jnp.mean(after * after, axis=1, keepdims=True) + 1e-05)
        r.scale2[span] = jnp.broadcast_to(scale, (z.chunk, LANES))
        own = scatter1.rows(p.t, c)
        r.n2[own] = (after * scale * r.gain2[...][None, :]).astype(BF)
        gather2.send(c)
        return carry

    lax.fori_loop(0, CHUNKS, second_norm, 0)

    def feed_forward(c, carry):
        gather2.receive(c)
        both = dot(take(r.n2, c), r.wgu[...])
        act_back = dot_right(take(r.cot, c), r.wd[...])
        gate, up = both[:, :units], both[:, units:]
        s = 1.0 / (1.0 + jnp.exp(-gate))
        silu = gate * s
        put(r.act, c, (silu * up).astype(BF))
        gate_back = (act_back * up * s * (1.0 + gate * (1.0 - s))).astype(BF)
        up_back = (act_back * silu).astype(BF)
        put(r.gub, c, gate_back, slice(0, units))
        put(r.gub, c, up_back, slice(units, 2 * units))
        back = dot_right(gate_back, r.wgu[:, 0:units]) + dot_right(up_back, r.wgu[:, units:])
        put(r.part3, c, back.astype(BF))
        scatter3.send(c)

        @pl.when(c > 0)
        def _():
            scatter3.middle(c - 1)

        return carry

    lax.fori_loop(0, CHUNKS, feed_forward, 0)
    scatter3.middle(CHUNKS - 1)

    tile = 2 * LANES

    def gate_up_tile(j, carry):
        at = pl.ds(pl.multiple_of(j * tile, tile), tile)
        r.gu_part[at] = dot(r.n2[:, at].T, r.gub[0:length]).astype(BF)
        return carry

    lax.fori_loop(0, width // tile, gate_up_tile, 0)
    spread("gu")

    r.sums[...] = jnp.zeros_like(r.sums)

    def norm_back(grad, values, scale, gain):
        scaled = grad * gain
        mean = jnp.mean(scaled * values, axis=1, keepdims=True)
        total = jnp.sum(grad * values * scale, axis=0, keepdims=True)
        return scale * scaled - values * (scale * scale * scale * mean), total

    def second_back(c, carry):
        span = scatter3.span(c)
        grad = scatter3.finish(c)
        row_grad, total = norm_back(grad, r.after[span], r.scale2[span, 0:1], r.gain2[...][None, :])
        r.sums[1, 0:1] += total
        own = scatter3.rows(p.t, c)
        after_grad = r.cot[own].astype(F32) + row_grad
        r.aftergrad[span] = after_grad
        r.ab[own] = after_grad.astype(BF)
        gather3.send(c)
        return carry

    lax.fori_loop(0, CHUNKS, second_back, 0)

    def branch_two(c, carry):
        put(r.part2, c, dot(take(r.act, c), r.wd[...]).astype(BF))
        scatter2.send(c)
        return carry

    lax.fori_loop(0, CHUNKS, branch_two, 0)
    pair_sums(0)
    for c in range(CHUNKS):
        scatter2.middle(c)

    def down_tile(j, carry):
        at = pl.ds(pl.multiple_of(j * tile, tile), tile)
        r.dn_part[at] = dot(r.cot[:, at].T, r.act[...]).astype(BF)
        return carry

    lax.fori_loop(0, width // tile, down_tile, 0)
    spread("dn")
    pair_sums(2)

    def attended_back(c, carry):
        gather3.receive(c)
        back = dot_right(take(r.ab, c), r.wop[...])
        inverse = take(r.inverse, c)
        for h in range(heads):
            at = slice(h * LANES, (h + 1) * LANES)
            put(r.do, c, (back[:, at] * inverse[:, h : h + 1]).astype(BF), at)
        return carry

    lax.fori_loop(0, CHUNKS, attended_back, 0)

    def unrotate(grads, span):
        grads = grads.astype(BF).astype(F32)
        turned = grads * r.cosine[span] - swap_halves(grads) * r.sines[span]
        return turned.astype(BF)

    def upright(block):
        return jnp.concatenate([block, jnp.zeros_like(block)], axis=0).T

    def attend_back(h, first, keys, kept, whole):
        span, at = slice(first, first + rows), slice(h * LANES, (h + 1) * LANES)
        do, q = r.do[span, at], r.q[span, at]
        weights = kept[h]
        prob_back = dot_right(do, r.v[0:keys, at])
        centre = jnp.sum(do.astype(F32) * r.att[span, at].astype(F32), axis=1, keepdims=True)
        score_back = (weights.astype(F32) * (prob_back - centre)).astype(BF)
        query_back = dot(score_back, r.k[0:keys, at]) * HD**-0.5
        r.mixb[span, at] = unrotate(query_back, span)
        key_back, value_back = dot(q.T[:HD], score_back), dot(do.T[:HD], weights)
        if whole:
            r.dk[...] = key_back
            r.dv[...] = value_back
        else:
            r.dk[:, 0:keys] += key_back
            r.dv[:, 0:keys] += value_back

    n1_turned, ab_turned = r.gub.at[0:width], r.wgu

    def turned_tile(j, carry):
        at = pl.ds(pl.multiple_of(j * tile, tile), tile)
        n1_turned[at] = r.n1[:, at].T
        ab_turned[at] = r.ab[:, at].T
        return carry

    lax.fori_loop(0, width // tile, turned_tile, 0)

    def head_tiles(h):
        part = getattr(r, f"at{h}_part")
        lanes = [slice(c * padded + h * LANES, c * padded + (h + 1) * LANES) for c in range(3)]

        mixed = jnp.concatenate([r.mixb[:, span] for span in lanes], axis=1)
        grad = dot(n1_turned[...], mixed)
        outer = dot(ab_turned[...], r.att[:, h * LANES : (h + 1) * LANES])
        first = grad[:, :LANES] + roll64(grad[:, LANES : 2 * LANES])
        second = grad[:, 2 * LANES :] + roll64(outer)
        part[:, 0:LANES] = first.astype(BF)
        part[:, LANES:] = second.astype(BF)

    pair_sums(1)
    for h in range(heads):
        for i in reversed(range(SPLIT)):
            first, keys, kept = blocks[i]
            attend_back(h, first, keys, kept, i == SPLIT - 1)
        for i in range(SPLIT):
            span = slice(i * rows, (i + 1) * rows)
            at = padded + h * LANES
            key_back = upright(r.dk[:, span]) * math.log(2.0)
            r.mixb[span, at : at + LANES] = unrotate(key_back, span)
            at = 2 * padded + h * LANES
            r.mixb[span, at : at + LANES] = upright(r.dv[:, span]).astype(BF)
        if h < heads - 1:
            head_tiles(h)
            spread(f"at{h}")
            pair_sums((1, 2)[h])
    scatter1.close()

    def first_norm_part(c, carry):
        put(r.part1, c, dot(take(r.mixb, c), r.wap[...]).astype(BF))
        scatter4.send(c)

        @pl.when(c > 0)
        def _():
            scatter4.middle(c - 1)

        return carry

    lax.fori_loop(0, CHUNKS, first_norm_part, 0)
    scatter4.middle(CHUNKS - 1)
    pair_sums(4)
    head_tiles(heads - 1)
    spread(f"at{heads - 1}")
    pair_sums(4)

    def block_out(c, carry):
        span = scatter2.span(c)
        r.block_out[span] = (r.after[span] + scatter2.finish(c)).astype(BF)
        return carry

    lax.fori_loop(0, CHUNKS, block_out, 0)

    def first_back(c, carry):
        span = scatter4.span(c)
        grad = scatter4.finish(c)
        row_grad, total = norm_back(grad, r.inputs[span], r.scale1[span, 0:1], r.gain1[...][None, :])
        r.sums[0, 0:1] += total
        embed_grad = r.aftergrad[span] + row_grad
        r.embed_grad[span] = embed_grad
        r.lifted[span] = embed_grad.astype(BF)
        return carry

    lax.fori_loop(0, CHUNKS, first_back, 0)

    row_back = dot_right(r.lifted[...], r.nw[...]).astype(BF)
    low_table = lane_of((slots, z.pair_width)) < z.table_width
    outgoing = jnp.where(low_table, dot(r.pick_t[0], row_back), dot(r.pick_t[1], row_back))
    r.back_out[...] = outgoing.astype(BF)
    pair_sums(0)

    def slots_of(block, turn, of):
        start = block * slots + (turn * n + of) * half_cap
        return pl.ds(pl.multiple_of(start, half_cap), half_cap)

    def back_copy(step, turn, incoming=False):
        to = peer(step)
        of = to if incoming else p.d
        return make_copy(
            r.back_out.at[slots_of(0, turn, to)],
            r.back_in.at[slots_of(p.t, turn, of)],
            r.back_sem.at[0, 0],
            r.back_sem.at[1, turn * n + of],
            dp=to,
        )

    def pass_copy(kind, turn, of, incoming=False):
        block = ((p.t, p.t1), (p.t, p.t2), (p.t2, p.t3))[kind][1 if incoming else 0]
        ref = r.back_in.at[slots_of(block, turn, of)]
        at = turn * n + of
        target = p.t2 if kind == 1 else p.t1
        return make_copy(
            ref, ref, r.pass_sem.at[2 * kind, at], r.pass_sem.at[2 * kind + 1, at], tensor=target
        )

    for turn in range(2):
        for step in range(1, n):
            back_copy(n - step, turn).start()
    for turn in range(2):
        r.back_in[slots_of(p.t, turn, p.d)] = r.back_out[slots_of(0, turn, p.d)]

    gains = jnp.concatenate(
        [r.sums[0, 0:1], r.sums[1, 0:1], jnp.zeros((LANES - 2, width), F32)], axis=0
    )
    small = jnp.concatenate([dot(r.lifted[...].T, r.grams[...]), gains.T], axis=1)
    if z.inside:
        for j in range(n * SPLIT):
            value = small[j * z.small : (j + 1) * z.small].astype(BF)
            r.sm_part[j % SPLIT, j // SPLIT] = value

        def small_near(slot):
            block = p.t3 if slot else p.t1
            return make_copy(
                r.sm_part.at[block],
                r.sm_near.at[slot],
                r.sm_sem.at[2 * slot],
                r.sm_sem.at[2 * slot + 1],
                tensor=p.t1,
            )

        small_far = make_copy(r.sm_send, r.sm_far, r.sm_sem.at[4], r.sm_sem.at[5], tensor=p.t2)

        def small_copy(step, incoming=False):
            to = peer(step)
            at = to if incoming else p.d
            return make_copy(
                r.sm_out.at[to], r.sm_in.at[at], r.sp_sem.at[0, 0], r.sp_sem.at[1, at], dp=to
            )

        small_near(1).start()
        small_near(0).start()
        small_near(1).wait_recv()
        r.sm_send[...] = (r.sm_part[p.t2].astype(F32) + r.sm_near[1].astype(F32)).astype(BF)
        small_far.start()
    else:
        r.sm_total[...] = small

    for turn in range(2):
        for step in range(n):
            if step > 0:
                back_copy(step, turn, True).wait_recv()
            pass_copy(1, turn, peer(step)).start()
            pass_copy(0, turn, peer(step)).start()
    if z.inside:
        small_near(0).wait_recv()
        small_far.wait_recv()
        total = r.sm_part[p.t].astype(F32) + r.sm_near[0].astype(F32) + r.sm_far[...].astype(F32)
        r.sm_out[...] = total.astype(BF)
        for step in range(1, n):
            small_copy(step).start()
        r.sm_in[p.d] = r.sm_out[p.d]
        pair_sums(6)
    for turn in range(2):
        for step in range(n):
            of = peer(step)
            pass_copy(1, turn, of, True).wait_recv()
            pass_copy(2, turn, of).start()
    for i in range(3):
        lid_copy(i, True).wait_recv()
    kept = z.table_rows // SPLIT
    low_table = lane_of((kept, LANES)) < HD
    wanted = row_of((kept, slots)) + p.t * kept

    def add_rows(b, fresh=False):
        block = pl.ds(pl.multiple_of(b * slots, slots), slots)
        hits = [onehot(r.lids[b, k][0:1] == wanted) for k in range(2)]
        left = dot(hits[0], r.back_in[block, 0 : 2 * LANES])
        right = dot(hits[1], r.back_in[block, LANES : 3 * LANES])
        sums = (left[:, :LANES], jnp.where(low_table, left[:, LANES:], right[:, :LANES]), right[:, LANES:])
        for g, value in enumerate(sums):
            at = slice(g * LANES, (g + 1) * LANES)
            r.table_grads[:, at] = value if fresh else r.table_grads[:, at] + value

    add_rows(p.t, True)
    for turn in range(2):
        for step in range(n):
            pass_copy(0, turn, peer(step), True).wait_recv()
    add_rows(p.t1)
    add_rows(p.t2)
    pair_sums(99)
    for turn in range(2):
        for step in range(n):
            pass_copy(2, turn, peer(step), True).wait_recv()
    add_rows(p.t3)

    if z.inside:
        for step in range(1, n):
            small_copy(step, True).wait_recv()
        r.sm_total[...] = jnp.sum(r.sm_in[...].astype(F32), axis=0)
        for spread in spreads.values():
            spread.finish()

    all_ids.wait_send()
    shared = [(r.rows_out, r.row_sem, cap), (r.back_out, r.back_sem, cap)]
    if z.inside:
        shared.append((r.sm_out, r.sp_sem, 1))
    for ref, sems, each in shared:
        ref = ref.at[pl.ds(0, (n - 1) * each)]
        make_copy(ref, ref, sems.at[0, 0], sems.at[1, 0], dp=peer(1)).wait_send()
    for i in range(3):
        lid_copy(i).wait_send()
    for gather in (gather1, gather2, gather3):
        gather.close()
    for scatter in scatters[1:]:
        scatter.close()
    for spread in spreads.values():
        spread.close()
    if z.inside:
        small_near(0).wait_send()
        small_near(1).wait_send()
        small_far.wait_send()
    for kind in range(3):
        for turn in range(2):
            for step in range(n):
                pass_copy(kind, turn, peer(step)).wait_send()


def finish_kernel(z, names, *refs):
    r = Refs(names, refs)
    r.block[...] = r.block_out[...]
    r.embed[...] = r.embed_grad[...]
    r.bigram[...] = r.table_grads[:, : 2 * LANES].T[: z.table_width]
    r.trigram[...] = r.table_grads[:, LANES:].T[2 * LANES - z.table_width :]
    r.ngram[...] = r.sm_total[:, : z.pair_width]
    gains = r.sm_total[:, z.pair_width :]
    r.first[...] = gains[:, 0:1].T
    r.second[...] = gains[:, 1:2].T
    r.gate[...] = r.gu_out[:, : z.units]
    r.up[...] = r.gu_out[:, z.units :]
    r.down[...] = r.dn_out[...]
    side = 3 * HD
    for h in range(z.heads):
        sums = getattr(r, f"at{h}_out")[...]
        r.attend[:, h * side : (h + 1) * side] = sums[:, :side]
        r.output[h * HD : (h + 1) * HD] = sums[:, LANES:].T[HD:]


def finish_outputs(z, got):
    kept = z.table_rows // SPLIT
    outs = dict(
        block=((z.rows, z.width), BF),
        embed=((z.rows, z.width), F32),
        bigram=((z.table_width, kept), F32),
        trigram=((z.table_width, kept), F32),
        ngram=((z.small, z.pair_width), F32),
        first=((1, z.small), F32),
        attend=((z.piece, 3 * HD * z.heads), F32),
        output=((HD * z.heads, z.piece), F32),
        second=((1, z.small), F32),
        gate=((z.piece, z.units), F32),
        up=((z.piece, z.units), F32),
        down=((z.piece, z.units), F32),
    )
    done = pl.pallas_call(
        functools.partial(finish_kernel, z, (*got, *outs)),
        out_shape=[jax.ShapeDtypeStruct(*item) for item in outs.values()],
        in_specs=[pl.BlockSpec(memory_space=pltpu.VMEM)] * len(got),
        out_specs=[pl.BlockSpec(memory_space=pltpu.VMEM)] * len(outs),
        name="finish",
    )(*got.values())
    done = dict(zip(outs, done, strict=True))
    for name in ("bigram", "trigram", "ngram", "down"):
        done[name] = done[name].T
    for name in ("first", "second"):
        done[name] = done[name].reshape(z.small)
    return tuple(done.values())


def shards(
    embedded,
    bigram_ids,
    trigram_ids,
    prefix_lens,
    bigram_table,
    trigram_table,
    ngram_weight,
    first_gain,
    attend_weight,
    output_weight,
    second_gain,
    gate_weight,
    up_weight,
    down_weight,
    cotangent,
):
    n = lax.axis_size("dp")
    rows, width = embedded.shape
    table_rows, table_width = bigram_table.shape
    heads, units = attend_weight.shape[1] // (3 * HD), gate_weight.shape[1]
    z = Sizes(n, rows, width, heads, units, table_rows, table_width)
    scratch, outs = scratch_of(z), outputs_of(z)
    names = (*INPUTS, *outs, *scratch)
    anywhere = pl.BlockSpec(memory_space=pl.ANY)
    in_specs = [anywhere] * len(INPUTS)
    in_specs[3] = pl.BlockSpec(memory_space=pltpu.SMEM)
    got = pl.pallas_call(
        functools.partial(block_kernel, z, names),
        out_shape=[jax.ShapeDtypeStruct(*item) for item in outs.values()],
        in_specs=in_specs,
        out_specs=[pl.BlockSpec(memory_space=pltpu.VMEM)] * len(outs),
        scratch_shapes=list(scratch.values()),
        compiler_params=pltpu.CompilerParams(
            collective_id=0, has_side_effects=True, vmem_limit_bytes=67043328
        ),
        name="block",
    )(
        embedded,
        bigram_ids.reshape(1, rows),
        trigram_ids.reshape(1, rows),
        prefix_lens,
        bigram_table.T,
        trigram_table.T,
        ngram_weight,
        first_gain,
        attend_weight.T,
        output_weight,
        second_gain,
        gate_weight,
        up_weight,
        down_weight,
        cotangent,
    )
    got = dict(zip(outs, got, strict=True))
    if not z.inside:

        def summed(part, axes):
            return lax.psum_scatter(part, axes, scatter_dimension=0, tiled=True)

        for name in ("gu", "dn", *(f"at{h}" for h in range(heads))):
            got[f"{name}_out"] = summed(got.pop(f"{name}_part").astype(F32), "dp")
        got["sm_total"] = summed(got["sm_total"], ("dp", "tensor"))
    return finish_outputs(z, got)


def solution(mesh):
    placed = (
        P(("dp", "tensor"), None),
        P(("dp", "tensor")),
        P(("dp", "tensor")),
        P("dp"),
        P("dp", None),
        P("dp", None),
        P(),
        P(),
        P(None, "tensor"),
        P("tensor", None),
        P(),
        P(None, "tensor"),
        P(None, "tensor"),
        P("tensor", None),
        P("dp", None),
    )
    return jax.shard_map(
        shards,
        mesh=mesh,
        in_specs=placed,
        out_specs=(
            P(("dp", "tensor"), None),
            P(("dp", "tensor"), None),
            P(("dp", "tensor"), None),
            P(("dp", "tensor"), None),
            P(None, ("dp", "tensor")),
            P(("dp", "tensor")),
            P("dp", "tensor"),
            P("tensor", "dp"),
            P(("dp", "tensor")),
            P("dp", "tensor"),
            P("dp", "tensor"),
            P("tensor", "dp"),
        ),
        check_vma=False,
    )
```

```python
import functools
import math

import jax
import jax.numpy as jnp
from jax import lax
from jax.experimental import pallas as pl
from jax.experimental.pallas import tpu as pltpu
from jax.sharding import PartitionSpec as P

BF = jnp.bfloat16
F32 = jnp.float32
HD = 64
LANES = 128
PREFIX_MOST = 512
SPLIT = 4
CHUNKS = 4

INPUTS = (
    "embedded", "bigram_ids", "trigram_ids", "prefix", "bigram_table", "trigram_table",
    "ngram_weight", "first_gain", "attend_weight", "output_weight", "second_gain",
    "gate_weight", "up_weight", "down_weight", "cotangent",
)


class Refs:
    def __init__(self, names, refs):
        self.__dict__.update(zip(names, refs, strict=True))


def dot(left, right):
    return jnp.dot(left, right, preferred_element_type=F32)


def dot_right(left, right):
    return lax.dot_general(left, right, (((1,), (1,)), ((), ())), preferred_element_type=F32)


def lane_of(shape):
    return lax.broadcasted_iota(jnp.int32, shape, len(shape) - 1)


def row_of(shape):
    return lax.broadcasted_iota(jnp.int32, shape, 0)


def onehot(test):
    return jnp.where(test, 1.0, 0.0).astype(BF)


def roll64(block):
    return pltpu.roll(block, 64, 1)


def swap_halves(block):
    return jnp.where(lane_of(block.shape) < 32, pltpu.roll(block, 96, 1), pltpu.roll(block, 32, 1))


class Sizes:
    def __init__(self, n, rows, width, heads, units, table_rows, table_width):
        self.n, self.rows, self.width, self.heads, self.units = n, rows, width, heads, units
        self.table_rows, self.table_width = table_rows, table_width
        self.length = rows * SPLIT
        self.keys = [max((i + 1) * rows, min(PREFIX_MOST, rows * SPLIT)) for i in range(SPLIT)]
        self.cap = max(16, 2 * rows // n)
        self.slots = n * self.cap
        self.padded = heads * LANES
        self.chunk = rows // CHUNKS
        self.piece = width // n
        self.pair_width = 2 * table_width
        self.small = width // (n * SPLIT)
        self.small_lanes = self.pair_width + LANES
        self.attn_lanes = 4 * HD
        self.inside = n == 8 and self.piece % 16 == 0 and self.small % 8 == 0


def make_copy(src, dst, send, recv, **where):
    return pltpu.make_async_remote_copy(
        src_ref=src, dst_ref=dst, send_sem=send, recv_sem=recv, device_id=where
    )


class Gather:
    def __init__(self, z, pos, full, sems):
        self.z, self.pos, self.full, self.sems = z, pos, full, sems

    def piece(self, block, c):
        start = pl.multiple_of(block * self.z.rows + c * self.z.chunk, self.z.chunk)
        return self.full.at[pl.ds(start, self.z.chunk)]

    def copy(self, kind, c, incoming=False):
        p = self.pos
        block = ((p.t, p.t1), (p.t, p.t2), (p.t2, p.t3))[kind][1 if incoming else 0]
        ref = self.piece(block, c)
        target = p.t2 if kind == 1 else p.t1
        return make_copy(
            ref, ref, self.sems.at[c, 2 * kind], self.sems.at[c, 2 * kind + 1], tensor=target
        )

    def send(self, c):
        self.copy(1, c).start()
        self.copy(0, c).start()

    def receive(self, c):
        self.copy(1, c, True).wait_recv()
        self.copy(2, c).start()
        self.copy(0, c, True).wait_recv()
        self.copy(2, c, True).wait_recv()

    def close(self):
        def body(c, carry):
            for kind in range(3):
                self.copy(kind, c).wait_send()
            return carry

        lax.fori_loop(0, CHUNKS, body, 0)


class Scatter:
    def __init__(self, z, pos, part, near, out, far, sems):
        self.z, self.pos, self.part, self.near = z, pos, part, near
        self.out, self.far, self.sems = out, far, sems

    def span(self, c):
        return pl.ds(pl.multiple_of(c * self.z.chunk, self.z.chunk), self.z.chunk)

    def rows(self, block, c):
        start = pl.multiple_of(block * self.z.rows + c * self.z.chunk, self.z.chunk)
        return pl.ds(start, self.z.chunk)

    def near_copy(self, slot, c):
        block = self.pos.t1 + slot * (self.pos.t3 - self.pos.t1)
        return make_copy(
            self.part.at[self.rows(block, c)],
            self.near.at[slot, self.span(c)],
            self.sems.at[c, 2 * slot],
            self.sems.at[c, 2 * slot + 1],
            tensor=self.pos.t1,
        )

    def far_copy(self, c):
        return make_copy(
            self.out.at[self.span(c)],
            self.far.at[self.span(c)],
            self.sems.at[c, 4],
            self.sems.at[c, 5],
            tensor=self.pos.t2,
        )

    def send(self, c):
        self.near_copy(1, c).start()
        self.near_copy(0, c).start()

    def middle(self, c):
        self.near_copy(1, c).wait_recv()
        own = self.part[self.rows(self.pos.t2, c)].astype(F32)
        self.out[self.span(c)] = (own + self.near[1, self.span(c)].astype(F32)).astype(BF)
        self.far_copy(c).start()

    def finish(self, c):
        self.near_copy(0, c).wait_recv()
        self.far_copy(c).wait_recv()
        own = self.part[self.rows(self.pos.t, c)].astype(F32)
        own = own + self.near[0, self.span(c)].astype(F32)
        return own + self.far[self.span(c)].astype(F32)

    def close(self):
        def body(c, carry):
            self.near_copy(0, c).wait_send()
            self.near_copy(1, c).wait_send()
            self.far_copy(c).wait_send()
            return carry

        lax.fori_loop(0, CHUNKS, body, 0)


class Spread:
    STEPS = 4

    def __init__(self, z, pos, axes, part, pair_in, next_out, next_in, out, sems):
        self.z, self.pos, self.part, self.pair_in = z, pos, part, pair_in
        self.next_out, self.next_in, self.out, self.sems = next_out, next_in, out, sems
        self.axes = axes
        self.order = (axes[1:], axes[1:2], axes[2:], ())

    def across(self, axes):
        place, parity = self.pos.place, self.pos.parity
        if "near" in axes:
            place = place + 1 - 2 * lax.rem(place, 2)
        if "far" in axes:
            place = lax.rem(place + 2, 4)
        if "x" in axes:
            parity = 1 - parity
        return 2 * place + parity

    def rows(self, peer):
        return pl.ds(pl.multiple_of(peer * self.z.piece, self.z.piece), self.z.piece)

    def pair_copy(self, step):
        return make_copy(
            self.part.at[self.rows(self.across(self.axes[:1] + self.order[step]))],
            self.pair_in.at[step],
            self.sems.at[0, step],
            self.sems.at[1, step],
            dp=self.across(self.axes[:1]),
        )

    def next_copy(self, step):
        return make_copy(
            self.next_out.at[step],
            self.next_in.at[step],
            self.sems.at[2, step],
            self.sems.at[3, step],
            dp=self.across(self.axes[1:2] if step < 2 else self.axes[2:]),
        )

    def send(self):
        for step in range(4):
            self.pair_copy(step).start()

    def middle(self, step):
        self.pair_copy(step).wait_recv()
        own = self.part[self.rows(self.across(self.order[step]))].astype(F32)
        total = own + self.pair_in[step].astype(F32)
        if step >= 2:
            self.next_copy(step - 2).wait_recv()
            total = total + self.next_in[step - 2].astype(F32)
        if step == 3:
            self.out[...] = total
        else:
            self.next_out[step] = total.astype(BF)
            self.next_copy(step).start()

    def finish(self):
        self.next_copy(2).wait_recv()
        self.out[...] += self.next_in[2].astype(F32)

    def close(self):
        for step in range(4):
            self.pair_copy(step).wait_send()
            if step < 3:
                self.next_copy(step).wait_send()


class Position:
    def __init__(self, z):
        self.d, self.t = lax.axis_index("dp"), lax.axis_index("tensor")
        core, side = lax.rem(self.t, 2), self.t // 2
        self.t1 = self.t + 1 - 2 * core
        self.t2 = self.t + 2 - 4 * side
        self.t3 = self.t1 + 2 - 4 * side
        self.parity, self.place = lax.rem(self.d, 2), self.d // 2


def scratch_of(z):
    n, rows, width, length, chunks = z.n, z.rows, z.width, z.length, CHUNKS
    vmem, dma = pltpu.VMEM, pltpu.SemaphoreType.DMA
    shapes = dict(
        emb=vmem((rows, width), BF),
        ids=vmem((2 * n, 1, rows), jnp.int32),
        own_ids=vmem((2, 1, rows), jnp.int32),
        pick=vmem((2, rows, z.slots), BF),
        table_b=vmem((z.table_width, z.table_rows), BF),
        table_t=vmem((z.table_width, z.table_rows), BF),
        nw=vmem((z.pair_width, width), BF),
        gain1=vmem((width,), F32),
        gain2=vmem((width,), F32),
        wap=vmem((3 * z.padded, width), BF),
        wop=vmem((z.padded, width), BF),
        wgu=vmem((width, 2 * z.units), BF),
        wd=vmem((z.units, width), BF),
        cot=vmem((length, width), BF),
        cosine=vmem((length, LANES), F32),
        sines=vmem((length, LANES), F32),
        pick_t=vmem((2, z.slots, rows), BF),
        lids=vmem((SPLIT, 2, 8, z.slots), jnp.int32),
        rows_out=vmem((z.slots, z.pair_width), BF),
        rows_in=vmem((z.slots, z.pair_width), BF),
        grams=vmem((rows, z.pair_width), BF),
        inputs=vmem((rows, width), F32),
        after=vmem((rows, width), F32),
        aftergrad=vmem((rows, width), F32),
        inverse=vmem((length, LANES), F32),
        scale1=vmem((rows, LANES), F32),
        scale2=vmem((rows, LANES), F32),
        n1=vmem((length, width), BF),
        n2=vmem((length, width), BF),
        ab=vmem((length, width), BF),
        q=vmem((length, z.padded), BF),
        k=vmem((length, z.padded), BF),
        v=vmem((length, z.padded), BF),
        probs0=vmem((z.heads, rows, z.keys[0]), BF),
        probs1=vmem((z.heads, rows, z.keys[1]), BF),
        probs2=vmem((z.heads, rows, z.keys[2]), BF),
        probs3=vmem((z.heads, rows, z.keys[3]), BF),
        att=vmem((length, z.padded), BF),
        do=vmem((length, z.padded), BF),
        dk=vmem((HD, length), F32),
        dv=vmem((HD, length), F32),
        mixb=vmem((length, 3 * z.padded), BF),
        act=vmem((length, z.units), BF),
        gub=vmem((max(length, width), 2 * z.units), BF),
        lifted=vmem((rows, width), BF),
        sums=vmem((2, 8, width), F32),
        back_out=vmem((z.slots, z.pair_width), BF),
        back_in=vmem((SPLIT * z.slots, z.pair_width), BF),
        in_sem=dma((12 + 4 * z.heads,)),
        id_sem=dma((2,)),
        row_sem=dma((2, n)),
        lid_sem=dma((2, 3)),
        back_sem=dma((2, 2 * n)),
        pass_sem=dma((6, 2 * n)),
        ag1_sem=dma((chunks, 6)),
        ag2_sem=dma((chunks, 6)),
        ag3_sem=dma((chunks, 6)),
    )
    for k in range(1, 4):
        shapes[f"part{k}"] = vmem((length, width), BF)
        shapes[f"near{k}"] = vmem((2, rows, width), BF)
        shapes[f"send{k}"] = vmem((rows, width), BF)
        shapes[f"far{k}"] = vmem((rows, width), BF)
        shapes[f"rs{k}_sem"] = dma((chunks, 6))
    shapes["rs4_sem"] = dma((chunks, 6))
    if z.inside:
        heads = [(f"at{h}", z.attn_lanes) for h in range(z.heads)]
        for name, lanes in (("ga", z.units), ("up", z.units), ("dn", z.units), *heads):
            shapes[f"{name}_part"] = vmem((width, lanes), BF)
            shapes[f"{name}_pair_in"] = vmem((4, z.piece, lanes), BF)
            shapes[f"{name}_next_out"] = vmem((3, z.piece, lanes), BF)
            shapes[f"{name}_next_in"] = vmem((3, z.piece, lanes), BF)
            shapes[f"{name}_sem"] = dma((4, 4))
        small = (n, z.small, z.small_lanes)
        shapes["sm_part"] = vmem((SPLIT, *small), BF)
        shapes["sm_near"] = vmem((2, *small), BF)
        shapes["sm_send"] = vmem(small, BF)
        shapes["sm_far"] = vmem(small, BF)
        shapes["sm_out"] = vmem(small, BF)
        shapes["sm_in"] = vmem(small, BF)
        shapes["sm_sem"] = dma((6,))
        shapes["sp_sem"] = dma((2, n))
    return shapes


def outputs_of(z):
    n, rows, width = z.n, z.rows, z.width
    shapes = dict(
        block_out=((rows, width), BF),
        embed_grad=((rows, width), F32),
        table_grads=((z.table_rows // SPLIT, z.pair_width), F32),
    )
    if z.inside:
        shapes["ga_out"] = ((z.piece, z.units), F32)
        shapes["up_out"] = ((z.piece, z.units), F32)
        shapes["dn_out"] = ((z.piece, z.units), F32)
        for h in range(z.heads):
            shapes[f"at{h}_out"] = ((z.piece, z.attn_lanes), F32)
        shapes["sm_total"] = ((z.small, z.small_lanes), F32)
    else:
        shapes["ga_part"] = ((width, z.units), BF)
        shapes["up_part"] = ((width, z.units), BF)
        shapes["dn_part"] = ((width, z.units), BF)
        for h in range(z.heads):
            shapes[f"at{h}_part"] = ((width, z.attn_lanes), BF)
        shapes["sm_total"] = ((width, z.small_lanes), F32)
    return shapes


def block_kernel(z, names, *refs):
    r = Refs(names, refs)
    p = Position(z)
    n, rows, width, length = z.n, z.rows, z.width, z.length
    cap, slots, units, padded, heads = z.cap, z.slots, z.units, z.padded, z.heads
    gather1 = Gather(z, p, r.n1, r.ag1_sem)
    gather2 = Gather(z, p, r.n2, r.ag2_sem)
    gather3 = Gather(z, p, r.ab, r.ag3_sem)
    scatters = [
        Scatter(
            z, p, getattr(r, f"part{k}"), getattr(r, f"near{k}"), getattr(r, f"send{k}"),
            getattr(r, f"far{k}"), sems,
        )
        for k, sems in ((1, r.rs1_sem), (2, r.rs2_sem), (3, r.rs3_sem), (1, r.rs4_sem))
    ]
    scatter1, scatter2, scatter3, scatter4 = scatters
    spreads = {}
    if z.inside:
        for name in ("ga", "up", "dn", *(f"at{h}" for h in range(heads))):
            axes = ("near", "far", "x") if name == "ga" else ("x", "near", "far")
            spreads[name] = Spread(
                z, p, axes, getattr(r, f"{name}_part"), getattr(r, f"{name}_pair_in"),
                getattr(r, f"{name}_next_out"), getattr(r, f"{name}_next_in"),
                getattr(r, f"{name}_out"), getattr(r, f"{name}_sem"),
            )

    def peer(step):
        return lax.rem(p.d + step, n)

    barrier = pltpu.get_barrier_semaphore()
    for step in range(1, n):
        pl.semaphore_signal(barrier, inc=1, device_id={"dp": peer(step)})
    for target in (p.t1, p.t2, p.t3):
        pl.semaphore_signal(barrier, inc=1, device_id={"tensor": target})

    loads = [
        (r.bigram_ids, r.own_ids.at[0]),
        (r.trigram_ids, r.own_ids.at[1]),
        (r.bigram_table, r.table_b),
        (r.trigram_table, r.table_t),
        (r.embedded, r.emb),
        (r.ngram_weight, r.nw),
        (r.first_gain, r.gain1),
        (r.second_gain, r.gain2),
        (r.gate_weight, r.wgu.at[:, pl.ds(0, units)]),
        (r.up_weight, r.wgu.at[:, pl.ds(units, units)]),
        (r.down_weight, r.wd),
        (r.cotangent, r.cot),
    ]
    for h in range(heads):
        for c in range(3):
            src = r.attend_weight.at[pl.ds((3 * h + c) * HD, HD)]
            loads.append((src, r.wap.at[pl.ds(c * padded + h * LANES, HD)]))
        src = r.output_weight.at[pl.ds(h * HD, HD)]
        loads.append((src, r.wop.at[pl.ds(h * LANES, HD)]))
    loads = [pltpu.make_async_copy(src, dst, r.in_sem.at[i]) for i, (src, dst) in enumerate(loads)]
    for load in loads[:4]:
        load.start()

    pl.semaphore_wait(barrier, n - 1 + 3)

    def id_copy(step, k):
        return make_copy(
            (r.bigram_ids, r.trigram_ids)[k],
            r.ids.at[k * n + p.d],
            r.id_sem.at[0],
            r.id_sem.at[1],
            dp=peer(step),
        )

    for step in range(1, n):
        for k in range(2):
            id_copy(step, k).start()
    for load in loads[4:]:
        load.start()

    lane = lane_of((32, LANES))
    low = jnp.where(lane < 32, lane, lane - 32)
    frequency = jnp.exp(low.astype(F32) * (-2.0 * math.log(10000.0) / HD))
    place = row_of((32, LANES)).astype(F32)
    coarse, fine = place * 32.0 * frequency, place * frequency
    cos_coarse, sin_coarse = jnp.cos(coarse), jnp.sin(coarse)
    used = lane < HD
    cos_fine = jnp.where(used, jnp.cos(fine), 0.0)
    sin_fine = jnp.where(used, jnp.sin(fine), 0.0)
    sign = jnp.where(lane < 32, -1.0, 1.0)
    for a in range(length // 32):
        ca, sa = cos_coarse[a : a + 1], sin_coarse[a : a + 1]
        r.cosine[a * 32 : (a + 1) * 32] = ca * cos_fine - sa * sin_fine
        r.sines[a * 32 : (a + 1) * 32] = sign * (sa * cos_fine + ca * sin_fine)

    loads[0].wait()
    loads[1].wait()
    earlier = onehot(row_of((rows, rows)) < lane_of((rows, rows)))
    later = onehot(row_of((rows, rows)) > lane_of((rows, rows)))
    lane = lane_of((rows, LANES))
    start, half_cap = (lane * z.table_rows).astype(F32), cap // 2
    for k in range(2):
        r.ids[k * n + p.d] = r.own_ids[k]
        column = jnp.broadcast_to(r.own_ids[k].astype(F32), (LANES, rows)).T
        held = (column >= start) & (column < start + z.table_rows)
        ranks = dot(later, onehot(held))
        slot = jnp.where(held, ranks + (lane * cap).astype(F32), 0.0)
        slot = jnp.sum(slot, axis=1, keepdims=True)
        r.pick[k] = onehot(slot.astype(jnp.int32) == lane_of((rows, slots)))
        second = jnp.where(ranks >= half_cap, float((n - 1) * half_cap), 0.0)
        slot = jnp.where(held, ranks + (lane * half_cap).astype(F32) + second, 0.0)
        slot = jnp.sum(slot, axis=1, keepdims=True)
        across = jnp.broadcast_to(slot, (rows, LANES)).T[0:1]
        r.pick_t[k] = onehot(across.astype(jnp.int32) == row_of((slots, rows)))

    for h in range(heads):
        empty = jnp.zeros((LANES - HD, width), BF)
        for c in range(3):
            at = c * padded + h * LANES + HD
            r.wap[at : at + LANES - HD] = empty
        r.wop[h * LANES + HD : (h + 1) * LANES] = empty

    loads[2].wait()
    loads[3].wait()
    all_ids = r.ids.at[pl.ds(0, 2 * (n - 1))]
    all_ids = make_copy(all_ids, all_ids, r.id_sem.at[0], r.id_sem.at[1], dp=peer(1))
    all_ids.wait_recv()
    asked = jnp.concatenate([r.ids[i] for i in range(2 * n)], axis=0)
    first_row = p.d * z.table_rows
    mine = (asked >= first_row) & (asked < first_row + z.table_rows)
    ranks = dot(onehot(mine), earlier)
    tags = jnp.where(mine, ranks, -1.0).astype(jnp.int32)
    local = jnp.where(mine, asked - first_row + 1, 0).astype(F32)
    picked = []
    for k in range(2):
        columns = []
        for i in range(n):
            at = k * n + i
            hit = tags[at : at + 1] == row_of((cap, rows))
            value = jnp.where(hit, local[at : at + 1], 0.0)
            columns.append(jnp.sum(value, axis=1, keepdims=True) - 1.0)
        picked.append(jnp.concatenate(columns, axis=0).astype(jnp.int32))
        columns = [item[:half_cap] for item in columns] + [item[half_cap:] for item in columns]
        column = jnp.concatenate(columns, axis=0)
        across = jnp.broadcast_to(column, (slots, LANES)).T[0:8]
        r.lids[p.t, k] = across.astype(jnp.int32)
    half = slots // 2

    def row_copy(step):
        to = peer(step)
        return make_copy(
            r.rows_out.at[pl.ds(pl.multiple_of(to * cap, cap), cap)],
            r.rows_in.at[pl.ds(pl.multiple_of(p.d * cap, cap), cap)],
            r.row_sem.at[0, 0],
            r.row_sem.at[1, p.d],
            dp=to,
        )

    def row_arrival(step):
        of = peer(step)
        ref = r.rows_in.at[pl.ds(pl.multiple_of(of * cap, cap), cap)]
        return make_copy(ref, ref, r.row_sem.at[0, 0], r.row_sem.at[1, of], dp=of)

    for part in range(2):
        found = []
        for k, table in enumerate((r.table_b, r.table_t)):
            chosen = picked[k][part * half : (part + 1) * half]
            hits = onehot(chosen == lane_of((half, z.table_rows)))
            both = dot_right(hits, table[...])
            fill = jnp.zeros((half, 2 * LANES - z.table_width), F32)
            found.append((both[:, :LANES], jnp.concatenate([both[:, LANES:], fill], axis=1)))
        low_half = lane_of((half, LANES)) < HD
        rolled = [roll64(block) for block in found[1]]
        span = slice(part * half, (part + 1) * half)
        r.rows_out[span, 0:LANES] = found[0][0].astype(BF)
        middle = jnp.where(low_half, found[0][1], rolled[0])
        r.rows_out[span, LANES : 2 * LANES] = middle.astype(BF)
        r.rows_out[span, 2 * LANES :] = jnp.where(low_half, rolled[0], rolled[1]).astype(BF)
    for step in range(1, n):
        row_copy(n - step).start()
    own_slots = pl.ds(pl.multiple_of(p.d * cap, cap), cap)
    r.rows_in[own_slots] = r.rows_out[own_slots]

    for load in loads[4:8]:
        load.wait()
    for step in range(1, n):
        row_arrival(step).wait_recv()
    fetched = r.rows_in[...]
    low_table = lane_of((rows, z.pair_width)) < z.table_width
    grams = jnp.where(low_table, dot(r.pick[0], fetched), dot(r.pick[1], fetched)).astype(BF)
    r.grams[...] = grams
    inputs = r.emb[...].astype(F32) + dot(grams, r.nw[...])
    r.inputs[...] = inputs
    scale = lax.rsqrt(jnp.mean(inputs * inputs, axis=1, keepdims=True) + 1e-05)
    r.scale1[...] = jnp.broadcast_to(scale, (rows, LANES))
    own_rows = pl.ds(pl.multiple_of(p.t * rows, rows), rows)
    r.n1[own_rows] = (inputs * scale * r.gain1[...][None, :]).astype(BF)
    for c in range(CHUNKS):
        gather1.send(c)

    def lid_copy(i, incoming=False):
        target = (p.t1, p.t2, p.t3)[i]
        ref = r.lids.at[target if incoming else p.t]
        return make_copy(ref, ref, r.lid_sem.at[0, i], r.lid_sem.at[1, i], tensor=target)

    for i in range(3):
        lid_copy(i).start()

    def spans(c):
        return [
            pl.ds(pl.multiple_of(b * rows + c * z.chunk, z.chunk), z.chunk) for b in range(SPLIT)
        ]

    def take(ref, c, *rest):
        return jnp.concatenate([ref[(span, *rest)] for span in spans(c)], axis=0)

    def put(ref, c, value, *rest):
        for b, span in enumerate(spans(c)):
            ref[(span, *rest)] = value[b * z.chunk : (b + 1) * z.chunk]

    for load in loads[8:]:
        load.wait()

    def project(c, carry):
        gather1.receive(c)
        mixture = dot_right(take(r.n1, c), r.wap[...])
        cosine, sines = take(r.cosine, c), take(r.sines, c)
        for h in range(heads):
            for i, ref in enumerate((r.q, r.k)):
                at = i * padded + h * LANES
                block = mixture[:, at : at + LANES]
                turned = block * cosine + swap_halves(block) * sines
                if i == 0:
                    turned = turned * (HD**-0.5 * math.log2(math.e))
                put(ref, c, turned.astype(BF), slice(h * LANES, (h + 1) * LANES))
            at = 2 * padded + h * LANES
            block = mixture[:, at : at + LANES]
            block = jnp.where(lane_of(block.shape) == HD, 1.0, block)
            put(r.v, c, block.astype(BF), slice(h * LANES, (h + 1) * LANES))
        return carry

    lax.fori_loop(0, CHUNKS, project, 0)

    prefix = r.prefix[0]
    probs = (r.probs0, r.probs1, r.probs2, r.probs3)
    blocks = [(i * rows, z.keys[i], probs[i]) for i in range(SPLIT)]

    def attend(first, keys, kept):
        span = slice(first, first + rows)
        lane = lane_of((rows, LANES))
        row, column = row_of((rows, rows)), lane_of((rows, rows))

        def score_tiles(h):
            at = slice(h * LANES, (h + 1) * LANES)
            tiles = []
            for start in range(0, keys, rows):
                scores = dot_right(r.q[span, at], r.k[start : start + rows, at])
                allowed = None
                if start == first:
                    allowed = column <= row
                if start + rows > first + 1 and start < PREFIX_MOST:
                    in_prefix = column < prefix - start
                    allowed = in_prefix if allowed is None else allowed | in_prefix
                if allowed is not None:
                    scores = jnp.where(allowed, scores, -1000000000.0)
                tiles.append(scores)
            return tiles

        inverses = jnp.zeros((rows, LANES), F32)
        every = [score_tiles(h) for h in range(heads)]
        tops = [jnp.max(functools.reduce(jnp.maximum, tiles), axis=1, keepdims=True) for tiles in every]
        totals = []
        for h in range(heads):
            at = slice(h * LANES, (h + 1) * LANES)
            total = jnp.zeros((rows, LANES), F32)
            for j, scores in enumerate(every[h]):
                weights = jnp.exp2(scores - tops[h]).astype(BF)
                kept[h, :, j * rows : (j + 1) * rows] = weights
                total = total + dot(weights, r.v[j * rows : (j + 1) * rows, at])
            totals.append(total)
        for h, total in enumerate(totals):
            at = slice(h * LANES, (h + 1) * LANES)
            inverse = 1.0 / total[:, HD : HD + 1]
            r.att[span, at] = jnp.where(lane < HD, total * inverse, 0.0).astype(BF)
            inverses = jnp.where(lane == h, inverse, inverses)
        r.inverse[span] = inverses
        r.part1[span] = dot(r.att[span], r.wop[...]).astype(BF)

    def attend_step(step, carry):
        core, side = lax.rem(p.t, 2), p.t // 2
        side = side + (1 - step // 2) * (1 - 2 * side)
        core = core + (1 - lax.rem(step, 2)) * (1 - 2 * core)
        wanted = 2 * side + core
        for i, block in enumerate(blocks):

            @pl.when(wanted == i)
            def _(block=block):
                attend(*block)

        @pl.when(lax.rem(step, 2) == 0)
        def _():
            for c in range(CHUNKS):
                scatter1.near_copy(1 - step // 2, c).start()

        @pl.when(step == 1)
        def _():
            for c in range(CHUNKS):
                scatter1.middle(c)

        return carry

    lax.fori_loop(0, SPLIT, attend_step, 0)

    waiting = []

    def spread(name):
        if z.inside:
            spreads[name].send()
            waiting.extend((name, step) for step in range(Spread.STEPS))

    def pair_sums(count):
        for name, step in waiting[:count]:
            spreads[name].middle(step)
        del waiting[:count]

    def second_norm(c, carry):
        span = scatter1.span(c)
        after = r.inputs[span] + scatter1.finish(c)
        r.after[span] = after
        scale = lax.rsqrt(jnp.mean(after * after, axis=1, keepdims=True) + 1e-05)
        r.scale2[span] = jnp.broadcast_to(scale, (z.chunk, LANES))
        own = scatter1.rows(p.t, c)
        r.n2[own] = (after * scale * r.gain2[...][None, :]).astype(BF)
        gather2.send(c)
        return carry

    lax.fori_loop(0, CHUNKS, second_norm, 0)

    def feed_forward(c, carry):
        gather2.receive(c)
        both = dot(take(r.n2, c), r.wgu[...])
        act_back = dot_right(take(r.cot, c), r.wd[...])
        gate, up = both[:, :units], both[:, units:]
        s = 1.0 / (1.0 + jnp.exp(-gate))
        silu = gate * s
        put(r.act, c, (silu * up).astype(BF))
        gate_back = (act_back * up * s * (1.0 + gate * (1.0 - s))).astype(BF)
        up_back = (act_back * silu).astype(BF)
        put(r.gub, c, gate_back, slice(0, units))
        put(r.gub, c, up_back, slice(units, 2 * units))
        back = dot_right(gate_back, r.wgu[:, 0:units]) + dot_right(up_back, r.wgu[:, units:])
        put(r.part3, c, back.astype(BF))
        scatter3.send(c)

        @pl.when(c > 0)
        def _():
            scatter3.middle(c - 1)

        return carry

    lax.fori_loop(0, CHUNKS, feed_forward, 0)
    scatter3.middle(CHUNKS - 1)

    tile = 2 * LANES

    def gate_up_tile(j, carry):
        at = pl.ds(pl.multiple_of(j * tile, tile), tile)
        both = dot(r.n2[:, at].T, r.gub[0:length]).astype(BF)
        r.ga_part[at] = both[:, :units]
        r.up_part[at] = both[:, units:]
        return carry

    lax.fori_loop(0, width // tile, gate_up_tile, 0)
    if z.inside:
        spreads["ga"].send()
        spreads["up"].send()
        waiting.extend((name, step) for step in range(Spread.STEPS) for name in ("ga", "up"))

    r.sums[...] = jnp.zeros_like(r.sums)

    def norm_back(grad, values, scale, gain):
        scaled = grad * gain
        mean = jnp.mean(scaled * values, axis=1, keepdims=True)
        total = jnp.sum(grad * values * scale, axis=0, keepdims=True)
        return scale * scaled - values * (scale * scale * scale * mean), total

    def second_back(c, carry):
        span = scatter3.span(c)
        grad = scatter3.finish(c)
        row_grad, total = norm_back(grad, r.after[span], r.scale2[span, 0:1], r.gain2[...][None, :])
        r.sums[1, 0:1] += total
        own = scatter3.rows(p.t, c)
        after_grad = r.cot[own].astype(F32) + row_grad
        r.aftergrad[span] = after_grad
        r.ab[own] = after_grad.astype(BF)
        gather3.send(c)
        return carry

    lax.fori_loop(0, CHUNKS, second_back, 0)


    def branch_two(c, carry):
        put(r.part2, c, dot(take(r.act, c), r.wd[...]).astype(BF))
        scatter2.send(c)
        return carry

    lax.fori_loop(0, CHUNKS, branch_two, 0)
    for c in range(CHUNKS):
        scatter2.middle(c)

    def down_tile(j, carry):
        at = pl.ds(pl.multiple_of(j * tile, tile), tile)
        r.dn_part[at] = dot(r.cot[:, at].T, r.act[...]).astype(BF)
        return carry

    lax.fori_loop(0, width // tile, down_tile, 0)
    spread("dn")
    pair_sums(4)

    def attended_back(c, carry):
        gather3.receive(c)
        back = dot_right(take(r.ab, c), r.wop[...])
        inverse = take(r.inverse, c)
        for h in range(heads):
            at = slice(h * LANES, (h + 1) * LANES)
            put(r.do, c, (back[:, at] * inverse[:, h : h + 1]).astype(BF), at)
        return carry

    lax.fori_loop(0, CHUNKS, attended_back, 0)

    def unrotate(grads, span):
        grads = grads.astype(BF).astype(F32)
        turned = grads * r.cosine[span] - swap_halves(grads) * r.sines[span]
        return turned.astype(BF)

    def upright(block):
        return jnp.concatenate([block, jnp.zeros_like(block)], axis=0).T

    def attend_back(h, first, keys, kept, whole):
        span, at = slice(first, first + rows), slice(h * LANES, (h + 1) * LANES)
        do, q = r.do[span, at], r.q[span, at]
        weights = kept[h]
        prob_back = dot_right(do, r.v[0:keys, at])
        centre = jnp.sum(do.astype(F32) * r.att[span, at].astype(F32), axis=1, keepdims=True)
        score_back = (weights.astype(F32) * (prob_back - centre)).astype(BF)
        query_back = dot(score_back, r.k[0:keys, at]) * HD**-0.5
        r.mixb[span, at] = unrotate(query_back, span)
        key_back, value_back = dot(q.T[:HD], score_back), dot(do.T[:HD], weights)
        if whole:
            r.dk[...] = key_back
            r.dv[...] = value_back
        else:
            r.dk[:, 0:keys] += key_back
            r.dv[:, 0:keys] += value_back

    n1_turned, ab_turned = r.gub.at[0:width], r.wgu

    def turned_tile(j, carry):
        at = pl.ds(pl.multiple_of(j * tile, tile), tile)
        n1_turned[at] = r.n1[:, at].T
        ab_turned[at] = r.ab[:, at].T
        return carry

    lax.fori_loop(0, width // tile, turned_tile, 0)

    def head_tiles(h):
        part = getattr(r, f"at{h}_part")
        lanes = [slice(c * padded + h * LANES, c * padded + (h + 1) * LANES) for c in range(3)]

        mixed = jnp.concatenate([r.mixb[:, span] for span in lanes], axis=1)
        grad = dot(n1_turned[...], mixed)
        outer = dot(ab_turned[...], r.att[:, h * LANES : (h + 1) * LANES])
        first = grad[:, :LANES] + roll64(grad[:, LANES : 2 * LANES])
        second = grad[:, 2 * LANES :] + roll64(outer)
        part[:, 0:LANES] = first.astype(BF)
        part[:, LANES:] = second.astype(BF)

    for h in range(heads):
        for i in reversed(range(SPLIT)):
            first, keys, kept = blocks[i]
            attend_back(h, first, keys, kept, i == SPLIT - 1)
        for i in range(SPLIT):
            span = slice(i * rows, (i + 1) * rows)
            at = padded + h * LANES
            key_back = upright(r.dk[:, span]) * math.log(2.0)
            r.mixb[span, at : at + LANES] = unrotate(key_back, span)
            at = 2 * padded + h * LANES
            r.mixb[span, at : at + LANES] = upright(r.dv[:, span]).astype(BF)
        if h < heads - 1:
            head_tiles(h)
            spread(f"at{h}")
            pair_sums((4, 2)[h])
    scatter1.close()

    def first_norm_part(c, carry):
        put(r.part1, c, dot(take(r.mixb, c), r.wap[...]).astype(BF))
        scatter4.send(c)

        @pl.when(c > 0)
        def _():
            scatter4.middle(c - 1)

        return carry

    lax.fori_loop(0, CHUNKS, first_norm_part, 0)
    scatter4.middle(CHUNKS - 1)
    pair_sums(3)
    head_tiles(heads - 1)
    spread(f"at{heads - 1}")
    pair_sums(5)

    def block_out(c, carry):
        span = scatter2.span(c)
        r.block_out[span] = (r.after[span] + scatter2.finish(c)).astype(BF)
        return carry

    lax.fori_loop(0, CHUNKS, block_out, 0)

    def first_back(c, carry):
        span = scatter4.span(c)
        grad = scatter4.finish(c)
        row_grad, total = norm_back(grad, r.inputs[span], r.scale1[span, 0:1], r.gain1[...][None, :])
        r.sums[0, 0:1] += total
        embed_grad = r.aftergrad[span] + row_grad
        r.embed_grad[span] = embed_grad
        r.lifted[span] = embed_grad.astype(BF)
        return carry

    lax.fori_loop(0, CHUNKS, first_back, 0)

    row_back = dot_right(r.lifted[...], r.nw[...]).astype(BF)
    low_table = lane_of((slots, z.pair_width)) < z.table_width
    outgoing = jnp.where(low_table, dot(r.pick_t[0], row_back), dot(r.pick_t[1], row_back))
    r.back_out[...] = outgoing.astype(BF)

    def slots_of(block, turn, of):
        start = block * slots + (turn * n + of) * half_cap
        return pl.ds(pl.multiple_of(start, half_cap), half_cap)

    def back_copy(step, turn, incoming=False):
        to = peer(step)
        of = to if incoming else p.d
        return make_copy(
            r.back_out.at[slots_of(0, turn, to)],
            r.back_in.at[slots_of(p.t, turn, of)],
            r.back_sem.at[0, 0],
            r.back_sem.at[1, turn * n + of],
            dp=to,
        )

    def pass_copy(kind, turn, of, incoming=False):
        block = ((p.t, p.t1), (p.t, p.t2), (p.t2, p.t3))[kind][1 if incoming else 0]
        ref = r.back_in.at[slots_of(block, turn, of)]
        at = turn * n + of
        target = p.t2 if kind == 1 else p.t1
        return make_copy(
            ref, ref, r.pass_sem.at[2 * kind, at], r.pass_sem.at[2 * kind + 1, at], tensor=target
        )

    for turn in range(2):
        for step in range(1, n):
            back_copy(n - step, turn).start()
    for turn in range(2):
        r.back_in[slots_of(p.t, turn, p.d)] = r.back_out[slots_of(0, turn, p.d)]

    gains = jnp.concatenate(
        [r.sums[0, 0:1], r.sums[1, 0:1], jnp.zeros((LANES - 2, width), F32)], axis=0
    )
    small = jnp.concatenate([dot(r.lifted[...].T, r.grams[...]), gains.T], axis=1)
    if z.inside:
        for j in range(n * SPLIT):
            value = small[j * z.small : (j + 1) * z.small].astype(BF)
            r.sm_part[j % SPLIT, j // SPLIT] = value

        def small_near(slot):
            block = p.t3 if slot else p.t1
            return make_copy(
                r.sm_part.at[block],
                r.sm_near.at[slot],
                r.sm_sem.at[2 * slot],
                r.sm_sem.at[2 * slot + 1],
                tensor=p.t1,
            )

        small_far = make_copy(r.sm_send, r.sm_far, r.sm_sem.at[4], r.sm_sem.at[5], tensor=p.t2)

        def small_copy(step, incoming=False):
            to = peer(step)
            at = to if incoming else p.d
            return make_copy(
                r.sm_out.at[to], r.sm_in.at[at], r.sp_sem.at[0, 0], r.sp_sem.at[1, at], dp=to
            )

        small_near(1).start()
        small_near(0).start()
        small_near(1).wait_recv()
        r.sm_send[...] = (r.sm_part[p.t2].astype(F32) + r.sm_near[1].astype(F32)).astype(BF)
        small_far.start()
    else:
        r.sm_total[...] = small

    for turn in range(2):
        for step in range(n):
            if step > 0:
                back_copy(step, turn, True).wait_recv()
            pass_copy(1, turn, peer(step)).start()
            pass_copy(0, turn, peer(step)).start()
    if z.inside:
        small_near(0).wait_recv()
        small_far.wait_recv()
        total = r.sm_part[p.t].astype(F32) + r.sm_near[0].astype(F32) + r.sm_far[...].astype(F32)
        r.sm_out[...] = total.astype(BF)
        for step in range(1, n):
            small_copy(step).start()
        r.sm_in[p.d] = r.sm_out[p.d]
        pair_sums(6)
    for turn in range(2):
        for step in range(n):
            of = peer(step)
            pass_copy(1, turn, of, True).wait_recv()
            pass_copy(2, turn, of).start()
    for i in range(3):
        lid_copy(i, True).wait_recv()
    kept = z.table_rows // SPLIT
    low_table = lane_of((kept, LANES)) < HD
    wanted = row_of((kept, slots)) + p.t * kept

    def add_rows(b, fresh=False):
        block = pl.ds(pl.multiple_of(b * slots, slots), slots)
        hits = [onehot(r.lids[b, k][0:1] == wanted) for k in range(2)]
        left = dot(hits[0], r.back_in[block, 0 : 2 * LANES])
        right = dot(hits[1], r.back_in[block, LANES : 3 * LANES])
        sums = (left[:, :LANES], jnp.where(low_table, left[:, LANES:], right[:, :LANES]), right[:, LANES:])
        for g, value in enumerate(sums):
            at = slice(g * LANES, (g + 1) * LANES)
            r.table_grads[:, at] = value if fresh else r.table_grads[:, at] + value

    add_rows(p.t, True)
    for turn in range(2):
        for step in range(n):
            pass_copy(0, turn, peer(step), True).wait_recv()
    add_rows(p.t1)
    add_rows(p.t2)
    pair_sums(99)
    for turn in range(2):
        for step in range(n):
            pass_copy(2, turn, peer(step), True).wait_recv()
    add_rows(p.t3)

    if z.inside:
        for step in range(1, n):
            small_copy(step, True).wait_recv()
        r.sm_total[...] = jnp.sum(r.sm_in[...].astype(F32), axis=0)
        for spread in spreads.values():
            spread.finish()

    all_ids.wait_send()
    shared = [(r.rows_out, r.row_sem, cap), (r.back_out, r.back_sem, cap)]
    if z.inside:
        shared.append((r.sm_out, r.sp_sem, 1))
    for ref, sems, each in shared:
        ref = ref.at[pl.ds(0, (n - 1) * each)]
        make_copy(ref, ref, sems.at[0, 0], sems.at[1, 0], dp=peer(1)).wait_send()
    for i in range(3):
        lid_copy(i).wait_send()
    for gather in (gather1, gather2, gather3):
        gather.close()
    for scatter in scatters[1:]:
        scatter.close()
    for spread in spreads.values():
        spread.close()
    if z.inside:
        small_near(0).wait_send()
        small_near(1).wait_send()
        small_far.wait_send()
    for kind in range(3):
        for turn in range(2):
            for step in range(n):
                pass_copy(kind, turn, peer(step)).wait_send()


def finish_kernel(z, names, *refs):
    r = Refs(names, refs)
    r.block[...] = r.block_out[...]
    r.embed[...] = r.embed_grad[...]
    r.bigram[...] = r.table_grads[:, : 2 * LANES].T[: z.table_width]
    r.trigram[...] = r.table_grads[:, LANES:].T[2 * LANES - z.table_width :]
    r.ngram[...] = r.sm_total[:, : z.pair_width]
    gains = r.sm_total[:, z.pair_width :]
    r.first[...] = gains[:, 0:1].T
    r.second[...] = gains[:, 1:2].T
    r.gate[...] = r.ga_out[...]
    r.up[...] = r.up_out[...]
    r.down[...] = r.dn_out[...]
    side = 3 * HD
    for h in range(z.heads):
        sums = getattr(r, f"at{h}_out")[...]
        r.attend[:, h * side : (h + 1) * side] = sums[:, :side]
        r.output[h * HD : (h + 1) * HD] = sums[:, LANES:].T[HD:]


def finish_outputs(z, got):
    kept = z.table_rows // SPLIT
    outs = dict(
        block=((z.rows, z.width), BF),
        embed=((z.rows, z.width), F32),
        bigram=((z.table_width, kept), F32),
        trigram=((z.table_width, kept), F32),
        ngram=((z.small, z.pair_width), F32),
        first=((1, z.small), F32),
        attend=((z.piece, 3 * HD * z.heads), F32),
        output=((HD * z.heads, z.piece), F32),
        second=((1, z.small), F32),
        gate=((z.piece, z.units), F32),
        up=((z.piece, z.units), F32),
        down=((z.piece, z.units), F32),
    )
    done = pl.pallas_call(
        functools.partial(finish_kernel, z, (*got, *outs)),
        out_shape=[jax.ShapeDtypeStruct(*item) for item in outs.values()],
        in_specs=[pl.BlockSpec(memory_space=pltpu.VMEM)] * len(got),
        out_specs=[pl.BlockSpec(memory_space=pltpu.VMEM)] * len(outs),
        name="finish",
    )(*got.values())
    done = dict(zip(outs, done, strict=True))
    for name in ("bigram", "trigram", "ngram", "down"):
        done[name] = done[name].T
    for name in ("first", "second"):
        done[name] = done[name].reshape(z.small)
    return tuple(done.values())


def shards(
    embedded,
    bigram_ids,
    trigram_ids,
    prefix_lens,
    bigram_table,
    trigram_table,
    ngram_weight,
    first_gain,
    attend_weight,
    output_weight,
    second_gain,
    gate_weight,
    up_weight,
    down_weight,
    cotangent,
):
    n = lax.axis_size("dp")
    rows, width = embedded.shape
    table_rows, table_width = bigram_table.shape
    heads, units = attend_weight.shape[1] // (3 * HD), gate_weight.shape[1]
    z = Sizes(n, rows, width, heads, units, table_rows, table_width)
    scratch, outs = scratch_of(z), outputs_of(z)
    names = (*INPUTS, *outs, *scratch)
    anywhere = pl.BlockSpec(memory_space=pl.ANY)
    in_specs = [anywhere] * len(INPUTS)
    in_specs[3] = pl.BlockSpec(memory_space=pltpu.SMEM)
    got = pl.pallas_call(
        functools.partial(block_kernel, z, names),
        out_shape=[jax.ShapeDtypeStruct(*item) for item in outs.values()],
        in_specs=in_specs,
        out_specs=[pl.BlockSpec(memory_space=pltpu.VMEM)] * len(outs),
        scratch_shapes=list(scratch.values()),
        compiler_params=pltpu.CompilerParams(
            collective_id=0, has_side_effects=True, vmem_limit_bytes=67043328
        ),
        name="block",
    )(
        embedded,
        bigram_ids.reshape(1, rows),
        trigram_ids.reshape(1, rows),
        prefix_lens,
        bigram_table.T,
        trigram_table.T,
        ngram_weight,
        first_gain,
        attend_weight.T,
        output_weight,
        second_gain,
        gate_weight,
        up_weight,
        down_weight,
        cotangent,
    )
    got = dict(zip(outs, got, strict=True))
    if not z.inside:

        def summed(part, axes):
            return lax.psum_scatter(part, axes, scatter_dimension=0, tiled=True)

        for name in ("ga", "up", "dn", *(f"at{h}" for h in range(heads))):
            got[f"{name}_out"] = summed(got.pop(f"{name}_part").astype(F32), "dp")
        got["sm_total"] = summed(got["sm_total"], ("dp", "tensor"))
    return finish_outputs(z, got)


def solution(mesh):
    placed = (
        P(("dp", "tensor"), None),
        P(("dp", "tensor")),
        P(("dp", "tensor")),
        P("dp"),
        P("dp", None),
        P("dp", None),
        P(),
        P(),
        P(None, "tensor"),
        P("tensor", None),
        P(),
        P(None, "tensor"),
        P(None, "tensor"),
        P("tensor", None),
        P("dp", None),
    )
    return jax.shard_map(
        shards,
        mesh=mesh,
        in_specs=placed,
        out_specs=(
            P(("dp", "tensor"), None),
            P(("dp", "tensor"), None),
            P(("dp", "tensor"), None),
            P(("dp", "tensor"), None),
            P(None, ("dp", "tensor")),
            P(("dp", "tensor")),
            P("dp", "tensor"),
            P("tensor", "dp"),
            P(("dp", "tensor")),
            P("dp", "tensor"),
            P("dp", "tensor"),
            P("tensor", "dp"),
        ),
        check_vma=False,
    )
```

```python
import functools
import math

import jax
import jax.numpy as jnp
from jax import lax
from jax.experimental import pallas as pl
from jax.experimental.pallas import tpu as pltpu
from jax.sharding import PartitionSpec as P

BF = jnp.bfloat16
F32 = jnp.float32
HD = 64
LANES = 128
PREFIX_MOST = 512
SPLIT = 4
CHUNKS = 4

INPUTS = (
    "embedded", "bigram_ids", "trigram_ids", "prefix", "bigram_table", "trigram_table",
    "ngram_weight", "first_gain", "attend_weight", "output_weight", "second_gain",
    "gate_weight", "up_weight", "down_weight", "cotangent",
)


class Refs:
    def __init__(self, names, refs):
        self.__dict__.update(zip(names, refs, strict=True))


def dot(left, right):
    return jnp.dot(left, right, preferred_element_type=F32)


def dot_right(left, right):
    return lax.dot_general(left, right, (((1,), (1,)), ((), ())), preferred_element_type=F32)


def lane_of(shape):
    return lax.broadcasted_iota(jnp.int32, shape, len(shape) - 1)


def row_of(shape):
    return lax.broadcasted_iota(jnp.int32, shape, 0)


def onehot(test):
    return jnp.where(test, 1.0, 0.0).astype(BF)


def roll64(block):
    return pltpu.roll(block, 64, 1)


def swap_halves(block):
    return jnp.where(lane_of(block.shape) < 32, pltpu.roll(block, 96, 1), pltpu.roll(block, 32, 1))


class Sizes:
    def __init__(self, n, rows, width, heads, units, table_rows, table_width):
        self.n, self.rows, self.width, self.heads, self.units = n, rows, width, heads, units
        self.table_rows, self.table_width = table_rows, table_width
        self.length = rows * SPLIT
        self.keys = [max((i + 1) * rows, min(PREFIX_MOST, rows * SPLIT)) for i in range(SPLIT)]
        self.cap = max(16, 2 * rows // n)
        self.slots = n * self.cap
        self.padded = heads * LANES
        self.chunk = rows // CHUNKS
        self.piece = width // n
        self.pair_width = 2 * table_width
        self.small = width // (n * SPLIT)
        self.small_lanes = self.pair_width + LANES
        self.attn_lanes = 4 * HD
        self.inside = n == 8 and self.piece % 16 == 0 and self.small % 8 == 0


def make_copy(src, dst, send, recv, **where):
    return pltpu.make_async_remote_copy(
        src_ref=src, dst_ref=dst, send_sem=send, recv_sem=recv, device_id=where
    )


class Gather:
    def __init__(self, z, pos, full, sems):
        self.z, self.pos, self.full, self.sems = z, pos, full, sems

    def piece(self, block, c):
        start = pl.multiple_of(block * self.z.rows + c * self.z.chunk, self.z.chunk)
        return self.full.at[pl.ds(start, self.z.chunk)]

    def copy(self, kind, c, incoming=False):
        p = self.pos
        block = ((p.t, p.t1), (p.t, p.t2), (p.t2, p.t3))[kind][1 if incoming else 0]
        ref = self.piece(block, c)
        target = p.t2 if kind == 1 else p.t1
        return make_copy(
            ref, ref, self.sems.at[c, 2 * kind], self.sems.at[c, 2 * kind + 1], tensor=target
        )

    def send(self, c):
        self.copy(1, c).start()
        self.copy(0, c).start()

    def receive(self, c):
        self.copy(1, c, True).wait_recv()
        self.copy(2, c).start()
        self.copy(0, c, True).wait_recv()
        self.copy(2, c, True).wait_recv()

    def close(self):
        def body(c, carry):
            for kind in range(3):
                self.copy(kind, c).wait_send()
            return carry

        lax.fori_loop(0, CHUNKS, body, 0)


class Scatter:
    def __init__(self, z, pos, part, near, out, far, sems):
        self.z, self.pos, self.part, self.near = z, pos, part, near
        self.out, self.far, self.sems = out, far, sems

    def span(self, c):
        return pl.ds(pl.multiple_of(c * self.z.chunk, self.z.chunk), self.z.chunk)

    def rows(self, block, c):
        start = pl.multiple_of(block * self.z.rows + c * self.z.chunk, self.z.chunk)
        return pl.ds(start, self.z.chunk)

    def near_copy(self, slot, c):
        block = self.pos.t1 + slot * (self.pos.t3 - self.pos.t1)
        return make_copy(
            self.part.at[self.rows(block, c)],
            self.near.at[slot, self.span(c)],
            self.sems.at[c, 2 * slot],
            self.sems.at[c, 2 * slot + 1],
            tensor=self.pos.t1,
        )

    def far_copy(self, c):
        return make_copy(
            self.out.at[self.span(c)],
            self.far.at[self.span(c)],
            self.sems.at[c, 4],
            self.sems.at[c, 5],
            tensor=self.pos.t2,
        )

    def send(self, c):
        self.near_copy(1, c).start()
        self.near_copy(0, c).start()

    def middle(self, c):
        self.near_copy(1, c).wait_recv()
        own = self.part[self.rows(self.pos.t2, c)].astype(F32)
        self.out[self.span(c)] = (own + self.near[1, self.span(c)].astype(F32)).astype(BF)
        self.far_copy(c).start()

    def finish(self, c):
        self.near_copy(0, c).wait_recv()
        self.far_copy(c).wait_recv()
        own = self.part[self.rows(self.pos.t, c)].astype(F32)
        own = own + self.near[0, self.span(c)].astype(F32)
        return own + self.far[self.span(c)].astype(F32)

    def close(self):
        def body(c, carry):
            self.near_copy(0, c).wait_send()
            self.near_copy(1, c).wait_send()
            self.far_copy(c).wait_send()
            return carry

        lax.fori_loop(0, CHUNKS, body, 0)


class Spread:
    STEPS = 4

    def __init__(self, z, pos, axes, part, pair_in, next_out, next_in, out, sems):
        self.z, self.pos, self.part, self.pair_in = z, pos, part, pair_in
        self.next_out, self.next_in, self.out, self.sems = next_out, next_in, out, sems
        self.axes = axes
        self.order = (axes[1:], axes[1:2], axes[2:], ())

    def across(self, axes):
        place, parity = self.pos.place, self.pos.parity
        if "near" in axes:
            place = place + 1 - 2 * lax.rem(place, 2)
        if "far" in axes:
            place = lax.rem(place + 2, 4)
        if "x" in axes:
            parity = 1 - parity
        return 2 * place + parity

    def rows(self, peer):
        return pl.ds(pl.multiple_of(peer * self.z.piece, self.z.piece), self.z.piece)

    def pair_copy(self, step):
        return make_copy(
            self.part.at[self.rows(self.across(self.axes[:1] + self.order[step]))],
            self.pair_in.at[step],
            self.sems.at[0, step],
            self.sems.at[1, step],
            dp=self.across(self.axes[:1]),
        )

    def next_copy(self, step):
        return make_copy(
            self.next_out.at[step],
            self.next_in.at[step],
            self.sems.at[2, step],
            self.sems.at[3, step],
            dp=self.across(self.axes[1:2] if step < 2 else self.axes[2:]),
        )

    def send(self):
        for step in range(4):
            self.pair_copy(step).start()

    def middle(self, step):
        self.pair_copy(step).wait_recv()
        own = self.part[self.rows(self.across(self.order[step]))].astype(F32)
        total = own + self.pair_in[step].astype(F32)
        if step >= 2:
            self.next_copy(step - 2).wait_recv()
            total = total + self.next_in[step - 2].astype(F32)
        if step == 3:
            self.out[...] = total
        else:
            self.next_out[step] = total.astype(BF)
            self.next_copy(step).start()

    def finish(self):
        self.next_copy(2).wait_recv()
        self.out[...] += self.next_in[2].astype(F32)

    def close(self):
        for step in range(4):
            self.pair_copy(step).wait_send()
            if step < 3:
                self.next_copy(step).wait_send()


class Position:
    def __init__(self, z):
        self.d, self.t = lax.axis_index("dp"), lax.axis_index("tensor")
        core, side = lax.rem(self.t, 2), self.t // 2
        self.t1 = self.t + 1 - 2 * core
        self.t2 = self.t + 2 - 4 * side
        self.t3 = self.t1 + 2 - 4 * side
        self.parity, self.place = lax.rem(self.d, 2), self.d // 2


def scratch_of(z):
    n, rows, width, length, chunks = z.n, z.rows, z.width, z.length, CHUNKS
    vmem, dma = pltpu.VMEM, pltpu.SemaphoreType.DMA
    shapes = dict(
        emb=vmem((rows, width), BF),
        ids=vmem((2 * n, 1, rows), jnp.int32),
        own_ids=vmem((2, 1, rows), jnp.int32),
        pick=vmem((2, rows, z.slots), BF),
        table_b=vmem((z.table_width, z.table_rows), BF),
        table_t=vmem((z.table_width, z.table_rows), BF),
        nw=vmem((z.pair_width, width), BF),
        gain1=vmem((width,), F32),
        gain2=vmem((width,), F32),
        wap=vmem((3 * z.padded, width), BF),
        wop=vmem((z.padded, width), BF),
        wgu=vmem((width, 2 * z.units), BF),
        wd=vmem((z.units, width), BF),
        cot=vmem((length, width), BF),
        cosine=vmem((length, LANES), F32),
        sines=vmem((length, LANES), F32),
        pick_t=vmem((2, z.slots, rows), BF),
        lids=vmem((SPLIT, 2, 8, z.slots), jnp.int32),
        rows_out=vmem((z.slots, z.pair_width), BF),
        rows_in=vmem((z.slots, z.pair_width), BF),
        grams=vmem((rows, z.pair_width), BF),
        inputs=vmem((rows, width), F32),
        after=vmem((rows, width), F32),
        aftergrad=vmem((rows, width), F32),
        inverse=vmem((length, LANES), F32),
        scale1=vmem((rows, LANES), F32),
        scale2=vmem((rows, LANES), F32),
        n1=vmem((length, width), BF),
        n2=vmem((length, width), BF),
        ab=vmem((length, width), BF),
        q=vmem((length, z.padded), BF),
        k=vmem((length, z.padded), BF),
        v=vmem((length, z.padded), BF),
        probs0=vmem((z.heads, rows, z.keys[0]), BF),
        probs1=vmem((z.heads, rows, z.keys[1]), BF),
        probs2=vmem((z.heads, rows, z.keys[2]), BF),
        probs3=vmem((z.heads, rows, z.keys[3]), BF),
        att=vmem((length, z.padded), BF),
        do=vmem((length, z.padded), BF),
        dk=vmem((HD, length), F32),
        dv=vmem((HD, length), F32),
        mixb=vmem((length, 3 * z.padded), BF),
        act=vmem((length, z.units), BF),
        gub=vmem((max(length, width), 2 * z.units), BF),
        lifted=vmem((rows, width), BF),
        sums=vmem((2, 8, width), F32),
        back_out=vmem((z.slots, z.pair_width), BF),
        back_in=vmem((SPLIT * z.slots, z.pair_width), BF),
        in_sem=dma((12 + 4 * z.heads,)),
        id_sem=dma((2,)),
        row_sem=dma((2, n)),
        lid_sem=dma((2, 3)),
        back_sem=dma((2, 2 * n)),
        pass_sem=dma((6, 2 * n)),
        ag1_sem=dma((chunks, 6)),
        ag2_sem=dma((chunks, 6)),
        ag3_sem=dma((chunks, 6)),
    )
    for k in range(1, 4):
        shapes[f"part{k}"] = vmem((length, width), BF)
        shapes[f"near{k}"] = vmem((2, rows, width), BF)
        shapes[f"send{k}"] = vmem((rows, width), BF)
        shapes[f"far{k}"] = vmem((rows, width), BF)
        shapes[f"rs{k}_sem"] = dma((chunks, 6))
    shapes["rs4_sem"] = dma((chunks, 6))
    if z.inside:
        heads = [(f"at{h}", z.attn_lanes) for h in range(z.heads)]
        for name, lanes in (("ga", z.units), ("up", z.units), ("dn", z.units), *heads):
            shapes[f"{name}_part"] = vmem((width, lanes), BF)
            shapes[f"{name}_pair_in"] = vmem((4, z.piece, lanes), BF)
            shapes[f"{name}_next_out"] = vmem((3, z.piece, lanes), BF)
            shapes[f"{name}_next_in"] = vmem((3, z.piece, lanes), BF)
            shapes[f"{name}_sem"] = dma((4, 4))
        small = (n, z.small, z.small_lanes)
        shapes["sm_part"] = vmem((SPLIT, *small), BF)
        shapes["sm_near"] = vmem((2, *small), BF)
        shapes["sm_send"] = vmem(small, BF)
        shapes["sm_far"] = vmem(small, BF)
        shapes["sm_out"] = vmem(small, BF)
        shapes["sm_in"] = vmem(small, BF)
        shapes["sm_sem"] = dma((6,))
        shapes["sp_sem"] = dma((2, n))
    return shapes


def outputs_of(z):
    n, rows, width = z.n, z.rows, z.width
    shapes = dict(
        block_out=((rows, width), BF),
        embed_grad=((rows, width), F32),
        table_grads=((z.table_rows // SPLIT, z.pair_width), F32),
    )
    if z.inside:
        shapes["ga_out"] = ((z.piece, z.units), F32)
        shapes["up_out"] = ((z.piece, z.units), F32)
        shapes["dn_out"] = ((z.piece, z.units), F32)
        for h in range(z.heads):
            shapes[f"at{h}_out"] = ((z.piece, z.attn_lanes), F32)
        shapes["sm_total"] = ((z.small, z.small_lanes), F32)
    else:
        shapes["ga_part"] = ((width, z.units), BF)
        shapes["up_part"] = ((width, z.units), BF)
        shapes["dn_part"] = ((width, z.units), BF)
        for h in range(z.heads):
            shapes[f"at{h}_part"] = ((width, z.attn_lanes), BF)
        shapes["sm_total"] = ((width, z.small_lanes), F32)
    return shapes


def block_kernel(z, names, *refs):
    r = Refs(names, refs)
    p = Position(z)
    n, rows, width, length = z.n, z.rows, z.width, z.length
    cap, slots, units, padded, heads = z.cap, z.slots, z.units, z.padded, z.heads
    gather1 = Gather(z, p, r.n1, r.ag1_sem)
    gather2 = Gather(z, p, r.n2, r.ag2_sem)
    gather3 = Gather(z, p, r.ab, r.ag3_sem)
    scatters = [
        Scatter(
            z, p, getattr(r, f"part{k}"), getattr(r, f"near{k}"), getattr(r, f"send{k}"),
            getattr(r, f"far{k}"), sems,
        )
        for k, sems in ((1, r.rs1_sem), (2, r.rs2_sem), (3, r.rs3_sem), (1, r.rs4_sem))
    ]
    scatter1, scatter2, scatter3, scatter4 = scatters
    spreads = {}
    if z.inside:
        for name in ("ga", "up", "dn", *(f"at{h}" for h in range(heads))):
            axes = ("near", "far", "x") if name == "ga" else ("x", "near", "far")
            spreads[name] = Spread(
                z, p, axes, getattr(r, f"{name}_part"), getattr(r, f"{name}_pair_in"),
                getattr(r, f"{name}_next_out"), getattr(r, f"{name}_next_in"),
                getattr(r, f"{name}_out"), getattr(r, f"{name}_sem"),
            )

    def peer(step):
        return lax.rem(p.d + step, n)

    barrier = pltpu.get_barrier_semaphore()
    for step in range(1, n):
        pl.semaphore_signal(barrier, inc=1, device_id={"dp": peer(step)})
    for target in (p.t1, p.t2, p.t3):
        pl.semaphore_signal(barrier, inc=1, device_id={"tensor": target})

    loads = [
        (r.bigram_ids, r.own_ids.at[0]),
        (r.trigram_ids, r.own_ids.at[1]),
        (r.bigram_table, r.table_b),
        (r.trigram_table, r.table_t),
        (r.embedded, r.emb),
        (r.ngram_weight, r.nw),
        (r.first_gain, r.gain1),
        (r.second_gain, r.gain2),
        (r.gate_weight, r.wgu.at[:, pl.ds(0, units)]),
        (r.up_weight, r.wgu.at[:, pl.ds(units, units)]),
        (r.down_weight, r.wd),
        (r.cotangent, r.cot),
    ]
    for h in range(heads):
        for c in range(3):
            src = r.attend_weight.at[pl.ds((3 * h + c) * HD, HD)]
            loads.append((src, r.wap.at[pl.ds(c * padded + h * LANES, HD)]))
        src = r.output_weight.at[pl.ds(h * HD, HD)]
        loads.append((src, r.wop.at[pl.ds(h * LANES, HD)]))
    loads = [pltpu.make_async_copy(src, dst, r.in_sem.at[i]) for i, (src, dst) in enumerate(loads)]
    for load in loads[:4]:
        load.start()

    pl.semaphore_wait(barrier, n - 1 + 3)

    def id_copy(step, k):
        return make_copy(
            (r.bigram_ids, r.trigram_ids)[k],
            r.ids.at[k * n + p.d],
            r.id_sem.at[0],
            r.id_sem.at[1],
            dp=peer(step),
        )

    for step in range(1, n):
        for k in range(2):
            id_copy(step, k).start()
    for load in loads[4:]:
        load.start()

    lane = lane_of((32, LANES))
    low = jnp.where(lane < 32, lane, lane - 32)
    frequency = jnp.exp(low.astype(F32) * (-2.0 * math.log(10000.0) / HD))
    place = row_of((32, LANES)).astype(F32)
    coarse, fine = place * 32.0 * frequency, place * frequency
    cos_coarse, sin_coarse = jnp.cos(coarse), jnp.sin(coarse)
    used = lane < HD
    cos_fine = jnp.where(used, jnp.cos(fine), 0.0)
    sin_fine = jnp.where(used, jnp.sin(fine), 0.0)
    sign = jnp.where(lane < 32, -1.0, 1.0)
    for a in range(length // 32):
        ca, sa = cos_coarse[a : a + 1], sin_coarse[a : a + 1]
        r.cosine[a * 32 : (a + 1) * 32] = ca * cos_fine - sa * sin_fine
        r.sines[a * 32 : (a + 1) * 32] = sign * (sa * cos_fine + ca * sin_fine)

    loads[0].wait()
    loads[1].wait()
    earlier = onehot(row_of((rows, rows)) < lane_of((rows, rows)))
    later = onehot(row_of((rows, rows)) > lane_of((rows, rows)))
    lane = lane_of((rows, LANES))
    start, half_cap = (lane * z.table_rows).astype(F32), cap // 2
    for k in range(2):
        r.ids[k * n + p.d] = r.own_ids[k]
        column = jnp.broadcast_to(r.own_ids[k].astype(F32), (LANES, rows)).T
        held = (column >= start) & (column < start + z.table_rows)
        ranks = dot(later, onehot(held))
        slot = jnp.where(held, ranks + (lane * cap).astype(F32), 0.0)
        slot = jnp.sum(slot, axis=1, keepdims=True)
        r.pick[k] = onehot(slot.astype(jnp.int32) == lane_of((rows, slots)))
        second = jnp.where(ranks >= half_cap, float((n - 1) * half_cap), 0.0)
        slot = jnp.where(held, ranks + (lane * half_cap).astype(F32) + second, 0.0)
        slot = jnp.sum(slot, axis=1, keepdims=True)
        across = jnp.broadcast_to(slot, (rows, LANES)).T[0:1]
        r.pick_t[k] = onehot(across.astype(jnp.int32) == row_of((slots, rows)))

    for h in range(heads):
        empty = jnp.zeros((LANES - HD, width), BF)
        for c in range(3):
            at = c * padded + h * LANES + HD
            r.wap[at : at + LANES - HD] = empty
        r.wop[h * LANES + HD : (h + 1) * LANES] = empty

    loads[2].wait()
    loads[3].wait()
    all_ids = r.ids.at[pl.ds(0, 2 * (n - 1))]
    all_ids = make_copy(all_ids, all_ids, r.id_sem.at[0], r.id_sem.at[1], dp=peer(1))
    all_ids.wait_recv()
    asked = jnp.concatenate([r.ids[i] for i in range(2 * n)], axis=0)
    first_row = p.d * z.table_rows
    mine = (asked >= first_row) & (asked < first_row + z.table_rows)
    ranks = dot(onehot(mine), earlier)
    tags = jnp.where(mine, ranks, -1.0).astype(jnp.int32)
    local = jnp.where(mine, asked - first_row + 1, 0).astype(F32)
    picked = []
    for k in range(2):
        columns = []
        for i in range(n):
            at = k * n + i
            hit = tags[at : at + 1] == row_of((cap, rows))
            value = jnp.where(hit, local[at : at + 1], 0.0)
            columns.append(jnp.sum(value, axis=1, keepdims=True) - 1.0)
        picked.append(jnp.concatenate(columns, axis=0).astype(jnp.int32))
        columns = [item[:half_cap] for item in columns] + [item[half_cap:] for item in columns]
        column = jnp.concatenate(columns, axis=0)
        across = jnp.broadcast_to(column, (slots, LANES)).T[0:8]
        r.lids[p.t, k] = across.astype(jnp.int32)
    half = slots // 2

    def row_copy(step):
        to = peer(step)
        return make_copy(
            r.rows_out.at[pl.ds(pl.multiple_of(to * cap, cap), cap)],
            r.rows_in.at[pl.ds(pl.multiple_of(p.d * cap, cap), cap)],
            r.row_sem.at[0, 0],
            r.row_sem.at[1, p.d],
            dp=to,
        )

    def row_arrival(step):
        of = peer(step)
        ref = r.rows_in.at[pl.ds(pl.multiple_of(of * cap, cap), cap)]
        return make_copy(ref, ref, r.row_sem.at[0, 0], r.row_sem.at[1, of], dp=of)

    for part in range(2):
        found = []
        for k, table in enumerate((r.table_b, r.table_t)):
            chosen = picked[k][part * half : (part + 1) * half]
            hits = onehot(chosen == lane_of((half, z.table_rows)))
            both = dot_right(hits, table[...])
            fill = jnp.zeros((half, 2 * LANES - z.table_width), F32)
            found.append((both[:, :LANES], jnp.concatenate([both[:, LANES:], fill], axis=1)))
        low_half = lane_of((half, LANES)) < HD
        rolled = [roll64(block) for block in found[1]]
        span = slice(part * half, (part + 1) * half)
        r.rows_out[span, 0:LANES] = found[0][0].astype(BF)
        middle = jnp.where(low_half, found[0][1], rolled[0])
        r.rows_out[span, LANES : 2 * LANES] = middle.astype(BF)
        r.rows_out[span, 2 * LANES :] = jnp.where(low_half, rolled[0], rolled[1]).astype(BF)
    for step in range(1, n):
        row_copy(n - step).start()
    own_slots = pl.ds(pl.multiple_of(p.d * cap, cap), cap)
    r.rows_in[own_slots] = r.rows_out[own_slots]

    for load in loads[4:8]:
        load.wait()
    for step in range(1, n):
        row_arrival(step).wait_recv()
    fetched = r.rows_in[...]
    low_table = lane_of((rows, z.pair_width)) < z.table_width
    grams = jnp.where(low_table, dot(r.pick[0], fetched), dot(r.pick[1], fetched)).astype(BF)
    r.grams[...] = grams
    inputs = r.emb[...].astype(F32) + dot(grams, r.nw[...])
    r.inputs[...] = inputs
    scale = lax.rsqrt(jnp.mean(inputs * inputs, axis=1, keepdims=True) + 1e-05)
    r.scale1[...] = jnp.broadcast_to(scale, (rows, LANES))
    own_rows = pl.ds(pl.multiple_of(p.t * rows, rows), rows)
    r.n1[own_rows] = (inputs * scale * r.gain1[...][None, :]).astype(BF)
    for c in range(CHUNKS):
        gather1.send(c)

    def lid_copy(i, incoming=False):
        target = (p.t1, p.t2, p.t3)[i]
        ref = r.lids.at[target if incoming else p.t]
        return make_copy(ref, ref, r.lid_sem.at[0, i], r.lid_sem.at[1, i], tensor=target)

    for i in range(3):
        lid_copy(i).start()

    def spans(c):
        return [
            pl.ds(pl.multiple_of(b * rows + c * z.chunk, z.chunk), z.chunk) for b in range(SPLIT)
        ]

    def take(ref, c, *rest):
        return jnp.concatenate([ref[(span, *rest)] for span in spans(c)], axis=0)

    def put(ref, c, value, *rest):
        for b, span in enumerate(spans(c)):
            ref[(span, *rest)] = value[b * z.chunk : (b + 1) * z.chunk]

    for load in loads[8:]:
        load.wait()

    def project(c, carry):
        gather1.receive(c)
        mixture = dot_right(take(r.n1, c), r.wap[...])
        cosine, sines = take(r.cosine, c), take(r.sines, c)
        for h in range(heads):
            for i, ref in enumerate((r.q, r.k)):
                at = i * padded + h * LANES
                block = mixture[:, at : at + LANES]
                turned = block * cosine + swap_halves(block) * sines
                if i == 0:
                    turned = turned * (HD**-0.5 * math.log2(math.e))
                put(ref, c, turned.astype(BF), slice(h * LANES, (h + 1) * LANES))
            at = 2 * padded + h * LANES
            block = mixture[:, at : at + LANES]
            block = jnp.where(lane_of(block.shape) == HD, 1.0, block)
            put(r.v, c, block.astype(BF), slice(h * LANES, (h + 1) * LANES))
        return carry

    lax.fori_loop(0, CHUNKS, project, 0)

    prefix = r.prefix[0]
    probs = (r.probs0, r.probs1, r.probs2, r.probs3)
    blocks = [(i * rows, z.keys[i], probs[i]) for i in range(SPLIT)]

    def attend(first, keys, kept):
        span = slice(first, first + rows)
        lane = lane_of((rows, LANES))
        row, column = row_of((rows, rows)), lane_of((rows, rows))

        def score_tiles(h):
            at = slice(h * LANES, (h + 1) * LANES)
            tiles = []
            for start in range(0, keys, rows):
                scores = dot_right(r.q[span, at], r.k[start : start + rows, at])
                allowed = None
                if start == first:
                    allowed = column <= row
                if start + rows > first + 1 and start < PREFIX_MOST:
                    in_prefix = column < prefix - start
                    allowed = in_prefix if allowed is None else allowed | in_prefix
                if allowed is not None:
                    scores = jnp.where(allowed, scores, -1000000000.0)
                tiles.append(scores)
            return tiles

        inverses = jnp.zeros((rows, LANES), F32)
        every = [score_tiles(h) for h in range(heads)]
        tops = [jnp.max(functools.reduce(jnp.maximum, tiles), axis=1, keepdims=True) for tiles in every]
        totals = []
        for h in range(heads):
            at = slice(h * LANES, (h + 1) * LANES)
            total = jnp.zeros((rows, LANES), F32)
            for j, scores in enumerate(every[h]):
                weights = jnp.exp2(scores - tops[h]).astype(BF)
                kept[h, :, j * rows : (j + 1) * rows] = weights
                total = total + dot(weights, r.v[j * rows : (j + 1) * rows, at])
            totals.append(total)
        for h, total in enumerate(totals):
            at = slice(h * LANES, (h + 1) * LANES)
            inverse = 1.0 / total[:, HD : HD + 1]
            r.att[span, at] = jnp.where(lane < HD, total * inverse, 0.0).astype(BF)
            inverses = jnp.where(lane == h, inverse, inverses)
        r.inverse[span] = inverses
        r.part1[span] = dot(r.att[span], r.wop[...]).astype(BF)

    def attend_step(step, carry):
        core, side = lax.rem(p.t, 2), p.t // 2
        side = side + (1 - step // 2) * (1 - 2 * side)
        core = core + (1 - lax.rem(step, 2)) * (1 - 2 * core)
        wanted = 2 * side + core
        for i, block in enumerate(blocks):

            @pl.when(wanted == i)
            def _(block=block):
                attend(*block)

        @pl.when(lax.rem(step, 2) == 0)
        def _():
            for c in range(CHUNKS):
                scatter1.near_copy(1 - step // 2, c).start()

        @pl.when(step == 1)
        def _():
            for c in range(CHUNKS):
                scatter1.middle(c)

        return carry

    lax.fori_loop(0, SPLIT, attend_step, 0)

    waiting = []

    def spread(name):
        if z.inside:
            spreads[name].send()
            waiting.extend((name, step) for step in range(Spread.STEPS))

    def pair_sums(count):
        for name, step in waiting[:count]:
            spreads[name].middle(step)
        del waiting[:count]

    def second_norm(c, carry):
        span = scatter1.span(c)
        after = r.inputs[span] + scatter1.finish(c)
        r.after[span] = after
        scale = lax.rsqrt(jnp.mean(after * after, axis=1, keepdims=True) + 1e-05)
        r.scale2[span] = jnp.broadcast_to(scale, (z.chunk, LANES))
        own = scatter1.rows(p.t, c)
        r.n2[own] = (after * scale * r.gain2[...][None, :]).astype(BF)
        gather2.send(c)
        return carry

    lax.fori_loop(0, CHUNKS, second_norm, 0)

    def feed_forward(c, carry):
        gather2.receive(c)
        both = dot(take(r.n2, c), r.wgu[...])
        act_back = dot_right(take(r.cot, c), r.wd[...])
        gate, up = both[:, :units], both[:, units:]
        s = 1.0 / (1.0 + jnp.exp(-gate))
        silu = gate * s
        put(r.act, c, (silu * up).astype(BF))
        gate_back = (act_back * up * s * (1.0 + gate * (1.0 - s))).astype(BF)
        up_back = (act_back * silu).astype(BF)
        put(r.gub, c, gate_back, slice(0, units))
        put(r.gub, c, up_back, slice(units, 2 * units))
        back = dot_right(gate_back, r.wgu[:, 0:units]) + dot_right(up_back, r.wgu[:, units:])
        put(r.part3, c, back.astype(BF))
        scatter3.send(c)

        @pl.when(c > 0)
        def _():
            scatter3.middle(c - 1)

        return carry

    lax.fori_loop(0, CHUNKS, feed_forward, 0)
    scatter3.middle(CHUNKS - 1)

    tile = 2 * LANES

    def gate_up_tile(j, carry):
        at = pl.ds(pl.multiple_of(j * tile, tile), tile)
        both = dot(r.n2[:, at].T, r.gub[0:length]).astype(BF)
        r.ga_part[at] = both[:, :units]
        r.up_part[at] = both[:, units:]
        return carry

    lax.fori_loop(0, width // tile, gate_up_tile, 0)
    if z.inside:
        spreads["ga"].send()
        spreads["up"].send()
        waiting.extend((name, step) for step in range(Spread.STEPS) for name in ("ga", "up"))

    r.sums[...] = jnp.zeros_like(r.sums)

    def norm_back(grad, values, scale, gain):
        scaled = grad * gain
        mean = jnp.mean(scaled * values, axis=1, keepdims=True)
        total = jnp.sum(grad * values * scale, axis=0, keepdims=True)
        return scale * scaled - values * (scale * scale * scale * mean), total

    def second_back(c, carry):
        span = scatter3.span(c)
        grad = scatter3.finish(c)
        row_grad, total = norm_back(grad, r.after[span], r.scale2[span, 0:1], r.gain2[...][None, :])
        r.sums[1, 0:1] += total
        own = scatter3.rows(p.t, c)
        after_grad = r.cot[own].astype(F32) + row_grad
        r.aftergrad[span] = after_grad
        r.ab[own] = after_grad.astype(BF)
        gather3.send(c)
        return carry

    lax.fori_loop(0, CHUNKS, second_back, 0)


    def branch_two(c, carry):
        put(r.part2, c, dot(take(r.act, c), r.wd[...]).astype(BF))
        scatter2.send(c)
        return carry

    lax.fori_loop(0, CHUNKS, branch_two, 0)
    for c in range(CHUNKS):
        scatter2.middle(c)

    def down_tile(j, carry):
        at = pl.ds(pl.multiple_of(j * tile, tile), tile)
        r.dn_part[at] = dot(r.cot[:, at].T, r.act[...]).astype(BF)
        return carry

    lax.fori_loop(0, width // tile, down_tile, 0)
    spread("dn")
    pair_sums(4)

    n1_turned, ab_turned = r.gub.at[0:width], r.wgu

    def turned_tokens(j, carry):
        at = pl.ds(pl.multiple_of(j * tile, tile), tile)
        n1_turned[at] = r.n1[:, at].T
        return carry

    lax.fori_loop(0, width // tile, turned_tokens, 0)

    def attended_back(c, carry):
        gather3.receive(c)
        back = dot_right(take(r.ab, c), r.wop[...])
        inverse = take(r.inverse, c)
        for h in range(heads):
            at = slice(h * LANES, (h + 1) * LANES)
            put(r.do, c, (back[:, at] * inverse[:, h : h + 1]).astype(BF), at)
        return carry

    lax.fori_loop(0, CHUNKS, attended_back, 0)

    def unrotate(grads, span):
        grads = grads.astype(BF).astype(F32)
        turned = grads * r.cosine[span] - swap_halves(grads) * r.sines[span]
        return turned.astype(BF)

    def upright(block):
        return jnp.concatenate([block, jnp.zeros_like(block)], axis=0).T

    def attend_back(h, first, keys, kept, whole):
        span, at = slice(first, first + rows), slice(h * LANES, (h + 1) * LANES)
        do, q = r.do[span, at], r.q[span, at]
        weights = kept[h]
        prob_back = dot_right(do, r.v[0:keys, at])
        centre = jnp.sum(do.astype(F32) * r.att[span, at].astype(F32), axis=1, keepdims=True)
        score_back = (weights.astype(F32) * (prob_back - centre)).astype(BF)
        query_back = dot(score_back, r.k[0:keys, at]) * HD**-0.5
        r.mixb[span, at] = unrotate(query_back, span)
        key_back, value_back = dot(q.T[:HD], score_back), dot(do.T[:HD], weights)
        if whole:
            r.dk[...] = key_back
            r.dv[...] = value_back
        else:
            r.dk[:, 0:keys] += key_back
            r.dv[:, 0:keys] += value_back

    def turned_grads(j, carry):
        at = pl.ds(pl.multiple_of(j * tile, tile), tile)
        ab_turned[at] = r.ab[:, at].T
        return carry

    lax.fori_loop(0, width // tile, turned_grads, 0)

    def head_tiles(h):
        part = getattr(r, f"at{h}_part")
        lanes = [slice(c * padded + h * LANES, c * padded + (h + 1) * LANES) for c in range(3)]

        mixed = jnp.concatenate([r.mixb[:, span] for span in lanes], axis=1)
        grad = dot(n1_turned[...], mixed)
        outer = dot(ab_turned[...], r.att[:, h * LANES : (h + 1) * LANES])
        first = grad[:, :LANES] + roll64(grad[:, LANES : 2 * LANES])
        second = grad[:, 2 * LANES :] + roll64(outer)
        part[:, 0:LANES] = first.astype(BF)
        part[:, LANES:] = second.astype(BF)

    for h in range(heads):
        for i in reversed(range(SPLIT)):
            first, keys, kept = blocks[i]
            attend_back(h, first, keys, kept, i == SPLIT - 1)
        for i in range(SPLIT):
            span = slice(i * rows, (i + 1) * rows)
            at = padded + h * LANES
            key_back = upright(r.dk[:, span]) * math.log(2.0)
            r.mixb[span, at : at + LANES] = unrotate(key_back, span)
            at = 2 * padded + h * LANES
            r.mixb[span, at : at + LANES] = upright(r.dv[:, span]).astype(BF)
        if h < heads - 1:
            head_tiles(h)
            spread(f"at{h}")
            pair_sums((4, 2)[h])
    scatter1.close()

    def first_norm_part(c, carry):
        put(r.part1, c, dot(take(r.mixb, c), r.wap[...]).astype(BF))
        scatter4.send(c)

        @pl.when(c > 0)
        def _():
            scatter4.middle(c - 1)

        return carry

    lax.fori_loop(0, CHUNKS, first_norm_part, 0)
    scatter4.middle(CHUNKS - 1)
    pair_sums(3)
    head_tiles(heads - 1)
    spread(f"at{heads - 1}")
    pair_sums(5)

    def block_out(c, carry):
        span = scatter2.span(c)
        r.block_out[span] = (r.after[span] + scatter2.finish(c)).astype(BF)
        return carry

    lax.fori_loop(0, CHUNKS, block_out, 0)

    def first_back(c, carry):
        span = scatter4.span(c)
        grad = scatter4.finish(c)
        row_grad, total = norm_back(grad, r.inputs[span], r.scale1[span, 0:1], r.gain1[...][None, :])
        r.sums[0, 0:1] += total
        embed_grad = r.aftergrad[span] + row_grad
        r.embed_grad[span] = embed_grad
        r.lifted[span] = embed_grad.astype(BF)
        return carry

    lax.fori_loop(0, CHUNKS, first_back, 0)

    row_back = dot_right(r.lifted[...], r.nw[...]).astype(BF)
    low_table = lane_of((slots, z.pair_width)) < z.table_width
    outgoing = jnp.where(low_table, dot(r.pick_t[0], row_back), dot(r.pick_t[1], row_back))
    r.back_out[...] = outgoing.astype(BF)

    def slots_of(block, turn, of):
        start = block * slots + (turn * n + of) * half_cap
        return pl.ds(pl.multiple_of(start, half_cap), half_cap)

    def back_copy(step, turn, incoming=False):
        to = peer(step)
        of = to if incoming else p.d
        return make_copy(
            r.back_out.at[slots_of(0, turn, to)],
            r.back_in.at[slots_of(p.t, turn, of)],
            r.back_sem.at[0, 0],
            r.back_sem.at[1, turn * n + of],
            dp=to,
        )

    def pass_copy(kind, turn, of, incoming=False):
        block = ((p.t, p.t1), (p.t, p.t2), (p.t2, p.t3))[kind][1 if incoming else 0]
        ref = r.back_in.at[slots_of(block, turn, of)]
        at = turn * n + of
        target = p.t2 if kind == 1 else p.t1
        return make_copy(
            ref, ref, r.pass_sem.at[2 * kind, at], r.pass_sem.at[2 * kind + 1, at], tensor=target
        )

    for turn in range(2):
        for step in range(1, n):
            back_copy(n - step, turn).start()
    for turn in range(2):
        r.back_in[slots_of(p.t, turn, p.d)] = r.back_out[slots_of(0, turn, p.d)]

    gains = jnp.concatenate(
        [r.sums[0, 0:1], r.sums[1, 0:1], jnp.zeros((LANES - 2, width), F32)], axis=0
    )
    small = jnp.concatenate([dot(r.lifted[...].T, r.grams[...]), gains.T], axis=1)
    if z.inside:
        for j in range(n * SPLIT):
            value = small[j * z.small : (j + 1) * z.small].astype(BF)
            r.sm_part[j % SPLIT, j // SPLIT] = value

        def small_near(slot):
            block = p.t3 if slot else p.t1
            return make_copy(
                r.sm_part.at[block],
                r.sm_near.at[slot],
                r.sm_sem.at[2 * slot],
                r.sm_sem.at[2 * slot + 1],
                tensor=p.t1,
            )

        small_far = make_copy(r.sm_send, r.sm_far, r.sm_sem.at[4], r.sm_sem.at[5], tensor=p.t2)

        def small_copy(step, incoming=False):
            to = peer(step)
            at = to if incoming else p.d
            return make_copy(
                r.sm_out.at[to], r.sm_in.at[at], r.sp_sem.at[0, 0], r.sp_sem.at[1, at], dp=to
            )

        small_near(1).start()
        small_near(0).start()
        small_near(1).wait_recv()
        r.sm_send[...] = (r.sm_part[p.t2].astype(F32) + r.sm_near[1].astype(F32)).astype(BF)
        small_far.start()
    else:
        r.sm_total[...] = small

    for turn in range(2):
        for step in range(n):
            if step > 0:
                back_copy(step, turn, True).wait_recv()
            pass_copy(1, turn, peer(step)).start()
            pass_copy(0, turn, peer(step)).start()
    if z.inside:
        small_near(0).wait_recv()
        small_far.wait_recv()
        total = r.sm_part[p.t].astype(F32) + r.sm_near[0].astype(F32) + r.sm_far[...].astype(F32)
        r.sm_out[...] = total.astype(BF)
        for step in range(1, n):
            small_copy(step).start()
        r.sm_in[p.d] = r.sm_out[p.d]
        pair_sums(6)
    for turn in range(2):
        for step in range(n):
            of = peer(step)
            pass_copy(1, turn, of, True).wait_recv()
            pass_copy(2, turn, of).start()
    for i in range(3):
        lid_copy(i, True).wait_recv()
    kept = z.table_rows // SPLIT
    low_table = lane_of((kept, LANES)) < HD
    wanted = row_of((kept, slots)) + p.t * kept

    def add_rows(b, fresh=False):
        block = pl.ds(pl.multiple_of(b * slots, slots), slots)
        hits = [onehot(r.lids[b, k][0:1] == wanted) for k in range(2)]
        left = dot(hits[0], r.back_in[block, 0 : 2 * LANES])
        right = dot(hits[1], r.back_in[block, LANES : 3 * LANES])
        sums = (left[:, :LANES], jnp.where(low_table, left[:, LANES:], right[:, :LANES]), right[:, LANES:])
        for g, value in enumerate(sums):
            at = slice(g * LANES, (g + 1) * LANES)
            r.table_grads[:, at] = value if fresh else r.table_grads[:, at] + value

    add_rows(p.t, True)
    for turn in range(2):
        for step in range(n):
            pass_copy(0, turn, peer(step), True).wait_recv()
    add_rows(p.t1)
    add_rows(p.t2)
    pair_sums(99)
    for turn in range(2):
        for step in range(n):
            pass_copy(2, turn, peer(step), True).wait_recv()
    add_rows(p.t3)

    if z.inside:
        for step in range(1, n):
            small_copy(step, True).wait_recv()
        r.sm_total[...] = jnp.sum(r.sm_in[...].astype(F32), axis=0)
        for spread in spreads.values():
            spread.finish()

    all_ids.wait_send()
    shared = [(r.rows_out, r.row_sem, cap), (r.back_out, r.back_sem, cap)]
    if z.inside:
        shared.append((r.sm_out, r.sp_sem, 1))
    for ref, sems, each in shared:
        ref = ref.at[pl.ds(0, (n - 1) * each)]
        make_copy(ref, ref, sems.at[0, 0], sems.at[1, 0], dp=peer(1)).wait_send()
    for i in range(3):
        lid_copy(i).wait_send()
    for gather in (gather1, gather2, gather3):
        gather.close()
    for scatter in scatters[1:]:
        scatter.close()
    for spread in spreads.values():
        spread.close()
    if z.inside:
        small_near(0).wait_send()
        small_near(1).wait_send()
        small_far.wait_send()
    for kind in range(3):
        for turn in range(2):
            for step in range(n):
                pass_copy(kind, turn, peer(step)).wait_send()


def finish_kernel(z, names, *refs):
    r = Refs(names, refs)
    r.block[...] = r.block_out[...]
    r.embed[...] = r.embed_grad[...]
    r.bigram[...] = r.table_grads[:, : 2 * LANES].T[: z.table_width]
    r.trigram[...] = r.table_grads[:, LANES:].T[2 * LANES - z.table_width :]
    r.ngram[...] = r.sm_total[:, : z.pair_width]
    gains = r.sm_total[:, z.pair_width :]
    r.first[...] = gains[:, 0:1].T
    r.second[...] = gains[:, 1:2].T
    r.gate[...] = r.ga_out[...]
    r.up[...] = r.up_out[...]
    r.down[...] = r.dn_out[...]
    side = 3 * HD
    for h in range(z.heads):
        sums = getattr(r, f"at{h}_out")[...]
        r.attend[:, h * side : (h + 1) * side] = sums[:, :side]
        r.output[h * HD : (h + 1) * HD] = sums[:, LANES:].T[HD:]


def finish_outputs(z, got):
    kept = z.table_rows // SPLIT
    outs = dict(
        block=((z.rows, z.width), BF),
        embed=((z.rows, z.width), F32),
        bigram=((z.table_width, kept), F32),
        trigram=((z.table_width, kept), F32),
        ngram=((z.small, z.pair_width), F32),
        first=((1, z.small), F32),
        attend=((z.piece, 3 * HD * z.heads), F32),
        output=((HD * z.heads, z.piece), F32),
        second=((1, z.small), F32),
        gate=((z.piece, z.units), F32),
        up=((z.piece, z.units), F32),
        down=((z.piece, z.units), F32),
    )
    done = pl.pallas_call(
        functools.partial(finish_kernel, z, (*got, *outs)),
        out_shape=[jax.ShapeDtypeStruct(*item) for item in outs.values()],
        in_specs=[pl.BlockSpec(memory_space=pltpu.VMEM)] * len(got),
        out_specs=[pl.BlockSpec(memory_space=pltpu.VMEM)] * len(outs),
        name="finish",
    )(*got.values())
    done = dict(zip(outs, done, strict=True))
    for name in ("bigram", "trigram", "ngram", "down"):
        done[name] = done[name].T
    for name in ("first", "second"):
        done[name] = done[name].reshape(z.small)
    return tuple(done.values())


def shards(
    embedded,
    bigram_ids,
    trigram_ids,
    prefix_lens,
    bigram_table,
    trigram_table,
    ngram_weight,
    first_gain,
    attend_weight,
    output_weight,
    second_gain,
    gate_weight,
    up_weight,
    down_weight,
    cotangent,
):
    n = lax.axis_size("dp")
    rows, width = embedded.shape
    table_rows, table_width = bigram_table.shape
    heads, units = attend_weight.shape[1] // (3 * HD), gate_weight.shape[1]
    z = Sizes(n, rows, width, heads, units, table_rows, table_width)
    scratch, outs = scratch_of(z), outputs_of(z)
    names = (*INPUTS, *outs, *scratch)
    anywhere = pl.BlockSpec(memory_space=pl.ANY)
    in_specs = [anywhere] * len(INPUTS)
    in_specs[3] = pl.BlockSpec(memory_space=pltpu.SMEM)
    got = pl.pallas_call(
        functools.partial(block_kernel, z, names),
        out_shape=[jax.ShapeDtypeStruct(*item) for item in outs.values()],
        in_specs=in_specs,
        out_specs=[pl.BlockSpec(memory_space=pltpu.VMEM)] * len(outs),
        scratch_shapes=list(scratch.values()),
        compiler_params=pltpu.CompilerParams(
            collective_id=0, has_side_effects=True, vmem_limit_bytes=67043328
        ),
        name="block",
    )(
        embedded,
        bigram_ids.reshape(1, rows),
        trigram_ids.reshape(1, rows),
        prefix_lens,
        bigram_table.T,
        trigram_table.T,
        ngram_weight,
        first_gain,
        attend_weight.T,
        output_weight,
        second_gain,
        gate_weight,
        up_weight,
        down_weight,
        cotangent,
    )
    got = dict(zip(outs, got, strict=True))
    if not z.inside:

        def summed(part, axes):
            return lax.psum_scatter(part, axes, scatter_dimension=0, tiled=True)

        for name in ("ga", "up", "dn", *(f"at{h}" for h in range(heads))):
            got[f"{name}_out"] = summed(got.pop(f"{name}_part").astype(F32), "dp")
        got["sm_total"] = summed(got["sm_total"], ("dp", "tensor"))
    return finish_outputs(z, got)


def solution(mesh):
    placed = (
        P(("dp", "tensor"), None),
        P(("dp", "tensor")),
        P(("dp", "tensor")),
        P("dp"),
        P("dp", None),
        P("dp", None),
        P(),
        P(),
        P(None, "tensor"),
        P("tensor", None),
        P(),
        P(None, "tensor"),
        P(None, "tensor"),
        P("tensor", None),
        P("dp", None),
    )
    return jax.shard_map(
        shards,
        mesh=mesh,
        in_specs=placed,
        out_specs=(
            P(("dp", "tensor"), None),
            P(("dp", "tensor"), None),
            P(("dp", "tensor"), None),
            P(("dp", "tensor"), None),
            P(None, ("dp", "tensor")),
            P(("dp", "tensor")),
            P("dp", "tensor"),
            P("tensor", "dp"),
            P(("dp", "tensor")),
            P("dp", "tensor"),
            P("dp", "tensor"),
            P("tensor", "dp"),
        ),
        check_vma=False,
    )
```
